32 devices in a mesh: wide: 8 (over z, x), narrow: 4 (over y, core).
Axes of the slice: x: 2, y: 2, z: 4, core: 2. Of those that a mesh axis runs over, the one named last changes fastest.
Arguments:
- block_input: bfloat16 [4096, 2048], P('wide'), may hold values from -6 to 6
- attn_gain: bfloat16 [2048], replicated, may hold values from 0.5 to 1.5
- query_weight: bfloat16 [2048, 2048], P(None, 'narrow'), may hold values from -0.125 to 0.125
- key_weight: bfloat16 [2048, 2048], P(None, 'narrow'), may hold values from -0.125 to 0.125
- value_weight: bfloat16 [2048, 2048], P(None, 'narrow'), may hold values from -0.125 to 0.125
- query_gain: bfloat16 [2048], P('narrow'), may hold values from 0.5 to 1.5
- key_gain: bfloat16 [2048], P('narrow'), may hold values from 0.5 to 1.5
- out_weight: bfloat16 [2048, 2048], P('narrow'), may hold values from -1.5 to 1.5
- moe_gain: bfloat16 [2048], replicated, may hold values from 0.5 to 1.5
- router_weight: bfloat16 [2048, 32], replicated, may hold values from -0.0625 to 0.0625
- gate_weight: bfloat16 [32, 2048, 1024], P('wide', None, 'narrow'), may hold values from -0.125 to 0.125
- up_weight: bfloat16 [32, 2048, 1024], P('wide', None, 'narrow'), may hold values from -0.125 to 0.125
- down_weight: bfloat16 [32, 1024, 2048], P('wide', 'narrow'), may hold values from -6 to 6
- segment_ids: int32 [4096], P('wide'), may hold values from 0 to 3, as said below
- expert_ids: int32 [4096, 8], P(('wide', 'narrow')), may hold values from 0 to 31, all different within a row; in each aligned block of 128 rows (0 to 127, 128 to 255, ...) at most 48 rows name the same one
- out_cotangent: bfloat16 [4096, 2048], P(('wide', 'narrow')), may hold values from -6 to 6
Outputs:
- block_output: bfloat16 [4096, 2048], P(('wide', 'narrow'))
- input_grad: bfloat16 [4096, 2048], P(('wide', 'narrow'))
- attn_gain_grad: float32 [2048], replicated
- query_weight_grad: float32 [2048, 2048], P(None, 'narrow')
- key_weight_grad: float32 [2048, 2048], P(None, 'narrow')
- value_weight_grad: float32 [2048, 2048], P(None, 'narrow')
- query_gain_grad: float32 [2048], P('narrow')
- key_gain_grad: float32 [2048], P('narrow')
- out_weight_grad: float32 [2048, 2048], P('narrow')
- moe_gain_grad: float32 [2048], replicated
- router_weight_grad: float32 [2048, 32], replicated
- gate_weight_grad: float32 [32, 2048, 1024], P('wide', None, 'narrow')
- up_weight_grad: float32 [32, 2048, 1024], P('wide', None, 'narrow')
- down_weight_grad: float32 [32, 1024, 2048], P('wide', 'narrow')
The draws below stay inside these ranges and needn't reach their ends.
Inputs may be any that keep to these rules, and one draw needn't show every extreme that they name: `segment_ids`: within each group of 512 consecutive tokens the ids start at 0 and never fall; a sequence is a run of equal ids inside one group. One group holds a single sequence of 512 tokens, each other group up to four sequences. `expert_ids`: each row names 8 different experts. Among the rows of one device no expert is named more than 48 times, a bound that some block reaches.
All inputs are finite; a program needn't handle non-finite values.
Results may differ from the reference program's by a relative error of at most 0.025.
Values may be sent and summed in bfloat16 or wider, within the bound.
A program may use at most 448 MiB of HBM per device.

```python
import math
import jax
import jax.numpy as jnp
import numpy as np
from jax import lax

D = 2048
HEADS = 16
HEAD_DIM = 128
FF = 1024
TOP = 8
EXPERTS = 32
TOK_DEV = 128
TOK_W = 512
TOKENS = 4096
CAP = 48
SLOTS = 1536
N_WIDE = 8
N_NARROW = 4


def draw_segment_ids(key, part):
    group_count = TOKENS // TOK_W
    cut_key, whole_key = jax.random.split(jax.random.fold_in(key, 7))
    cuts = jax.random.randint(cut_key, (group_count, 3), 1, TOK_W)
    whole_group = jax.random.randint(whole_key, (), 0, group_count)
    places = jnp.arange(TOK_W, dtype=jnp.int32)
    labels = jnp.sum((places[None, :, None] >= cuts[:, None, :]).astype(jnp.int32), axis=-1)
    labels = jnp.where(jnp.arange(group_count, dtype=jnp.int32)[:, None] == whole_group, 0, labels)
    return labels.reshape(-1).astype(jnp.int32)


def shard_levels(stream_key, dims, cuts, least, largest):
    def one(axis_at, blocks):
        heights = jax.random.uniform(jax.random.fold_in(jax.random.fold_in(stream_key, 6), axis_at), (blocks,), jnp.float32, least / len(cuts), largest / len(cuts))
        return jnp.repeat(jnp.exp(heights), dims[axis_at] // blocks).reshape((-1,) + (1,) * (len(dims) - axis_at - 1))

    level = one(*cuts[0])
    for cut in cuts[1:]:
        level = level * one(*cut)
    return level


def assign_block(stream_key, own, number, rows, number_of, top, reach, skew):
    order = jax.random.permutation(stream_key, number_of)
    heavy_load, common = shares(number_of, rows * top, reach, skew, True), shares(number_of, rows * top, reach, skew, False)
    places = jnp.arange(number_of)

    def named(lengths, offset_by):
        used = int((lengths > 0).sum())
        fixed = max(1, used // 4)
        moved = fixed + (places - fixed + offset_by * (used - fixed)) % max(1, number_of - fixed)
        return jnp.zeros((number_of,), jnp.int32).at[order[jnp.where(places < fixed, places, moved)]].set(jnp.asarray(lengths, jnp.int32))

    lengths = jnp.where(number % 4 == 0, named(heavy_load, number // 4), named(common, number - number // 4 - 1))
    mixed = jax.random.permutation(jax.random.fold_in(own, 3), number_of)
    donor, receiver = mixed[0:number_of // 2 * 2:2], mixed[1:number_of // 2 * 2:2]
    room = jnp.minimum(lengths[donor] - 1, reach - lengths[receiver]) // 2
    room = jnp.where((donor == order[0]) | (receiver == order[0]) | (lengths[receiver] == 0), 0, jnp.maximum(room, 0))
    moved = jax.random.randint(jax.random.fold_in(own, 4), (number_of // 2,), 0, 1 << 20) % (room + 1)
    lengths = lengths.at[donor].add(-moved).at[receiver].add(moved)
    members = jnp.searchsorted(jnp.cumsum(lengths), jnp.arange(rows * top), side="right").astype(jnp.int32)
    table = members.reshape(top, rows).T
    table = table[jax.random.permutation(jax.random.fold_in(own, 1), rows)]
    offset_by = jax.random.randint(jax.random.fold_in(own, 2), (rows, 1), 0, top)
    return jnp.take_along_axis(table, (jnp.arange(top)[None, :] + offset_by) % top, axis=1)


def shares(number_of, total, reach, lean, full):
    weights = [(1 << 20) // math.isqrt(grade ** lean) + 1 for grade in range(1, number_of + 1)]
    largest = reach if full else min(reach, max(-(-total // number_of), total * weights[0] // sum(weights)))
    least = 1 if total - largest >= number_of - 1 else 0
    counts, spare = [largest] + [least] * (number_of - 1), total - largest - least * (number_of - 1)
    while spare > 0:
        free = [i for i in range(1, number_of) if counts[i] < largest] or [i for i in range(1, number_of) if counts[i] < reach]
        whole, budget = sum([weights[i] for i in free]), spare
        for i in free:
            extra = min(reach - counts[i], max(1, budget * weights[i] // whole), spare)
            counts[i] = counts[i] + extra
            spare = spare - extra
    return np.array(counts)


def gaussian(key, extent, deviation, limit, cuts=(), held_as=jnp.bfloat16):
    loudness = shard_levels(key, extent, cuts, -0.22, 0.18) if cuts else 1.0
    drawn = jax.random.normal(key, extent, jnp.float32) * deviation * loudness
    return jnp.minimum(jnp.maximum(drawn, -limit), limit).astype(held_as)


def setup_inputs(seed: int = 0) -> dict:
    key_of = jax.random.split(jax.random.key(seed), 17)
    block_input = gaussian(key_of[0], (TOKENS, D), 1.0, 6.0, ((0, 8),))
    attn_gain = jnp.clip(1.0 + 0.1 * jax.random.normal(key_of[1], (D,), jnp.float32), 0.5, 1.5).astype(jnp.bfloat16)
    query_weight = gaussian(key_of[2], (D, D), D ** -0.5, 0.125, ((1, 4),))
    key_weight = gaussian(key_of[3], (D, D), D ** -0.5, 0.125, ((1, 4),))
    value_weight = gaussian(key_of[4], (D, D), D ** -0.5, 0.125, ((1, 4),))
    query_gain = jnp.clip(1.0 + 0.1 * jax.random.normal(key_of[5], (D,), jnp.float32), 0.5, 1.5).astype(jnp.bfloat16)
    key_gain = jnp.clip(1.0 + 0.1 * jax.random.normal(key_of[6], (D,), jnp.float32), 0.5, 1.5).astype(jnp.bfloat16)
    out_weight = gaussian(key_of[7], (D, D), (max(D // 128, 1)) ** -0.5, 1.5, ((0, 4),))
    moe_gain = jnp.clip(1.0 + 0.1 * jax.random.normal(key_of[8], (D,), jnp.float32), 0.5, 1.5).astype(jnp.bfloat16)
    router_weight = gaussian(key_of[9], (D, EXPERTS), (4 * D) ** -0.5, 0.0625)
    gate_weight = gaussian(key_of[10], (EXPERTS, D, FF), D ** -0.5, 0.125, ((0, 8), (2, 4)))
    up_weight = gaussian(key_of[11], (EXPERTS, D, FF), D ** -0.5, 0.125, ((0, 8), (2, 4)))
    down_weight = gaussian(key_of[12], (EXPERTS, FF, D), 1 ** -0.5, 6.0, ((0, 8), (1, 4)))
    segment_ids = draw_segment_ids(jax.random.fold_in(key_of[16], 71), 0)
    expert_ids_keys = jax.random.split(jax.random.fold_in(key_of[14], 1), TOKENS // TOK_DEV)
    expert_ids_turns = jax.random.permutation(jax.random.fold_in(key_of[14], 3), TOKENS // TOK_DEV)
    expert_ids = jax.vmap(lambda own, number: assign_block(jax.random.fold_in(key_of[14], 2), own, number, TOK_DEV, EXPERTS, TOP, CAP, 2))(expert_ids_keys, expert_ids_turns).reshape((TOKENS, TOP))
    out_cotangent = gaussian(key_of[15], (TOKENS, D), 1.0, 6.0, ((0, 32),))
    return {"block_input": block_input, "attn_gain": attn_gain, "query_weight": query_weight, "key_weight": key_weight, "value_weight": value_weight, "query_gain": query_gain, "key_gain": key_gain, "out_weight": out_weight, "moe_gain": moe_gain, "router_weight": router_weight, "gate_weight": gate_weight, "up_weight": up_weight, "down_weight": down_weight, "segment_ids": segment_ids, "expert_ids": expert_ids, "out_cotangent": out_cotangent}


@jax.custom_vjp
def low(v):
    return lax.optimization_barrier(v.astype(jnp.bfloat16)).astype(jnp.float32)

@jax.custom_vjp
def low_back(v):
    return v

def low_keep(v):
    return (low(v), None)

def low_pass(kept, grad):
    return (grad,)

def back_keep(v):
    return (v, None)

def back_low(kept, grad):
    return (low(grad),)
low.defvjp(low_keep, low_pass)
low_back.defvjp(back_keep, back_low)
norm_epsilon = 1e-05
rope_base = 10000.0
masked_score = -1e+30

def matmul(left, right):
    return jnp.dot(left, right, preferred_element_type=jnp.float32, precision=lax.Precision.HIGHEST)

def rms_scale(values, gain):
    inverse = lax.rsqrt(lax.optimization_barrier(jnp.mean(values * values, axis=-1, keepdims=True)) + norm_epsilon)
    return values * inverse * gain

def rope_tables(length, head_size):
    half_size = head_size // 2
    exponent = jnp.arange(half_size, dtype=jnp.float32) * (2.0 / head_size)
    angle = jnp.arange(length, dtype=jnp.float32)[:, None] * (rope_base ** (-exponent))[None, :]
    return (jnp.cos(angle), jnp.sin(angle))

def head_post(projected, gain, rope_cos, rope_sin, head_size):
    tokens_here = projected.shape[0]
    normed = rms_scale(projected, gain).reshape(tokens_here, -1, head_size)
    half_size = head_size // 2
    first_half = normed[..., :half_size]
    second_half = normed[..., half_size:]
    cos_rows = rope_cos[:, None, :]
    sin_rows = rope_sin[:, None, :]
    turned = jnp.concatenate([first_half * cos_rows - second_half * sin_rows, second_half * cos_rows + first_half * sin_rows], axis=-1)
    return turned.reshape(tokens_here, -1)

def reference(block_input, attn_gain, query_weight, key_weight, value_weight, query_gain, key_gain, out_weight, moe_gain, router_weight, gate_weight, up_weight, down_weight, segment_ids, expert_ids, out_cotangent):
    device_count = N_WIDE * N_NARROW
    block_ids = expert_ids.reshape(device_count, TOK_DEV * TOP)
    expert_match = (block_ids[:, :, None] == jnp.arange(EXPERTS, dtype=jnp.int32)[None, None, :]).astype(jnp.int32)
    earlier = jnp.cumsum(expert_match, axis=1) - expert_match
    slot_of = lax.optimization_barrier(jnp.sum(earlier * expert_match, axis=2))
    owned_rows = (jnp.arange(device_count, dtype=jnp.int32)[:, None] * CAP + slot_of).reshape(TOKENS, TOP).astype(jnp.int32)
    group_segments = segment_ids.reshape(N_WIDE, TOK_W)
    rope_cos, rope_sin = rope_tables(TOK_W, HEAD_DIM)
    places = jnp.arange(TOK_W, dtype=jnp.int32)

    def forward(inputs, attn_scale, query_w, key_w, value_w, query_scale, key_scale, out_w, moe_scale, router_w, gate_w, up_w, down_w):
        normed_one = low(rms_scale(inputs, attn_scale))
        query_proj = low_back(matmul(normed_one, query_w))
        key_proj = low_back(matmul(normed_one, key_w))
        value_proj = low_back(matmul(normed_one, value_w))

        def group(items):
            query_part, key_part, value_part, segments = items
            queries = low(head_post(query_part, query_scale, rope_cos, rope_sin, HEAD_DIM) * HEAD_DIM ** (-0.5))
            keys = low(head_post(key_part, key_scale, rope_cos, rope_sin, HEAD_DIM))
            values = low(value_part)
            query_heads = queries.reshape(TOK_W, HEADS, HEAD_DIM)
            key_heads = keys.reshape(TOK_W, HEADS, HEAD_DIM)
            value_heads = values.reshape(TOK_W, HEADS, HEAD_DIM)
            scores = low_back(jnp.einsum('qhd,khd->hqk', query_heads, key_heads, precision=lax.Precision.HIGHEST))
            allowed = (segments[:, None] == segments[None, :]) & (places[:, None] >= places[None, :])
            probs = jax.nn.softmax(jnp.where(allowed[None], scores, masked_score), axis=-1)
            mixed_rows = jnp.einsum('hqk,khd->qhd', low(probs), value_heads, precision=lax.Precision.HIGHEST)
            return mixed_rows.reshape(TOK_W, D)
        grouped = lax.map(jax.checkpoint(group), (query_proj.reshape(N_WIDE, TOK_W, D), key_proj.reshape(N_WIDE, TOK_W, D), value_proj.reshape(N_WIDE, TOK_W, D), group_segments))
        heads_out = low(low_back(grouped.reshape(TOKENS, D)))
        attn = low_back(matmul(heads_out, out_w))
        hidden = inputs + attn
        normed_two = low(rms_scale(hidden, moe_scale))
        route_probs = jax.nn.softmax(matmul(normed_two, router_w), axis=-1)
        gates = jnp.take_along_axis(route_probs, expert_ids, axis=1)
        buffer = jnp.zeros((EXPERTS, SLOTS, D), jnp.float32)
        for choice_index in range(TOP):
            buffer = buffer.at[expert_ids[:, choice_index], owned_rows[:, choice_index]].set(normed_two)
        buffer = low_back(buffer)

        def expert(items):
            rows_in, gate_one, up_one, down_one = items
            gate_pre = low_back(matmul(rows_in, gate_one))
            up_pre = low_back(matmul(rows_in, up_one))
            activated = low(jax.nn.silu(gate_pre) * up_pre)
            return low_back(low(matmul(activated, down_one)))
        expert_out = lax.map(jax.checkpoint(expert), (buffer, gate_w, up_w, down_w))
        moe_out = jnp.zeros((TOKENS, D), jnp.float32)
        for choice_index in range(TOP):
            picked = expert_out[expert_ids[:, choice_index], owned_rows[:, choice_index]]
            moe_out = moe_out + gates[:, choice_index:choice_index + 1] * picked
        return hidden + moe_out
    floats = tuple((item.astype(jnp.float32) for item in (block_input, attn_gain, query_weight, key_weight, value_weight, query_gain, key_gain, out_weight, moe_gain, router_weight, gate_weight, up_weight, down_weight)))
    result, pullback = jax.vjp(forward, *floats)
    grads = pullback(out_cotangent.astype(jnp.float32))
    return (result.astype(jnp.bfloat16), grads[0].astype(jnp.bfloat16), grads[1], grads[2], grads[3], grads[4], grads[5], grads[6], grads[7], grads[8], grads[9], grads[10], grads[11], grads[12])
```

```python
import jax
import jax.numpy as jnp
from jax import lax
from jax.sharding import PartitionSpec as P

HEAD_DIM = 128
QBLK = 512


norm_epsilon = 1e-05
rope_base = 10000.0
masked_score = -1e30


def rms_scale(values, gain):
    inverse = lax.rsqrt(jnp.mean(values * values, axis=-1, keepdims=True) + norm_epsilon)
    return values * inverse * gain


def rope_tables(length, head_size):
    half_size = head_size // 2
    exponent = jnp.arange(half_size, dtype=jnp.float32) * (2.0 / head_size)
    angle = jnp.arange(length, dtype=jnp.float32)[:, None] * (rope_base ** (-exponent))[None, :]
    return (jnp.cos(angle), jnp.sin(angle))


def rotate(normed, rope_cos, rope_sin, head_size):
    tokens_here = normed.shape[0]
    by_head = normed.reshape(tokens_here, -1, head_size)
    half_size = head_size // 2
    first_half = by_head[..., :half_size]
    second_half = by_head[..., half_size:]
    cos_rows = rope_cos[:, None, :]
    sin_rows = rope_sin[:, None, :]
    turned = jnp.concatenate(
        [
            first_half * cos_rows - second_half * sin_rows,
            second_half * cos_rows + first_half * sin_rows,
        ],
        axis=-1,
    )
    return turned.reshape(tokens_here, -1)


def gated_unit(gate_pre, up_pre):
    return jax.nn.silu(gate_pre) * up_pre


def contract_rows(left, right):
    return lax.dot_general(
        left, right, (((0,), (0,)), ((), ())), preferred_element_type=jnp.float32
    )


def contract_last(left, right):
    return lax.dot_general(
        left, right, (((1,), (1,)), ((), ())), preferred_element_type=jnp.float32
    )


BOTH = ("wide", "narrow")


def gather_all(block):
    return lax.all_gather(block, BOTH, axis=0, tiled=True)


def scatter_all(parts):
    return lax.psum_scatter(parts, BOTH, scatter_dimension=0, tiled=True)


def local(
    block_input,
    attn_gain,
    query_weight,
    key_weight,
    value_weight,
    query_gain,
    key_gain,
    out_weight,
    moe_gain,
    router_weight,
    gate_weight,
    up_weight,
    down_weight,
    segment_ids,
    expert_ids,
    out_cotangent,
):
    group_rows, model_width = block_input.shape
    own_rows = out_cotangent.shape[0]
    local_width = query_weight.shape[1]
    head_size = HEAD_DIM
    local_heads = local_width // head_size
    wide_size = lax.axis_size("wide")
    experts_all = router_weight.shape[1]
    experts_here = gate_weight.shape[0]
    choose_count = expert_ids.shape[1]
    capacity = 3 * own_rows * choose_count // (2 * experts_all)
    row_begin = lax.axis_index("narrow") * own_rows
    blocks = group_rows // QBLK
    highest_precision = lax.Precision.HIGHEST
    block_count = wide_size * lax.axis_size("narrow")
    chosen = (expert_ids[:, :, None] == jnp.arange(experts_all)[None, None, :]).any(axis=1)
    token_order = jnp.arange(own_rows)
    earlier = jnp.dot(
        (token_order[:, None] > token_order[None, :]).astype(jnp.bfloat16),
        chosen.astype(jnp.bfloat16),
        preferred_element_type=jnp.float32,
    )
    places_all = gather_all(jnp.where(chosen, earlier, -1.0).T)
    grads_all = gather_all(out_cotangent)
    inputs_all = block_input.astype(jnp.float32)
    normed_one = rms_scale(inputs_all, attn_gain.astype(jnp.float32)).astype(jnp.bfloat16)
    joined_weight = jnp.concatenate([query_weight, key_weight, value_weight], axis=1)
    projected = jnp.dot(normed_one, joined_weight, preferred_element_type=jnp.float32)
    query_proj = projected[:, :local_width]
    key_proj = projected[:, local_width : 2 * local_width]
    value_proj = projected[:, 2 * local_width :]
    rope_cos, rope_sin = rope_tables(group_rows, head_size)
    query_total, key_total = lax.psum(
        (jnp.sum(query_proj * query_proj, axis=1), jnp.sum(key_proj * key_proj, axis=1)), "narrow"
    )
    query_inverse = lax.rsqrt(query_total / model_width + norm_epsilon)[:, None]
    key_inverse = lax.rsqrt(key_total / model_width + norm_epsilon)[:, None]
    query_scale = query_gain.astype(jnp.float32)
    key_scale = key_gain.astype(jnp.float32)
    query_normed = query_proj * query_inverse * query_scale
    key_normed = key_proj * key_inverse * key_scale

    def turn_both(query_in, key_in):
        return (
            rotate(query_in, rope_cos, rope_sin, head_size) * head_size ** (-0.5),
            rotate(key_in, rope_cos, rope_sin, head_size),
        )

    (turned_query, turned_key), turn_back = jax.vjp(turn_both, query_normed, key_normed)
    query_heads = turned_query.astype(jnp.bfloat16).reshape(group_rows, local_heads, head_size)
    key_heads = turned_key.astype(jnp.bfloat16).reshape(group_rows, local_heads, head_size)
    value_heads = value_proj.astype(jnp.bfloat16).reshape(group_rows, local_heads, head_size)
    positions = jnp.arange(group_rows)

    def block_scores(block_index):
        block_begin = block_index * QBLK
        query_block = lax.dynamic_slice_in_dim(query_heads, block_begin, QBLK, 0)
        query_segments = lax.dynamic_slice_in_dim(segment_ids, block_begin, QBLK, 0)
        query_places = block_begin + jnp.arange(QBLK)
        allowed = (query_segments[:, None] == segment_ids[None, :]) & (
            query_places[:, None] >= positions[None, :]
        )
        scores = jnp.einsum(
            "qhd,khd->hqk", query_block, key_heads, preferred_element_type=jnp.float32
        )
        return (query_block, jnp.where(allowed[None], scores, masked_score))

    def attend(block_index):
        query_block, scores = block_scores(block_index)
        highest = jnp.max(scores, axis=-1, keepdims=True)
        weights = jnp.exp(scores - highest)
        totals = jnp.sum(weights, axis=-1, keepdims=True)
        probs_low = (weights / totals).astype(jnp.bfloat16)
        mixed_rows = jnp.einsum(
            "hqk,khd->qhd", probs_low, value_heads, preferred_element_type=jnp.float32
        )
        return (mixed_rows, highest + jnp.log(totals))

    mixed_blocks, log_totals = lax.map(attend, jnp.arange(blocks))
    heads_out = mixed_blocks.reshape(group_rows, local_width).astype(jnp.bfloat16)
    attn_own = lax.psum_scatter(
        jnp.dot(heads_out, out_weight, preferred_element_type=jnp.float32).astype(jnp.bfloat16),
        "narrow",
        scatter_dimension=0,
        tiled=True,
    ).astype(jnp.float32)
    input_own = lax.dynamic_slice_in_dim(inputs_all, row_begin, own_rows, 0)
    hidden = input_own + attn_own
    normed_two_full, norm_two_back = jax.vjp(rms_scale, hidden, moe_gain.astype(jnp.float32))
    normed_two = normed_two_full.astype(jnp.bfloat16)
    logits = jnp.dot(normed_two, router_weight, preferred_element_type=jnp.float32)
    route_probs = jax.nn.softmax(logits, axis=-1)
    rows_all = gather_all(normed_two)
    probs_all = gather_all(route_probs.T)
    expert_begin = lax.axis_index("wide") * experts_here
    places_here = lax.dynamic_slice_in_dim(
        places_all.reshape(block_count, experts_all, own_rows), expert_begin, experts_here, 1
    )
    probs_here = lax.dynamic_slice_in_dim(
        probs_all.reshape(block_count, experts_all, own_rows), expert_begin, experts_here, 1
    )
    pick = places_here[:, :, None, :] == jnp.arange(capacity, dtype=jnp.float32)[None, None, :, None]
    pick_low = pick.astype(jnp.bfloat16)
    slot_gate = jnp.sum(jnp.where(pick, probs_here[:, :, None, :], 0.0), axis=-1)
    slot_gate = slot_gate.transpose(1, 0, 2).reshape(experts_here, block_count * capacity, 1)

    def spread(rows):
        out = jnp.einsum(
            "best,btd->ebsd",
            pick_low,
            rows.reshape(block_count, own_rows, model_width),
            preferred_element_type=jnp.float32,
        )
        return out.astype(jnp.bfloat16).reshape(experts_here, block_count * capacity, model_width)

    def collect(slots):
        out = jnp.einsum(
            "best,ebsd->btd",
            pick_low,
            slots.reshape(experts_here, block_count, capacity, model_width),
            preferred_element_type=jnp.float32,
        )
        return out.astype(jnp.bfloat16).reshape(block_count * own_rows, model_width)

    slot_rows = spread(rows_all)
    slot_grads = spread(grads_all)
    gate_pre = jnp.einsum("erd,edf->erf", slot_rows, gate_weight, preferred_element_type=jnp.float32)
    up_pre = jnp.einsum("erd,edf->erf", slot_rows, up_weight, preferred_element_type=jnp.float32)
    activated, unit_back = jax.vjp(gated_unit, gate_pre, up_pre)
    gated_act = (activated * slot_gate).astype(jnp.bfloat16)
    raw_act_grad = jnp.einsum(
        "erd,efd->erf", slot_grads, down_weight, preferred_element_type=jnp.float32
    )
    slot_gate_grads = jnp.sum(activated * raw_act_grad, axis=-1)
    gate_grad_full, up_grad_full = unit_back(raw_act_grad * slot_gate)
    gate_grad_low = gate_grad_full.astype(jnp.bfloat16)
    up_grad_low = up_grad_full.astype(jnp.bfloat16)
    gate_grad_parts = jnp.einsum(
        "best,ebs->bet",
        pick.astype(jnp.float32),
        slot_gate_grads.reshape(experts_here, block_count, capacity),
        precision=highest_precision,
    )
    gate_grad_wide = lax.dynamic_update_slice_in_dim(
        jnp.zeros((block_count, experts_all, own_rows), jnp.float32), gate_grad_parts, expert_begin, 1
    )
    prob_grads = scatter_all(gate_grad_wide.reshape(block_count * experts_all, own_rows)).T
    back_slots = jnp.einsum(
        "erf,edf->erd", gate_grad_low, gate_weight, preferred_element_type=jnp.float32
    ) + jnp.einsum("erf,edf->erd", up_grad_low, up_weight, preferred_element_type=jnp.float32)
    rows_back = scatter_all(collect(back_slots.astype(jnp.bfloat16))).astype(jnp.float32)
    out_slots = jnp.einsum(
        "erf,efd->erd", gated_act, down_weight, preferred_element_type=jnp.float32
    )
    moe_out = scatter_all(collect(out_slots.astype(jnp.bfloat16))).astype(jnp.float32)
    down_weight_grad = jnp.einsum(
        "erf,erd->efd", gated_act, slot_grads, preferred_element_type=jnp.float32
    )
    gate_weight_grad = jnp.einsum(
        "erd,erf->edf", slot_rows, gate_grad_low, preferred_element_type=jnp.float32
    )
    up_weight_grad = jnp.einsum(
        "erd,erf->edf", slot_rows, up_grad_low, preferred_element_type=jnp.float32
    )
    block_output = (hidden + moe_out).astype(jnp.bfloat16)
    logit_grads = route_probs * (
        prob_grads - jnp.sum(route_probs * prob_grads, axis=-1, keepdims=True)
    )
    router_part = lax.dot_general(
        normed_two.astype(jnp.float32),
        logit_grads,
        (((0,), (0,)), ((), ())),
        precision=highest_precision,
    )
    router_back = lax.dot_general(
        logit_grads,
        router_weight.astype(jnp.float32),
        (((1,), (1,)), ((), ())),
        precision=highest_precision,
    )
    normed_two_grad = rows_back + router_back
    cotangent_full = out_cotangent.astype(jnp.float32)
    hidden_path, moe_gain_part = norm_two_back(normed_two_grad)
    hidden_grad = cotangent_full + hidden_path
    hidden_grad_low = hidden_grad.astype(jnp.bfloat16)
    gathered_piece = lax.all_gather(hidden_grad_low, "narrow", axis=0, tiled=True)
    heads_grad_acc = contract_last(gathered_piece, out_weight)
    out_weight_acc = contract_rows(heads_out, gathered_piece)
    heads_grad_low = heads_grad_acc.astype(jnp.bfloat16).reshape(group_rows, local_heads, head_size)

    def back_block(running, items):
        key_acc, value_acc = running
        block_index, log_total = items
        query_block, scores = block_scores(block_index)
        probs = jnp.exp(scores - log_total)
        probs_low = probs.astype(jnp.bfloat16)
        grad_block = lax.dynamic_slice_in_dim(heads_grad_low, block_index * QBLK, QBLK, 0)
        weight_grads = jnp.einsum(
            "qhd,khd->hqk", grad_block, value_heads, preferred_element_type=jnp.float32
        )
        row_dots = jnp.sum(probs * weight_grads, axis=-1, keepdims=True)
        score_grads = (probs * (weight_grads - row_dots)).astype(jnp.bfloat16)
        query_grad_block = jnp.einsum(
            "hqk,khd->qhd", score_grads, key_heads, preferred_element_type=jnp.float32
        )
        key_acc = key_acc + jnp.einsum(
            "hqk,qhd->khd", score_grads, query_block, preferred_element_type=jnp.float32
        )
        value_acc = value_acc + jnp.einsum(
            "hqk,qhd->khd", probs_low, grad_block, preferred_element_type=jnp.float32
        )
        return ((key_acc, value_acc), query_grad_block)

    zero_heads = jnp.zeros((group_rows, local_heads, head_size), jnp.float32)
    (key_grad, value_grad), query_grads = lax.scan(
        back_block, (zero_heads, zero_heads), (jnp.arange(blocks), log_totals)
    )
    query_normed_grad, key_normed_grad = turn_back(
        (query_grads.reshape(group_rows, local_width), key_grad.reshape(group_rows, local_width))
    )
    query_gain_part = jnp.sum(query_normed_grad * query_proj * query_inverse, axis=0)
    key_gain_part = jnp.sum(key_normed_grad * key_proj * key_inverse, axis=0)
    query_gained = query_normed_grad * query_scale
    key_gained = key_normed_grad * key_scale
    query_dot, key_dot = lax.psum(
        (jnp.sum(query_proj * query_gained, axis=1), jnp.sum(key_proj * key_gained, axis=1)),
        "narrow",
    )
    query_proj_grad = (
        query_inverse * query_gained
        - query_proj * query_inverse**3 * (query_dot / model_width)[:, None]
    )
    key_proj_grad = (
        key_inverse * key_gained - key_proj * key_inverse**3 * (key_dot / model_width)[:, None]
    )
    proj_grad_low = jnp.concatenate(
        [query_proj_grad, key_proj_grad, value_grad.reshape(group_rows, local_width)], axis=1
    ).astype(jnp.bfloat16)
    joined_grad = contract_rows(normed_one, proj_grad_low)
    normed_one_grad = lax.psum_scatter(
        contract_last(proj_grad_low, joined_weight).astype(jnp.bfloat16),
        "narrow",
        scatter_dimension=0,
        tiled=True,
    ).astype(jnp.float32)
    normed_again, norm_one_back = jax.vjp(rms_scale, input_own, attn_gain.astype(jnp.float32))
    input_path, attn_gain_part = norm_one_back(normed_one_grad)
    input_grad = (hidden_grad + input_path).astype(jnp.bfloat16)
    summed = (
        lax.psum(joined_grad[:, :local_width].astype(jnp.bfloat16), "wide").astype(jnp.float32),
        lax.psum(joined_grad[:, local_width : 2 * local_width].astype(jnp.bfloat16), "wide").astype(
            jnp.float32
        ),
        lax.psum(joined_grad[:, 2 * local_width :].astype(jnp.bfloat16), "wide").astype(
            jnp.float32
        ),
        lax.psum(out_weight_acc.astype(jnp.bfloat16), "wide").astype(jnp.float32),
        lax.psum(query_gain_part.astype(jnp.bfloat16), "wide").astype(jnp.float32),
        lax.psum(key_gain_part.astype(jnp.bfloat16), "wide").astype(jnp.float32),
    )
    (
        query_weight_grad,
        key_weight_grad,
        value_weight_grad,
        out_weight_grad,
        query_gain_grad,
        key_gain_grad,
    ) = summed
    router_weight_grad, attn_gain_grad, moe_gain_grad = lax.psum(
        (router_part, attn_gain_part, moe_gain_part), ("wide", "narrow")
    )
    return (
        block_output,
        input_grad,
        attn_gain_grad,
        query_weight_grad,
        key_weight_grad,
        value_weight_grad,
        query_gain_grad,
        key_gain_grad,
        out_weight_grad,
        moe_gain_grad,
        router_weight_grad,
        gate_weight_grad,
        up_weight_grad,
        down_weight_grad,
    )


def solution(mesh):
    in_specs = (
        P("wide", None),
        P(),
        P(None, "narrow"),
        P(None, "narrow"),
        P(None, "narrow"),
        P("narrow"),
        P("narrow"),
        P("narrow", None),
        P(),
        P(),
        P("wide", None, "narrow"),
        P("wide", None, "narrow"),
        P("wide", "narrow", None),
        P("wide"),
        P(("wide", "narrow"), None),
        P(("wide", "narrow"), None),
    )
    out_specs = (
        P(("wide", "narrow"), None),
        P(("wide", "narrow"), None),
        P(),
        P(None, "narrow"),
        P(None, "narrow"),
        P(None, "narrow"),
        P("narrow"),
        P("narrow"),
        P("narrow", None),
        P(),
        P(),
        P("wide", None, "narrow"),
        P("wide", None, "narrow"),
        P("wide", "narrow", None),
    )
    return jax.shard_map(local, mesh=mesh, in_specs=in_specs, out_specs=out_specs, check_vma=False)
```

```python
import functools

import jax
import jax.numpy as jnp
from jax import lax
from jax.experimental import pallas as pl
from jax.experimental.pallas import tpu as pltpu
from jax.sharding import PartitionSpec as P

HEAD_DIM = 128
QBLK = 512


norm_epsilon = 1e-05
rope_base = 10000.0
masked_score = -1e30


def rms_scale(values, gain):
    inverse = lax.rsqrt(jnp.mean(values * values, axis=-1, keepdims=True) + norm_epsilon)
    return values * inverse * gain


def rope_tables(length, head_size):
    half_size = head_size // 2
    exponent = jnp.arange(half_size, dtype=jnp.float32) * (2.0 / head_size)
    angle = jnp.arange(length, dtype=jnp.float32)[:, None] * (rope_base ** (-exponent))[None, :]
    return (jnp.cos(angle), jnp.sin(angle))


def rotate(normed, rope_cos, rope_sin, head_size):
    tokens_here = normed.shape[0]
    by_head = normed.reshape(tokens_here, -1, head_size)
    half_size = head_size // 2
    first_half = by_head[..., :half_size]
    second_half = by_head[..., half_size:]
    cos_rows = rope_cos[:, None, :]
    sin_rows = rope_sin[:, None, :]
    turned = jnp.concatenate(
        [
            first_half * cos_rows - second_half * sin_rows,
            second_half * cos_rows + first_half * sin_rows,
        ],
        axis=-1,
    )
    return turned.reshape(tokens_here, -1)


def gated_unit(gate_pre, up_pre):
    return jax.nn.silu(gate_pre) * up_pre


def contract_rows(left, right):
    return lax.dot_general(
        left, right, (((0,), (0,)), ((), ())), preferred_element_type=jnp.float32
    )


def contract_last(left, right):
    return lax.dot_general(
        left, right, (((1,), (1,)), ((), ())), preferred_element_type=jnp.float32
    )


BOTH = ("wide", "narrow")


MESH = pl.DeviceIdType.MESH
LINE = 4
ADD_ROWS = 16


def flip(bit, on):
    return bit + on * (1 - 2 * bit)


class Place:
    def __init__(self):
        wide, narrow = lax.axis_index("wide"), lax.axis_index("narrow")
        self.z, self.x = wide // 2, lax.rem(wide, 2)
        self.y, self.core = narrow // 2, lax.rem(narrow, 2)

    def device(self, z, first, second, other_core=0):
        core = flip(self.core, other_core)
        x = flip(self.x, first * (1 - core) + second * core)
        y = flip(self.y, first * core + second * (1 - core))
        return (z * 2 + x, y * 2 + core)

    def block(self, z, first, second, other_core=0):
        wide, narrow = self.device(z, first, second, other_core)
        return wide * 4 + narrow


def greet(devices_and_conditions):
    barrier = pltpu.get_barrier_semaphore()
    total = 0
    for device, condition in devices_and_conditions:
        if condition is None:
            pl.semaphore_signal(barrier, inc=1, device_id=device, device_id_type=MESH)
            total = total + 1
        else:
            @pl.when(condition)
            def _():
                pl.semaphore_signal(barrier, inc=1, device_id=device, device_id_type=MESH)
            total = total + condition.astype(jnp.int32)
    pl.semaphore_wait(barrier, total)


def add_into(target, *sources):
    rows = target.shape[0]
    step = min(rows, ADD_ROWS)

    @pl.loop(0, rows // step)
    def _(i):
        part = pl.ds(pl.multiple_of(i * step, step), step)
        total = target[part].astype(jnp.float32)
        for source in sources:
            total = total + source[part].astype(jnp.float32)
        target[part] = total.astype(target.dtype)


def remote(source, target, send, recv, device):
    return pltpu.make_async_remote_copy(
        src_ref=source, dst_ref=target, send_sem=send, recv_sem=recv,
        device_id=device, device_id_type=MESH,
    )


PARTS = 2


def part_of(ref, part):
    rows = ref.shape[0] // PARTS
    return ref.at[pl.ds(part * rows, rows)]


def gather_kernel(count, *refs):
    ins, outs, held = refs[:count], refs[count:2 * count], refs[2 * count:3 * count]
    send, recv, own_in, own_out = refs[3 * count:]
    at = Place()
    z = at.z
    up, down = at.device(z + 1, 0, 0), at.device(z - 1, 0, 0)
    one, two, twin = at.device(z, 1, 0), at.device(z, 0, 1), at.device(z, 0, 0, 1)
    greet([(one, None), (two, None), (twin, None), (up, z < LINE - 1), (down, z > 0)])
    mine = at.block(z, 0, 0)
    routes = {"up": (0, up), "down": (1, down), "one": (2, one), "two": (3, two), "twin": (4, twin)}

    def copies(block, part, route, own=False):
        lane, device = routes[route]
        return [
            remote(part_of(ins[i] if own else outs[i].at[block], part), part_of(outs[i].at[block], part),
                   send.at[i, part, lane, block], recv.at[i, part, block], device)
            for i in range(count)
        ]

    def forward(block, part, *ways, own=False):
        for route in ways:
            for copy in copies(block, part, route, own):
                copy.start()

    def arrived(block, part):
        for copy in copies(block, part, "twin"):
            copy.wait_recv()

    loads = [pltpu.make_async_copy(ins[i], held[i], own_in.at[i]) for i in range(count)]
    for load in loads:
        load.start()
    for part in range(PARTS):
        pl.when(z < LINE - 1)(functools.partial(forward, mine, part, "up", own=True))
        pl.when(z > 0)(functools.partial(forward, mine, part, "down", own=True))
        forward(mine, part, "one", "two", "twin", own=True)
    stores = [pltpu.make_async_copy(held[i], outs[i].at[mine], own_out.at[i]) for i in range(count)]
    for load, store in zip(loads, stores):
        load.wait()
        store.start()

    def line_step(step, part):
        @pl.when(z - step >= 0)
        def _():
            block = at.block(z - step, 0, 0)
            arrived(block, part)
            pl.when(z < LINE - 1)(functools.partial(forward, block, part, "up"))
            forward(block, part, "one", "two", "twin")

        @pl.when(z + step < LINE)
        def _():
            block = at.block(z + step, 0, 0)
            arrived(block, part)
            pl.when(z > 0)(functools.partial(forward, block, part, "down"))
            forward(block, part, "one", "two", "twin")

    def face_step(step, part, first, second):
        def take(block):
            arrived(block, part)
            if not second:
                forward(block, part, "two")
            forward(block, part, "twin")
        if step == 0:
            take(at.block(z, first, second))
        else:
            @pl.when(z - step >= 0)
            def _():
                take(at.block(z - step, first, second))

            @pl.when(z + step < LINE)
            def _():
                take(at.block(z + step, first, second))

    for step in range(LINE + 2):
        for part in range(PARTS):
            if 1 <= step < LINE:
                line_step(step, part)
            if 0 <= step - 1 < LINE:
                face_step(step - 1, part, 1, 0)
                face_step(step - 1, part, 0, 1)
            if 0 <= step - 2 < LINE:
                face_step(step - 2, part, 1, 1)
    for first in (0, 1):
        for second in (0, 1):
            for line in range(LINE):
                for part in range(PARTS):
                    arrived(at.block(line, first, second, 1), part)
    for store in stores:
        store.wait()

    def sent(block, part, *ways):
        for route in ways:
            for copy in copies(block, part, route):
                copy.wait_send()

    for line in range(LINE):
        for part in range(PARTS):
            block = at.block(line, 0, 0)
            pl.when((z >= line) & (z < LINE - 1))(functools.partial(sent, block, part, "up"))
            pl.when((z <= line) & (z > 0))(functools.partial(sent, block, part, "down"))
            sent(block, part, "one", "two", "twin")
            sent(at.block(line, 1, 0), part, "two", "twin")
            sent(at.block(line, 0, 1), part, "twin")
            sent(at.block(line, 1, 1), part, "twin")


def gather_blocks(collective_id, *arrays):
    count, devices = len(arrays), lax.axis_size("wide") * lax.axis_size("narrow")
    moved = sum(a.size * a.dtype.itemsize for a in arrays)
    return pl.pallas_call(
        functools.partial(gather_kernel, count),
        name=f"gather_blocks_{collective_id}",
        out_shape=tuple(jax.ShapeDtypeStruct((devices,) + a.shape, a.dtype) for a in arrays),
        in_specs=[pl.BlockSpec(memory_space=pl.ANY)] * count,
        out_specs=tuple(pl.BlockSpec(memory_space=pl.ANY) for _ in arrays),
        scratch_shapes=[pltpu.VMEM(a.shape, a.dtype) for a in arrays]
        + [
            pltpu.SemaphoreType.DMA((count, PARTS, 5, devices)),
            pltpu.SemaphoreType.DMA((count, PARTS, devices)),
            pltpu.SemaphoreType.DMA((count,)),
            pltpu.SemaphoreType.DMA((count,)),
        ],
        compiler_params=pltpu.CompilerParams(collective_id=collective_id, has_side_effects=True),
        cost_estimate=pl.CostEstimate(flops=0, transcendentals=0, bytes_accessed=2 * devices * moved),
    )(*arrays)


ORDER = (3, 0, 2, 1)


def scatter_kernel(count, *refs):
    ins, outs = refs[:count], refs[count:2 * count]
    rest = [refs[2 * count + k * count:2 * count + (k + 1) * count] for k in range(6)]
    acc, from_twin, from_two, from_one, from_below, from_above = rest
    load_sem, store_sem, send, recv = refs[8 * count:]
    at = Place()
    z = at.z
    up, down = at.device(z + 1, 0, 0), at.device(z - 1, 0, 0)
    one, two, twin = at.device(z, 1, 0), at.device(z, 0, 1), at.device(z, 0, 0, 1)
    greet([(one, None), (two, None), (twin, None), (up, z < LINE - 1), (down, z > 0)])
    units = [(line, part) for line in ORDER for part in range(PARTS)]
    corners = [(1, 1), (1, 0), (0, 1), (0, 0)]

    def slot(line, second, first):
        return second * 8 + first * 4 + line

    def load(i, part, line, second, first):
        here = slot(line, second, first)
        return pltpu.make_async_copy(part_of(ins[i].at[at.block(line, first, second)], part),
                                     part_of(acc[i].at[here], part), load_sem.at[i, part, here])

    def hop(i, part, source, target, lane, device):
        return remote(part_of(source, part), part_of(target, part), send.at[i, part, lane], recv.at[i, part, lane], device)

    def to_twin(i, part, line, second, first):
        here = slot(line, second, first)
        return hop(i, part, ins[i].at[at.block(line, first, second, 1)], from_twin[i].at[here], here, twin)

    def to_two(i, part, line, first):
        return hop(i, part, acc[i].at[slot(line, 1, first)], from_two[i].at[first * 4 + line], 16 + first * 4 + line, two)

    def to_one(i, part, line):
        return hop(i, part, acc[i].at[slot(line, 0, 1)], from_one[i].at[line], 24 + line, one)

    def rise(i, part, line):
        return hop(i, part, acc[i].at[line], from_below[i].at[line], 28 + line, up)

    def fall(i, part, line):
        return hop(i, part, acc[i].at[line], from_above[i].at[line], 32 + line, down)

    def begin(line, part):
        for second, first in corners:
            for i in range(count):
                to_twin(i, part, line, second, first).start()
                load(i, part, line, second, first).start()

    def gathered(line, part, second, first):
        for i in range(count):
            load(i, part, line, second, first).wait()
            to_twin(i, part, line, second, first).wait_recv()
            sources = [from_twin[i].at[slot(line, second, first)]]
            if not second:
                to_two(i, part, line, first).wait_recv()
                sources.append(from_two[i].at[first * 4 + line])
                if not first:
                    to_one(i, part, line).wait_recv()
                    sources.append(from_one[i].at[line])
            add_into(part_of(acc[i].at[slot(line, second, first)], part), *[part_of(r, part) for r in sources])
            if second:
                to_two(i, part, line, first).start()
            elif first:
                to_one(i, part, line).start()

    def line_hop(line, part, hops):
        @pl.when(z == hops)
        def _():
            for i in range(count):
                if 0 < hops <= line:
                    rise(i, part, line).wait_recv()
                    add_into(part_of(acc[i].at[line], part), part_of(from_below[i].at[line], part))
                if hops < line:
                    rise(i, part, line).start()

        @pl.when(z == LINE - 1 - hops)
        def _():
            for i in range(count):
                if 0 < hops <= LINE - 1 - line:
                    fall(i, part, line).wait_recv()
                    add_into(part_of(acc[i].at[line], part), part_of(from_above[i].at[line], part))
                if hops < LINE - 1 - line:
                    fall(i, part, line).start()

    begin(*units[0])
    begin(*units[1])
    for step in range(len(units) + 2 + LINE):
        if step + 2 < len(units):
            begin(*units[step + 2])
        if step < len(units):
            gathered(*units[step], 1, 1)
            gathered(*units[step], 1, 0)
        if 0 <= step - 1 < len(units):
            gathered(*units[step - 1], 0, 1)
        if 0 <= step - 2 < len(units):
            gathered(*units[step - 2], 0, 0)
        for hops in range(LINE):
            if 0 <= step - 2 - hops < len(units):
                line_hop(*units[step - 2 - hops], hops)
    stores = [pltpu.make_async_copy(acc[i].at[z], outs[i], store_sem.at[i]) for i in range(count)]
    for store in stores:
        store.start()
    for line, part in units:
        for i in range(count):
            for second, first in corners:
                to_twin(i, part, line, second, first).wait_send()
            to_two(i, part, line, 0).wait_send()
            to_two(i, part, line, 1).wait_send()
            to_one(i, part, line).wait_send()
            if line > 0:
                pl.when(z < line)(rise(i, part, line).wait_send)
            if line < LINE - 1:
                pl.when(z > line)(fall(i, part, line).wait_send)
    for store in stores:
        store.wait()


def scatter_blocks(collective_id, *arrays):
    count = len(arrays)

    def slots(n):
        return [pltpu.VMEM((n,) + a.shape[1:], a.dtype) for a in arrays]
    return pl.pallas_call(
        functools.partial(scatter_kernel, count),
        name=f"scatter_blocks_{collective_id}",
        out_shape=tuple(jax.ShapeDtypeStruct(a.shape[1:], a.dtype) for a in arrays),
        in_specs=[pl.BlockSpec(memory_space=pl.ANY)] * count,
        out_specs=tuple(pl.BlockSpec(memory_space=pl.ANY) for _ in arrays),
        scratch_shapes=slots(16) + slots(16) + slots(8) + slots(4) + slots(4) + slots(4)
        + [
            pltpu.SemaphoreType.DMA((count, PARTS, 16)),
            pltpu.SemaphoreType.DMA((count,)),
            pltpu.SemaphoreType.DMA((count, PARTS, 36)),
            pltpu.SemaphoreType.DMA((count, PARTS, 36)),
        ],
        compiler_params=pltpu.CompilerParams(
            collective_id=collective_id, has_side_effects=True, vmem_limit_bytes=60 << 20),
        cost_estimate=pl.CostEstimate(
            flops=0, transcendentals=0, bytes_accessed=sum(a.size * a.dtype.itemsize for a in arrays)),
    )(*arrays)


def sum_task(at, kind, rows, source, result, held, from_pair, from_below, from_above, load_sem, send, recv, delay):
    z, x = at.z, at.x
    pair = ((z * 2 + 1 - x), at.y * 2 + at.core)
    up, down = ((z + 1) * 2 + x, at.y * 2 + at.core), ((z - 1) * 2 + x, at.y * 2 + at.core)
    pair_first = kind == "pair"
    for _ in range(delay):
        yield

    def part(ref, line, face):
        return ref.at[line, face, rows]

    if pair_first:
        def load(line):
            return pltpu.make_async_copy(part(source, line, x), held.at[line], load_sem.at[line])

        def give(line):
            return remote(part(source, line, 1 - x), from_pair.at[line], send.at[0, line], recv.at[0, line], pair)
        for line in ORDER:
            give(line).start()
            load(line).start()
        yield
        yield
        for line in ORDER:
            load(line).wait()
            give(line).wait_recv()
            add_into(held.at[line], from_pair.at[line])
    else:
        def load(line):
            return pltpu.make_async_copy(source.at[line, :, rows], held.at[line], load_sem.at[line])
        for line in ORDER:
            load(line).start()
        for line in ORDER:
            load(line).wait()

    def add(target, extra):
        if pair_first:
            add_into(target, extra)
        else:
            for face in (0, 1):
                add_into(target.at[face], extra.at[face])

    def rise(line):
        return remote(held.at[line], from_below.at[line], send.at[1, line], recv.at[1, line], up)

    def fall(line):
        return remote(held.at[line], from_above.at[line], send.at[2, line], recv.at[2, line], down)

    for line in range(LINE - 1, 0, -1):
        other = LINE - 1 - line

        @pl.when(z < line)
        def _():
            @pl.when(z > 0)
            def _():
                rise(line).wait_recv()
                add(held.at[line], from_below.at[line])
            rise(line).start()

        @pl.when(z > other)
        def _():
            @pl.when(z < LINE - 1)
            def _():
                fall(other).wait_recv()
                add(held.at[other], from_above.at[other])
            fall(other).start()
        yield

    @pl.when(z > 0)
    def _():
        rise(z).wait_recv()
        add(held.at[z], from_below.at[z])

    @pl.when(z < LINE - 1)
    def _():
        fall(z).wait_recv()
        add(held.at[z], from_above.at[z])

    if pair_first:
        def over(line):
            return remote(part(result, line, x), part(result, line, x), send.at[3, line], recv.at[3, line * 2 + x], pair)

        def other_over(line):
            return remote(part(result, line, 1 - x), part(result, line, 1 - x), send.at[3, line],
                          recv.at[3, line * 2 + 1 - x], pair)

        def climb(line):
            return remote(part(result, line, x), part(result, line, x), send.at[4, line], recv.at[3, line * 2 + x], up)

        def sink(line):
            return remote(part(result, line, x), part(result, line, x), send.at[5, line], recv.at[3, line * 2 + x], down)
        own = pltpu.make_async_copy(held.at[z], part(result, z, x), load_sem.at[4])
    else:
        mine = held.at[z]
        swap = remote(mine.at[1 - x], from_pair, send.at[0, 0], recv.at[0, 0], pair)
        swap.start()
        yield
        swap.wait_recv()
        add_into(mine.at[x], from_pair)
        own = pltpu.make_async_copy(mine.at[x], part(result, z, x), load_sem.at[4])

        def over_block(face):
            return remote(part(result, z, face), part(result, z, face), send.at[3, 0], recv.at[3, face], pair)

        def climb(line):
            return remote(result.at[line, :, rows], result.at[line, :, rows], send.at[4, line], recv.at[3, 4 + line], up)

        def sink(line):
            return remote(result.at[line, :, rows], result.at[line, :, rows], send.at[5, line], recv.at[3, 4 + line], down)
    own.start()
    own.wait()
    if pair_first:
        over(z).start()
    else:
        over_block(x).start()
        yield
        over_block(1 - x).wait_recv()

    @pl.when(z < LINE - 1)
    def _():
        climb(z).start()

    @pl.when(z > 0)
    def _():
        sink(z).start()
    yield
    for step in range(1, LINE):
        @pl.when(z - step >= 0)
        def _():
            climb(z - step).wait_recv()

            @pl.when(z < LINE - 1)
            def _():
                climb(z - step).start()
            if pair_first:
                over(z - step).start()

        @pl.when(z + step < LINE)
        def _():
            sink(z + step).wait_recv()

            @pl.when(z > 0)
            def _():
                sink(z + step).start()
            if pair_first:
                over(z + step).start()
        yield
    if pair_first:
        for line in range(LINE):
            other_over(line).wait_recv()
    for line in range(LINE):
        if pair_first:
            give(line).wait_send()
            over(line).wait_send()
        if line > 0:
            pl.when(z < line)(rise(line).wait_send)
        if line < LINE - 1:
            pl.when(z > line)(fall(line).wait_send)
        pl.when((z >= line) & (z < LINE - 1))(climb(line).wait_send)
        pl.when((z <= line) & (z > 0))(sink(line).wait_send)
    if not pair_first:
        swap.wait_send()
        over_block(x).wait_send()


CHUNK = 64


def sum_wide_kernel(plan, count, *refs):
    ins, outs, rest = refs[:count], refs[count:2 * count], list(refs[2 * count:])
    at = Place()
    pair = (at.z * 2 + 1 - at.x, at.y * 2 + at.core)
    up, down = ((at.z + 1) * 2 + at.x, at.y * 2 + at.core), ((at.z - 1) * 2 + at.x, at.y * 2 + at.core)
    greet([(pair, None), (up, at.z < LINE - 1), (down, at.z > 0)])
    load_sem, send, recv = rest[-3:]
    tasks = []
    for number, (which, begin, kind, delay) in enumerate(plan):
        held, from_pair, from_below, from_above = rest[4 * number:4 * number + 4]
        tasks.append(sum_task(at, kind, pl.ds(begin, CHUNK), ins[which], outs[which], held, from_pair, from_below,
                              from_above, load_sem.at[number], send.at[number], recv.at[number], delay))
    while tasks:
        tasks = [task for task in tasks if next(task, tasks) is not tasks]


def sum_wide(collective_id, plan, *arrays):
    count, steps = len(arrays), len(plan)
    scratch = []
    for which, _, kind, _ in plan:
        columns, dtype = arrays[which].shape[3], arrays[which].dtype
        lead = () if kind == "pair" else (2,)
        block = lead + (CHUNK, columns)
        scratch += [
            pltpu.VMEM((LINE,) + block, dtype),
            pltpu.VMEM(((LINE,) if kind == "pair" else ()) + (CHUNK, columns), dtype),
            pltpu.VMEM((LINE,) + block, dtype),
            pltpu.VMEM((LINE,) + block, dtype),
        ]
    moved = sum(a.size * a.dtype.itemsize for a in arrays)
    return pl.pallas_call(
        functools.partial(sum_wide_kernel, plan, count),
        name=f"sum_wide_{collective_id}",
        out_shape=tuple(jax.ShapeDtypeStruct(a.shape, a.dtype) for a in arrays),
        in_specs=[pl.BlockSpec(memory_space=pl.ANY)] * count,
        out_specs=tuple(pl.BlockSpec(memory_space=pl.ANY) for _ in arrays),
        scratch_shapes=scratch + [
            pltpu.SemaphoreType.DMA((steps, 5)),
            pltpu.SemaphoreType.DMA((steps, 6, 4)),
            pltpu.SemaphoreType.DMA((steps, 4, 8)),
        ],
        compiler_params=pltpu.CompilerParams(
            collective_id=collective_id, has_side_effects=True, vmem_limit_bytes=48 << 20),
        cost_estimate=pl.CostEstimate(flops=0, transcendentals=0, bytes_accessed=2 * moved),
    )(*arrays)


def own_exchange():
    return lax.axis_size("wide") == 8 and lax.axis_size("narrow") == 4


def gather_all(*arrays):
    if own_exchange():
        return gather_blocks(1, *arrays)
    return tuple(lax.all_gather(a, BOTH, axis=0) for a in arrays)


def scatter_all(*arrays):
    if own_exchange():
        return scatter_blocks(2, *arrays)
    return tuple(lax.psum_scatter(a, BOTH, scatter_dimension=0) for a in arrays)


SUM_PLAN = ((0, 0, "pair", 0), (1, 0, "line", 0), (0, 64, "pair", 1), (0, 128, "pair", 2), (0, 192, "pair", 3))


def total_wide(joined, out_part):
    if own_exchange():
        shapes = joined.shape, out_part.shape
        dealt = [a.reshape(LINE, 2, a.shape[0] // 8, a.shape[1]) for a in (joined, out_part)]
        return tuple(a.reshape(shape) for a, shape in zip(sum_wide(3, SUM_PLAN, *dealt), shapes))
    return lax.psum((joined, out_part), "wide")


def local(
    block_input,
    attn_gain,
    query_weight,
    key_weight,
    value_weight,
    query_gain,
    key_gain,
    out_weight,
    moe_gain,
    router_weight,
    gate_weight,
    up_weight,
    down_weight,
    segment_ids,
    expert_ids,
    out_cotangent,
):
    group_rows, model_width = block_input.shape
    own_rows = out_cotangent.shape[0]
    local_width = query_weight.shape[1]
    head_size = HEAD_DIM
    local_heads = local_width // head_size
    wide_size = lax.axis_size("wide")
    experts_all = router_weight.shape[1]
    experts_here = gate_weight.shape[0]
    choose_count = expert_ids.shape[1]
    capacity = 3 * own_rows * choose_count // (2 * experts_all)
    row_begin = lax.axis_index("narrow") * own_rows
    blocks = group_rows // QBLK
    highest_precision = lax.Precision.HIGHEST
    block_count = wide_size * lax.axis_size("narrow")
    chosen = (expert_ids[:, :, None] == jnp.arange(experts_all)[None, None, :]).any(axis=1)
    token_order = jnp.arange(own_rows)
    earlier = jnp.dot(
        (token_order[:, None] > token_order[None, :]).astype(jnp.bfloat16),
        chosen.astype(jnp.bfloat16),
        preferred_element_type=jnp.float32,
    )
    grads_all = lax.all_gather(out_cotangent, BOTH, axis=0)
    inputs_all = block_input.astype(jnp.float32)
    normed_one = rms_scale(inputs_all, attn_gain.astype(jnp.float32)).astype(jnp.bfloat16)
    joined_weight = jnp.concatenate([query_weight, key_weight, value_weight], axis=1)
    projected = jnp.dot(normed_one, joined_weight, preferred_element_type=jnp.float32)
    query_proj = projected[:, :local_width]
    key_proj = projected[:, local_width : 2 * local_width]
    value_proj = projected[:, 2 * local_width :]
    rope_cos, rope_sin = rope_tables(group_rows, head_size)
    query_total, key_total = lax.psum(
        (jnp.sum(query_proj * query_proj, axis=1), jnp.sum(key_proj * key_proj, axis=1)), "narrow"
    )
    query_inverse = lax.rsqrt(query_total / model_width + norm_epsilon)[:, None]
    key_inverse = lax.rsqrt(key_total / model_width + norm_epsilon)[:, None]
    query_scale = query_gain.astype(jnp.float32)
    key_scale = key_gain.astype(jnp.float32)
    query_normed = query_proj * query_inverse * query_scale
    key_normed = key_proj * key_inverse * key_scale

    def turn_both(query_in, key_in):
        return (
            rotate(query_in, rope_cos, rope_sin, head_size) * head_size ** (-0.5),
            rotate(key_in, rope_cos, rope_sin, head_size),
        )

    (turned_query, turned_key), turn_back = jax.vjp(turn_both, query_normed, key_normed)
    query_heads = turned_query.astype(jnp.bfloat16).reshape(group_rows, local_heads, head_size)
    key_heads = turned_key.astype(jnp.bfloat16).reshape(group_rows, local_heads, head_size)
    value_heads = value_proj.astype(jnp.bfloat16).reshape(group_rows, local_heads, head_size)
    positions = jnp.arange(group_rows)

    def block_scores(block_index):
        block_begin = block_index * QBLK
        query_block = lax.dynamic_slice_in_dim(query_heads, block_begin, QBLK, 0)
        query_segments = lax.dynamic_slice_in_dim(segment_ids, block_begin, QBLK, 0)
        query_places = block_begin + jnp.arange(QBLK)
        allowed = (query_segments[:, None] == segment_ids[None, :]) & (
            query_places[:, None] >= positions[None, :]
        )
        scores = jnp.einsum(
            "qhd,khd->hqk", query_block, key_heads, preferred_element_type=jnp.float32
        )
        return (query_block, jnp.where(allowed[None], scores, masked_score))

    def attend(block_index):
        query_block, scores = block_scores(block_index)
        highest = jnp.max(scores, axis=-1, keepdims=True)
        weights = jnp.exp(scores - highest)
        totals = jnp.sum(weights, axis=-1, keepdims=True)
        probs_low = (weights / totals).astype(jnp.bfloat16)
        mixed_rows = jnp.einsum(
            "hqk,khd->qhd", probs_low, value_heads, preferred_element_type=jnp.float32
        )
        return (mixed_rows, highest + jnp.log(totals))

    mixed_blocks, log_totals = lax.map(attend, jnp.arange(blocks))
    heads_out = mixed_blocks.reshape(group_rows, local_width).astype(jnp.bfloat16)
    attn_own = lax.psum_scatter(
        jnp.dot(heads_out, out_weight, preferred_element_type=jnp.float32).astype(jnp.bfloat16),
        "narrow",
        scatter_dimension=0,
        tiled=True,
    ).astype(jnp.float32)
    input_own = lax.dynamic_slice_in_dim(inputs_all, row_begin, own_rows, 0)
    hidden = input_own + attn_own
    normed_two_full, norm_two_back = jax.vjp(rms_scale, hidden, moe_gain.astype(jnp.float32))
    normed_two = normed_two_full.astype(jnp.bfloat16)
    logits = jnp.dot(normed_two, router_weight, preferred_element_type=jnp.float32)
    route_probs = jax.nn.softmax(logits, axis=-1)
    rows_all, routes_all = gather_all(
        normed_two, jnp.concatenate([route_probs.T, jnp.where(chosen, earlier, -1.0).T], axis=0)
    )
    expert_begin = lax.axis_index("wide") * experts_here
    probs_here = lax.dynamic_slice_in_dim(routes_all, expert_begin, experts_here, 1)
    places_here = lax.dynamic_slice_in_dim(routes_all, experts_all + expert_begin, experts_here, 1)
    pick = places_here[:, :, None, :] == jnp.arange(capacity, dtype=jnp.float32)[None, None, :, None]
    pick_low = pick.astype(jnp.bfloat16)
    slot_gate = jnp.sum(jnp.where(pick, probs_here[:, :, None, :], 0.0), axis=-1)
    slot_gate = slot_gate.transpose(1, 0, 2).reshape(experts_here, block_count * capacity, 1)

    def spread(rows):
        out = jnp.einsum(
            "best,btd->ebsd",
            pick_low,
            rows,
            preferred_element_type=jnp.float32,
        )
        return out.astype(jnp.bfloat16).reshape(experts_here, block_count * capacity, model_width)

    def collect(slots):
        out = jnp.einsum(
            "best,ebsd->btd",
            pick_low,
            slots.reshape(experts_here, block_count, capacity, model_width),
            preferred_element_type=jnp.float32,
        )
        return out.astype(jnp.bfloat16)

    slot_rows = spread(rows_all)
    slot_grads = spread(grads_all)
    gate_pre = jnp.einsum("erd,edf->erf", slot_rows, gate_weight, preferred_element_type=jnp.float32)
    up_pre = jnp.einsum("erd,edf->erf", slot_rows, up_weight, preferred_element_type=jnp.float32)
    activated, unit_back = jax.vjp(gated_unit, gate_pre, up_pre)
    gated_act = (activated * slot_gate).astype(jnp.bfloat16)
    raw_act_grad = jnp.einsum(
        "erd,efd->erf", slot_grads, down_weight, preferred_element_type=jnp.float32
    )
    slot_gate_grads = jnp.sum(activated * raw_act_grad, axis=-1)
    gate_grad_full, up_grad_full = unit_back(raw_act_grad * slot_gate)
    gate_grad_low = gate_grad_full.astype(jnp.bfloat16)
    up_grad_low = up_grad_full.astype(jnp.bfloat16)
    gate_grad_parts = jnp.einsum(
        "best,ebs->bet",
        pick.astype(jnp.float32),
        slot_gate_grads.reshape(experts_here, block_count, capacity),
        precision=highest_precision,
    )
    gate_grad_wide = lax.dynamic_update_slice_in_dim(
        jnp.zeros((block_count, experts_all, own_rows), jnp.float32), gate_grad_parts, expert_begin, 1
    )
    back_slots = jnp.einsum(
        "erf,edf->erd", gate_grad_low, gate_weight, preferred_element_type=jnp.float32
    ) + jnp.einsum("erf,edf->erd", up_grad_low, up_weight, preferred_element_type=jnp.float32)
    out_slots = jnp.einsum(
        "erf,efd->erd", gated_act, down_weight, preferred_element_type=jnp.float32
    )
    rows_back, prob_grads, moe_out = scatter_all(
        collect(back_slots.astype(jnp.bfloat16)), gate_grad_wide, collect(out_slots.astype(jnp.bfloat16))
    )
    rows_back, prob_grads, moe_out = rows_back.astype(jnp.float32), prob_grads.T, moe_out.astype(jnp.float32)
    down_weight_grad = jnp.einsum(
        "erf,erd->efd", gated_act, slot_grads, preferred_element_type=jnp.float32
    )
    gate_weight_grad = jnp.einsum(
        "erd,erf->edf", slot_rows, gate_grad_low, preferred_element_type=jnp.float32
    )
    up_weight_grad = jnp.einsum(
        "erd,erf->edf", slot_rows, up_grad_low, preferred_element_type=jnp.float32
    )
    block_output = (hidden + moe_out).astype(jnp.bfloat16)
    logit_grads = route_probs * (
        prob_grads - jnp.sum(route_probs * prob_grads, axis=-1, keepdims=True)
    )
    router_part = lax.dot_general(
        normed_two.astype(jnp.float32),
        logit_grads,
        (((0,), (0,)), ((), ())),
        precision=highest_precision,
    )
    router_back = lax.dot_general(
        logit_grads,
        router_weight.astype(jnp.float32),
        (((1,), (1,)), ((), ())),
        precision=highest_precision,
    )
    normed_two_grad = rows_back + router_back
    cotangent_full = out_cotangent.astype(jnp.float32)
    hidden_path, moe_gain_part = norm_two_back(normed_two_grad)
    hidden_grad = cotangent_full + hidden_path
    hidden_grad_low = hidden_grad.astype(jnp.bfloat16)
    gathered_piece = lax.all_gather(hidden_grad_low, "narrow", axis=0, tiled=True)
    heads_grad_acc = contract_last(gathered_piece, out_weight)
    out_weight_acc = contract_rows(heads_out, gathered_piece)
    heads_grad_low = heads_grad_acc.astype(jnp.bfloat16).reshape(group_rows, local_heads, head_size)

    def back_block(running, items):
        key_acc, value_acc = running
        block_index, log_total = items
        query_block, scores = block_scores(block_index)
        probs = jnp.exp(scores - log_total)
        probs_low = probs.astype(jnp.bfloat16)
        grad_block = lax.dynamic_slice_in_dim(heads_grad_low, block_index * QBLK, QBLK, 0)
        weight_grads = jnp.einsum(
            "qhd,khd->hqk", grad_block, value_heads, preferred_element_type=jnp.float32
        )
        row_dots = jnp.sum(probs * weight_grads, axis=-1, keepdims=True)
        score_grads = (probs * (weight_grads - row_dots)).astype(jnp.bfloat16)
        query_grad_block = jnp.einsum(
            "hqk,khd->qhd", score_grads, key_heads, preferred_element_type=jnp.float32
        )
        key_acc = key_acc + jnp.einsum(
            "hqk,qhd->khd", score_grads, query_block, preferred_element_type=jnp.float32
        )
        value_acc = value_acc + jnp.einsum(
            "hqk,qhd->khd", probs_low, grad_block, preferred_element_type=jnp.float32
        )
        return ((key_acc, value_acc), query_grad_block)

    zero_heads = jnp.zeros((group_rows, local_heads, head_size), jnp.float32)
    (key_grad, value_grad), query_grads = lax.scan(
        back_block, (zero_heads, zero_heads), (jnp.arange(blocks), log_totals)
    )
    query_normed_grad, key_normed_grad = turn_back(
        (query_grads.reshape(group_rows, local_width), key_grad.reshape(group_rows, local_width))
    )
    query_gain_part = jnp.sum(query_normed_grad * query_proj * query_inverse, axis=0)
    key_gain_part = jnp.sum(key_normed_grad * key_proj * key_inverse, axis=0)
    query_gained = query_normed_grad * query_scale
    key_gained = key_normed_grad * key_scale
    query_dot, key_dot = lax.psum(
        (jnp.sum(query_proj * query_gained, axis=1), jnp.sum(key_proj * key_gained, axis=1)),
        "narrow",
    )
    query_proj_grad = (
        query_inverse * query_gained
        - query_proj * query_inverse**3 * (query_dot / model_width)[:, None]
    )
    key_proj_grad = (
        key_inverse * key_gained - key_proj * key_inverse**3 * (key_dot / model_width)[:, None]
    )
    proj_grad_low = jnp.concatenate(
        [query_proj_grad, key_proj_grad, value_grad.reshape(group_rows, local_width)], axis=1
    ).astype(jnp.bfloat16)
    joined_grad = contract_rows(normed_one, proj_grad_low)
    normed_one_grad = lax.psum_scatter(
        contract_last(proj_grad_low, joined_weight).astype(jnp.bfloat16),
        "narrow",
        scatter_dimension=0,
        tiled=True,
    ).astype(jnp.float32)
    normed_again, norm_one_back = jax.vjp(rms_scale, input_own, attn_gain.astype(jnp.float32))
    input_path, attn_gain_part = norm_one_back(normed_one_grad)
    input_grad = (hidden_grad + input_path).astype(jnp.bfloat16)
    joined_total, out_total = total_wide(joined_grad.astype(jnp.bfloat16), out_weight_acc.astype(jnp.bfloat16))
    joined_total, out_weight_grad = joined_total.astype(jnp.float32), out_total.astype(jnp.float32)
    query_weight_grad = joined_total[:, :local_width]
    key_weight_grad = joined_total[:, local_width : 2 * local_width]
    value_weight_grad = joined_total[:, 2 * local_width :]
    query_gain_grad, key_gain_grad = lax.psum((query_gain_part, key_gain_part), "wide")
    router_weight_grad, attn_gain_grad, moe_gain_grad = lax.psum(
        (router_part, attn_gain_part, moe_gain_part), ("wide", "narrow")
    )
    return (
        block_output,
        input_grad,
        attn_gain_grad,
        query_weight_grad,
        key_weight_grad,
        value_weight_grad,
        query_gain_grad,
        key_gain_grad,
        out_weight_grad,
        moe_gain_grad,
        router_weight_grad,
        gate_weight_grad,
        up_weight_grad,
        down_weight_grad,
    )


def solution(mesh):
    in_specs = (
        P("wide", None),
        P(),
        P(None, "narrow"),
        P(None, "narrow"),
        P(None, "narrow"),
        P("narrow"),
        P("narrow"),
        P("narrow", None),
        P(),
        P(),
        P("wide", None, "narrow"),
        P("wide", None, "narrow"),
        P("wide", "narrow", None),
        P("wide"),
        P(("wide", "narrow"), None),
        P(("wide", "narrow"), None),
    )
    out_specs = (
        P(("wide", "narrow"), None),
        P(("wide", "narrow"), None),
        P(),
        P(None, "narrow"),
        P(None, "narrow"),
        P(None, "narrow"),
        P("narrow"),
        P("narrow"),
        P("narrow", None),
        P(),
        P(),
        P("wide", None, "narrow"),
        P("wide", None, "narrow"),
        P("wide", "narrow", None),
    )
    return jax.shard_map(local, mesh=mesh, in_specs=in_specs, out_specs=out_specs, check_vma=False)
```

```python
import functools

import jax
import jax.numpy as jnp
from jax import lax
from jax.experimental import pallas as pl
from jax.experimental.pallas import tpu as pltpu
from jax.sharding import PartitionSpec as P

HEAD_DIM = 128
QBLK = 512


norm_epsilon = 1e-05
rope_base = 10000.0
masked_score = -1e30


def rms_scale(values, gain):
    inverse = lax.rsqrt(jnp.mean(values * values, axis=-1, keepdims=True) + norm_epsilon)
    return values * inverse * gain


def rope_tables(length, head_size):
    half_size = head_size // 2
    exponent = jnp.arange(half_size, dtype=jnp.float32) * (2.0 / head_size)
    angle = jnp.arange(length, dtype=jnp.float32)[:, None] * (rope_base ** (-exponent))[None, :]
    return (jnp.cos(angle), jnp.sin(angle))


def rotate(normed, rope_cos, rope_sin, head_size):
    tokens_here = normed.shape[0]
    by_head = normed.reshape(tokens_here, -1, head_size)
    half_size = head_size // 2
    first_half = by_head[..., :half_size]
    second_half = by_head[..., half_size:]
    cos_rows = rope_cos[:, None, :]
    sin_rows = rope_sin[:, None, :]
    turned = jnp.concatenate(
        [
            first_half * cos_rows - second_half * sin_rows,
            second_half * cos_rows + first_half * sin_rows,
        ],
        axis=-1,
    )
    return turned.reshape(tokens_here, -1)


def gated_unit(gate_pre, up_pre):
    return jax.nn.silu(gate_pre) * up_pre


def contract_rows(left, right):
    return lax.dot_general(
        left, right, (((0,), (0,)), ((), ())), preferred_element_type=jnp.float32
    )


def contract_last(left, right):
    return lax.dot_general(
        left, right, (((1,), (1,)), ((), ())), preferred_element_type=jnp.float32
    )


BOTH = ("wide", "narrow")


MESH = pl.DeviceIdType.MESH
LINE = 4
ADD_ROWS = 16


def flip(bit, on):
    return bit + on * (1 - 2 * bit)


class Place:
    def __init__(self):
        wide, narrow = lax.axis_index("wide"), lax.axis_index("narrow")
        self.z, self.x = wide // 2, lax.rem(wide, 2)
        self.y, self.core = narrow // 2, lax.rem(narrow, 2)

    def device(self, z, first, second, other_core=0):
        core = flip(self.core, other_core)
        x = flip(self.x, first * (1 - core) + second * core)
        y = flip(self.y, first * core + second * (1 - core))
        return (z * 2 + x, y * 2 + core)

    def across(self, other_core=0):
        return (self.z * 2 + self.x, (1 - self.y) * 2 + flip(self.core, other_core))

    def block(self, z, first, second, other_core=0):
        wide, narrow = self.device(z, first, second, other_core)
        return wide * 4 + narrow


def greet(devices_and_conditions):
    barrier = pltpu.get_barrier_semaphore()
    total = 0
    for device, condition in devices_and_conditions:
        if condition is None:
            pl.semaphore_signal(barrier, inc=1, device_id=device, device_id_type=MESH)
            total = total + 1
        else:
            @pl.when(condition)
            def _():
                pl.semaphore_signal(barrier, inc=1, device_id=device, device_id_type=MESH)
            total = total + condition.astype(jnp.int32)
    pl.semaphore_wait(barrier, total)


def add_into(target, *sources):
    rows = target.shape[0]
    step = ADD_ROWS if rows % ADD_ROWS == 0 else 8

    @pl.loop(0, rows // step)
    def _(i):
        part = pl.ds(pl.multiple_of(i * step, step), step)
        total = target[part].astype(jnp.float32)
        for source in sources:
            total = total + source[part].astype(jnp.float32)
        target[part] = total.astype(target.dtype)


def remote(source, target, send, recv, device):
    return pltpu.make_async_remote_copy(
        src_ref=source, dst_ref=target, send_sem=send, recv_sem=recv,
        device_id=device, device_id_type=MESH,
    )


PARTS = 2


def part_of(ref, part):
    rows = ref.shape[0] // PARTS
    return ref.at[pl.ds(part * rows, rows)]


def gather_kernel(count, *refs):
    ins, outs, held = refs[:count], refs[count:2 * count], refs[2 * count:3 * count]
    send, recv, own_in, own_out = refs[3 * count:]
    at = Place()
    z = at.z
    up, down = at.device(z + 1, 0, 0), at.device(z - 1, 0, 0)
    one, two, twin = at.device(z, 1, 0), at.device(z, 0, 1), at.device(z, 0, 0, 1)
    greet([(one, None), (two, None), (twin, None), (up, z < LINE - 1), (down, z > 0)])
    mine = at.block(z, 0, 0)
    routes = {"up": (0, up), "down": (1, down), "one": (2, one), "two": (3, two), "twin": (4, twin)}

    def copies(block, part, route, own=False):
        lane, device = routes[route]
        return [
            remote(part_of(ins[i] if own else outs[i].at[block], part), part_of(outs[i].at[block], part),
                   send.at[i, part, lane, block], recv.at[i, part, block], device)
            for i in range(count)
        ]

    def forward(block, part, *ways, own=False):
        for route in ways:
            for copy in copies(block, part, route, own):
                copy.start()

    def arrived(block, part):
        for copy in copies(block, part, "twin"):
            copy.wait_recv()

    loads = [pltpu.make_async_copy(ins[i], held[i], own_in.at[i]) for i in range(count)]
    for load in loads:
        load.start()
    for part in range(PARTS):
        pl.when(z < LINE - 1)(functools.partial(forward, mine, part, "up", own=True))
        pl.when(z > 0)(functools.partial(forward, mine, part, "down", own=True))
        forward(mine, part, "one", "two", "twin", own=True)
    stores = [pltpu.make_async_copy(held[i], outs[i].at[mine], own_out.at[i]) for i in range(count)]
    for load, store in zip(loads, stores):
        load.wait()
        store.start()

    def line_step(step, part):
        @pl.when(z - step >= 0)
        def _():
            block = at.block(z - step, 0, 0)
            arrived(block, part)
            pl.when(z < LINE - 1)(functools.partial(forward, block, part, "up"))
            forward(block, part, "one", "two", "twin")

        @pl.when(z + step < LINE)
        def _():
            block = at.block(z + step, 0, 0)
            arrived(block, part)
            pl.when(z > 0)(functools.partial(forward, block, part, "down"))
            forward(block, part, "one", "two", "twin")

    def face_step(step, part, first, second):
        def take(block):
            arrived(block, part)
            if not second:
                forward(block, part, "two")
            forward(block, part, "twin")
        if step == 0:
            take(at.block(z, first, second))
        else:
            @pl.when(z - step >= 0)
            def _():
                take(at.block(z - step, first, second))

            @pl.when(z + step < LINE)
            def _():
                take(at.block(z + step, first, second))

    for step in range(LINE + 2):
        for part in range(PARTS):
            if 1 <= step < LINE:
                line_step(step, part)
            if 0 <= step - 1 < LINE:
                face_step(step - 1, part, 1, 0)
                face_step(step - 1, part, 0, 1)
            if 0 <= step - 2 < LINE:
                face_step(step - 2, part, 1, 1)
    for first in (0, 1):
        for second in (0, 1):
            for line in range(LINE):
                for part in range(PARTS):
                    arrived(at.block(line, first, second, 1), part)
    for store in stores:
        store.wait()

    def sent(block, part, *ways):
        for route in ways:
            for copy in copies(block, part, route):
                copy.wait_send()

    for line in range(LINE):
        for part in range(PARTS):
            block = at.block(line, 0, 0)
            pl.when((z >= line) & (z < LINE - 1))(functools.partial(sent, block, part, "up"))
            pl.when((z <= line) & (z > 0))(functools.partial(sent, block, part, "down"))
            sent(block, part, "one", "two", "twin")
            sent(at.block(line, 1, 0), part, "two", "twin")
            sent(at.block(line, 0, 1), part, "twin")
            sent(at.block(line, 1, 1), part, "twin")


def gather_blocks(collective_id, *arrays):
    count, devices = len(arrays), lax.axis_size("wide") * lax.axis_size("narrow")
    moved = sum(a.size * a.dtype.itemsize for a in arrays)
    return pl.pallas_call(
        functools.partial(gather_kernel, count),
        name=f"gather_blocks_{collective_id}",
        out_shape=tuple(jax.ShapeDtypeStruct((devices,) + a.shape, a.dtype) for a in arrays),
        in_specs=[pl.BlockSpec(memory_space=pl.ANY)] * count,
        out_specs=tuple(pl.BlockSpec(memory_space=pl.ANY) for _ in arrays),
        scratch_shapes=[pltpu.VMEM(a.shape, a.dtype) for a in arrays]
        + [
            pltpu.SemaphoreType.DMA((count, PARTS, 5, devices)),
            pltpu.SemaphoreType.DMA((count, PARTS, devices)),
            pltpu.SemaphoreType.DMA((count,)),
            pltpu.SemaphoreType.DMA((count,)),
        ],
        compiler_params=pltpu.CompilerParams(collective_id=collective_id, has_side_effects=True),
        cost_estimate=pl.CostEstimate(flops=0, transcendentals=0, bytes_accessed=2 * devices * moved),
    )(*arrays)


ORDER = (3, 0, 2, 1)


def scatter_kernel(count, *refs):
    ins, outs = refs[:count], refs[count:2 * count]
    rest = [refs[2 * count + k * count:2 * count + (k + 1) * count] for k in range(6)]
    acc, from_twin, from_two, from_one, from_below, from_above = rest
    load_sem, store_sem, send, recv = refs[8 * count:]
    at = Place()
    z = at.z
    up, down = at.device(z + 1, 0, 0), at.device(z - 1, 0, 0)
    one, two, twin = at.device(z, 1, 0), at.device(z, 0, 1), at.device(z, 0, 0, 1)
    greet([(one, None), (two, None), (twin, None), (up, z < LINE - 1), (down, z > 0)])
    units = [(line, part) for line in ORDER for part in range(PARTS)]
    corners = [(1, 1), (1, 0), (0, 1), (0, 0)]

    def slot(line, second, first):
        return second * 8 + first * 4 + line

    def load(i, part, line, second, first):
        here = slot(line, second, first)
        return pltpu.make_async_copy(part_of(ins[i].at[at.block(line, first, second)], part),
                                     part_of(acc[i].at[here], part), load_sem.at[i, part, here])

    def hop(i, part, source, target, lane, device):
        return remote(part_of(source, part), part_of(target, part), send.at[i, part, lane], recv.at[i, part, lane], device)

    def to_twin(i, part, line, second, first):
        here = slot(line, second, first)
        return hop(i, part, ins[i].at[at.block(line, first, second, 1)], from_twin[i].at[here], here, twin)

    def to_two(i, part, line, first):
        return hop(i, part, acc[i].at[slot(line, 1, first)], from_two[i].at[first * 4 + line], 16 + first * 4 + line, two)

    def to_one(i, part, line):
        return hop(i, part, acc[i].at[slot(line, 0, 1)], from_one[i].at[line], 24 + line, one)

    def rise(i, part, line):
        return hop(i, part, acc[i].at[line], from_below[i].at[line], 28 + line, up)

    def fall(i, part, line):
        return hop(i, part, acc[i].at[line], from_above[i].at[line], 32 + line, down)

    def begin(line, part):
        for second, first in corners:
            for i in range(count):
                to_twin(i, part, line, second, first).start()
                load(i, part, line, second, first).start()

    def gathered(line, part, second, first):
        for i in range(count):
            load(i, part, line, second, first).wait()
            to_twin(i, part, line, second, first).wait_recv()
            sources = [from_twin[i].at[slot(line, second, first)]]
            if not second:
                to_two(i, part, line, first).wait_recv()
                sources.append(from_two[i].at[first * 4 + line])
                if not first:
                    to_one(i, part, line).wait_recv()
                    sources.append(from_one[i].at[line])
            add_into(part_of(acc[i].at[slot(line, second, first)], part), *[part_of(r, part) for r in sources])
            if second:
                to_two(i, part, line, first).start()
            elif first:
                to_one(i, part, line).start()

    def line_hop(line, part, hops):
        @pl.when(z == hops)
        def _():
            for i in range(count):
                if 0 < hops <= line:
                    rise(i, part, line).wait_recv()
                    add_into(part_of(acc[i].at[line], part), part_of(from_below[i].at[line], part))
                if hops < line:
                    rise(i, part, line).start()

        @pl.when(z == LINE - 1 - hops)
        def _():
            for i in range(count):
                if 0 < hops <= LINE - 1 - line:
                    fall(i, part, line).wait_recv()
                    add_into(part_of(acc[i].at[line], part), part_of(from_above[i].at[line], part))
                if hops < LINE - 1 - line:
                    fall(i, part, line).start()

    begin(*units[0])
    begin(*units[1])
    for step in range(len(units) + 2 + LINE):
        if step + 2 < len(units):
            begin(*units[step + 2])
        if step < len(units):
            gathered(*units[step], 1, 1)
            gathered(*units[step], 1, 0)
        if 0 <= step - 1 < len(units):
            gathered(*units[step - 1], 0, 1)
        if 0 <= step - 2 < len(units):
            gathered(*units[step - 2], 0, 0)
        for hops in range(LINE):
            if 0 <= step - 2 - hops < len(units):
                line_hop(*units[step - 2 - hops], hops)
    stores = [pltpu.make_async_copy(acc[i].at[z], outs[i], store_sem.at[i]) for i in range(count)]
    for store in stores:
        store.start()
    for line, part in units:
        for i in range(count):
            for second, first in corners:
                to_twin(i, part, line, second, first).wait_send()
            to_two(i, part, line, 0).wait_send()
            to_two(i, part, line, 1).wait_send()
            to_one(i, part, line).wait_send()
            if line > 0:
                pl.when(z < line)(rise(i, part, line).wait_send)
            if line < LINE - 1:
                pl.when(z > line)(fall(i, part, line).wait_send)
    for store in stores:
        store.wait()


def scatter_blocks(collective_id, *arrays):
    count = len(arrays)

    def slots(n):
        return [pltpu.VMEM((n,) + a.shape[1:], a.dtype) for a in arrays]
    return pl.pallas_call(
        functools.partial(scatter_kernel, count),
        name=f"scatter_blocks_{collective_id}",
        out_shape=tuple(jax.ShapeDtypeStruct(a.shape[1:], a.dtype) for a in arrays),
        in_specs=[pl.BlockSpec(memory_space=pl.ANY)] * count,
        out_specs=tuple(pl.BlockSpec(memory_space=pl.ANY) for _ in arrays),
        scratch_shapes=slots(16) + slots(16) + slots(8) + slots(4) + slots(4) + slots(4)
        + [
            pltpu.SemaphoreType.DMA((count, PARTS, 16)),
            pltpu.SemaphoreType.DMA((count,)),
            pltpu.SemaphoreType.DMA((count, PARTS, 36)),
            pltpu.SemaphoreType.DMA((count, PARTS, 36)),
        ],
        compiler_params=pltpu.CompilerParams(
            collective_id=collective_id, has_side_effects=True, vmem_limit_bytes=60 << 20),
        cost_estimate=pl.CostEstimate(
            flops=0, transcendentals=0, bytes_accessed=sum(a.size * a.dtype.itemsize for a in arrays)),
    )(*arrays)


def sum_task(at, kind, rows, source, result, held, from_pair, from_below, from_above, load_sem, send, recv, delay, prepare=None):
    z, x = at.z, at.x
    pair = ((z * 2 + 1 - x), at.y * 2 + at.core)
    up, down = ((z + 1) * 2 + x, at.y * 2 + at.core), ((z - 1) * 2 + x, at.y * 2 + at.core)
    pair_first = kind == "pair"
    for _ in range(delay):
        yield

    def part(ref, line, face):
        return ref.at[line, face, rows]

    if pair_first:
        def load(line):
            return pltpu.make_async_copy(part(source, line, x), held.at[line], load_sem.at[line])

        def give(line):
            return remote(part(source, line, 1 - x), from_pair.at[line], send.at[0, line], recv.at[0, line], pair)
        for line in ORDER:
            give(line).start()
            load(line).start()
        yield
        yield
        for line in ORDER:
            load(line).wait()
            give(line).wait_recv()
            add_into(held.at[line], from_pair.at[line])
    else:
        def load(line):
            return pltpu.make_async_copy(source.at[line, :, rows], held.at[line], load_sem.at[line])
        for line in ORDER:
            load(line).start()
        for line in ORDER:
            load(line).wait()
        if prepare is not None:
            yield from prepare(held)

    def add(target, extra):
        if pair_first:
            add_into(target, extra)
        else:
            for face in (0, 1):
                add_into(target.at[face], extra.at[face])

    def rise(line):
        return remote(held.at[line], from_below.at[line], send.at[1, line], recv.at[1, line], up)

    def fall(line):
        return remote(held.at[line], from_above.at[line], send.at[2, line], recv.at[2, line], down)

    for line in range(LINE - 1, 0, -1):
        other = LINE - 1 - line

        @pl.when(z < line)
        def _():
            @pl.when(z > 0)
            def _():
                rise(line).wait_recv()
                add(held.at[line], from_below.at[line])
            rise(line).start()

        @pl.when(z > other)
        def _():
            @pl.when(z < LINE - 1)
            def _():
                fall(other).wait_recv()
                add(held.at[other], from_above.at[other])
            fall(other).start()
        yield

    @pl.when(z > 0)
    def _():
        rise(z).wait_recv()
        add(held.at[z], from_below.at[z])

    @pl.when(z < LINE - 1)
    def _():
        fall(z).wait_recv()
        add(held.at[z], from_above.at[z])

    if pair_first:
        def over(line):
            return remote(part(result, line, x), part(result, line, x), send.at[3, line], recv.at[3, line * 2 + x], pair)

        def other_over(line):
            return remote(part(result, line, 1 - x), part(result, line, 1 - x), send.at[3, line],
                          recv.at[3, line * 2 + 1 - x], pair)

        def climb(line):
            return remote(part(result, line, x), part(result, line, x), send.at[4, line], recv.at[3, line * 2 + x], up)

        def sink(line):
            return remote(part(result, line, x), part(result, line, x), send.at[5, line], recv.at[3, line * 2 + x], down)
        own = pltpu.make_async_copy(held.at[z], part(result, z, x), load_sem.at[4])
    else:
        mine = held.at[z]
        swap = remote(mine.at[1 - x], from_pair, send.at[0, 0], recv.at[0, 0], pair)
        swap.start()
        yield
        swap.wait_recv()
        add_into(mine.at[x], from_pair)
        own = pltpu.make_async_copy(mine.at[x], part(result, z, x), load_sem.at[4])

        def over_block(face):
            return remote(part(result, z, face), part(result, z, face), send.at[3, 0], recv.at[3, face], pair)

        def climb(line):
            return remote(result.at[line, :, rows], result.at[line, :, rows], send.at[4, line], recv.at[3, 4 + line], up)

        def sink(line):
            return remote(result.at[line, :, rows], result.at[line, :, rows], send.at[5, line], recv.at[3, 4 + line], down)
    own.start()
    own.wait()
    if pair_first:
        over(z).start()
    else:
        over_block(x).start()
        yield
        over_block(1 - x).wait_recv()

    @pl.when(z < LINE - 1)
    def _():
        climb(z).start()

    @pl.when(z > 0)
    def _():
        sink(z).start()
    yield
    for step in range(1, LINE):
        @pl.when(z - step >= 0)
        def _():
            climb(z - step).wait_recv()

            @pl.when(z < LINE - 1)
            def _():
                climb(z - step).start()
            if pair_first:
                over(z - step).start()

        @pl.when(z + step < LINE)
        def _():
            sink(z + step).wait_recv()

            @pl.when(z > 0)
            def _():
                sink(z + step).start()
            if pair_first:
                over(z + step).start()
        yield
    if pair_first:
        for line in range(LINE):
            other_over(line).wait_recv()
    for line in range(LINE):
        if pair_first:
            give(line).wait_send()
            over(line).wait_send()
        if line > 0:
            pl.when(z < line)(rise(line).wait_send)
        if line < LINE - 1:
            pl.when(z > line)(fall(line).wait_send)
        pl.when((z >= line) & (z < LINE - 1))(climb(line).wait_send)
        pl.when((z <= line) & (z > 0))(sink(line).wait_send)
    if not pair_first:
        swap.wait_send()
        over_block(x).wait_send()


def narrow_sum_task(at, source, result, mine, from_twin, from_peer, load_sem, send, recv):
    twin, peer = at.device(at.z, 0, 0, 1), at.across()

    def give(y):
        return remote(source.at[y * 2 + 1 - at.core], from_twin.at[y], send.at[y], recv.at[y], twin)

    def load(y):
        return pltpu.make_async_copy(source.at[y * 2 + at.core], mine.at[y], load_sem.at[y])
    order = (1 - at.y, at.y)
    for y in order:
        give(y).start()
        load(y).start()
    other, own = order
    over = remote(mine.at[other], from_peer, send.at[2], recv.at[2], peer)
    for y in order:
        load(y).wait()
        give(y).wait_recv()
        add_into(mine.at[y], from_twin.at[y])
        if y is other:
            over.start()
    yield
    over.wait_recv()
    add_into(mine.at[own], from_peer)
    store = pltpu.make_async_copy(mine.at[own], result, load_sem.at[2])
    store.start()
    yield
    store.wait()
    over.wait_send()
    for y in order:
        give(y).wait_send()


def narrow_sum_scratch(block, dtype):
    return [
        pltpu.VMEM((2,) + block, dtype),
        pltpu.VMEM((2,) + block, dtype),
        pltpu.VMEM(block, dtype),
        pltpu.SemaphoreType.DMA((3,)),
        pltpu.SemaphoreType.DMA((3,)),
        pltpu.SemaphoreType.DMA((3,)),
    ]


def run_tasks(tasks):
    while tasks:
        tasks = [task for task in tasks if next(task, tasks) is not tasks]


def narrow_sum_kernel(source, result, *scratch):
    at = Place()
    greet([(at.device(at.z, 0, 0, 1), None), (at.across(), None)])
    run_tasks([narrow_sum_task(at, source, result, *scratch)])


def narrow_sum(collective_id, parts):
    block = parts.shape[1:]
    return pl.pallas_call(
        narrow_sum_kernel,
        name=f"narrow_sum_{collective_id}",
        out_shape=jax.ShapeDtypeStruct(block, parts.dtype),
        in_specs=[pl.BlockSpec(memory_space=pl.ANY)],
        out_specs=pl.BlockSpec(memory_space=pl.ANY),
        scratch_shapes=narrow_sum_scratch(block, parts.dtype),
        compiler_params=pltpu.CompilerParams(collective_id=collective_id, has_side_effects=True),
    )(parts)


def narrow_gather_kernel(block, result, held, load_sem, send, recv):
    at = Place()
    twin, peer = at.device(at.z, 0, 0, 1), at.across()
    greet([(twin, None), (peer, None)])
    here, there = at.y * 2 + at.core, (1 - at.y) * 2 + at.core
    load = pltpu.make_async_copy(block, held, load_sem.at[0])
    load.start()
    over = remote(block, result.at[here], send.at[0], recv.at[here], peer)
    beside = remote(block, result.at[here], send.at[1], recv.at[here], twin)
    over.start()
    beside.start()
    load.wait()
    store = pltpu.make_async_copy(held, result.at[here], load_sem.at[1])
    store.start()
    passed = remote(result.at[there], result.at[there], send.at[2], recv.at[there], twin)
    passed.wait_recv()
    passed.start()
    for y in (0, 1):
        remote(block, result.at[y * 2 + 1 - at.core], send.at[1], recv.at[y * 2 + 1 - at.core], twin).wait_recv()
    for copy in (over, beside, passed):
        copy.wait_send()
    store.wait()


def narrow_gather(collective_id, block):
    return pl.pallas_call(
        narrow_gather_kernel,
        name=f"narrow_gather_{collective_id}",
        out_shape=jax.ShapeDtypeStruct((4,) + block.shape, block.dtype),
        in_specs=[pl.BlockSpec(memory_space=pl.ANY)],
        out_specs=pl.BlockSpec(memory_space=pl.ANY),
        scratch_shapes=[
            pltpu.VMEM(block.shape, block.dtype),
            pltpu.SemaphoreType.DMA((2,)),
            pltpu.SemaphoreType.DMA((3,)),
            pltpu.SemaphoreType.DMA((4,)),
        ],
        compiler_params=pltpu.CompilerParams(collective_id=collective_id, has_side_effects=True),
    )(block)


def narrow_total_kernel(values, result, others, send, recv):
    at = Place()
    places = [at.device(at.z, 0, 0, 1), at.across(), at.across(1)]
    greet([(place, None) for place in places])
    copies = [remote(values, others.at[i], send.at[i], recv.at[i], place) for i, place in enumerate(places)]
    for copy in copies:
        copy.start()
    for copy in copies:
        copy.wait()
    result[...] = (values[...] + others[0]) + (others[1] + others[2])


def narrow_total(collective_id, values):
    return pl.pallas_call(
        narrow_total_kernel,
        name=f"narrow_total_{collective_id}",
        out_shape=jax.ShapeDtypeStruct(values.shape, values.dtype),
        in_specs=[pl.BlockSpec(memory_space=pltpu.VMEM)],
        out_specs=pl.BlockSpec(memory_space=pltpu.VMEM),
        scratch_shapes=[
            pltpu.VMEM((3,) + values.shape, values.dtype),
            pltpu.SemaphoreType.DMA((3,)),
            pltpu.SemaphoreType.DMA((3,)),
        ],
        compiler_params=pltpu.CompilerParams(collective_id=collective_id, has_side_effects=True),
    )(values)


def final_sums_kernel(plan, count, *refs):
    ins, outs, rest = refs[:count], refs[count:2 * count], list(refs[2 * count:])
    at = Place()
    pair = (at.z * 2 + 1 - at.x, at.y * 2 + at.core)
    up, down = ((at.z + 1) * 2 + at.x, at.y * 2 + at.core), ((at.z - 1) * 2 + at.x, at.y * 2 + at.core)
    twin, peer = at.device(at.z, 0, 0, 1), at.across()
    greet([(pair, None), (twin, None), (peer, None), (up, at.z < LINE - 1), (down, at.z > 0)])
    narrow_scratch, rest = rest[-6:], rest[:-6]
    load_sem, send, recv, others, other_send, other_recv = rest[-6:]

    def over_narrow(held):
        beside = remote(ins[count - 2], others.at[0], other_send.at[0], other_recv.at[0], twin)
        beside.start()
        yield
        beside.wait_recv()
        for line in range(LINE):
            for face in (0, 1):
                add_into(held.at[line, face], others.at[0, line, face])
        across = remote(held, others.at[1], other_send.at[1], other_recv.at[1], peer)
        across.start()
        yield
        across.wait()
        beside.wait_send()
        for line in range(LINE):
            for face in (0, 1):
                add_into(held.at[line, face], others.at[1, line, face])
    tasks = [narrow_sum_task(at, ins[-1], outs[-1], *narrow_scratch)]
    for number, (which, begin, rows, kind, delay) in enumerate(plan):
        held, from_pair, from_below, from_above = rest[4 * number:4 * number + 4]
        tasks.append(sum_task(at, kind, pl.ds(begin, rows), ins[which], outs[which], held, from_pair, from_below,
                              from_above, load_sem.at[number], send.at[number], recv.at[number], delay,
                              over_narrow if which == count - 2 else None))
    run_tasks(tasks)


def final_sums(collective_id, plan, *arrays):
    count, steps = len(arrays), len(plan)
    scratch = []
    for which, _, rows, kind, _ in plan:
        columns, dtype = arrays[which].shape[3], arrays[which].dtype
        block = (() if kind == "pair" else (2,)) + (rows, columns)
        scratch += [
            pltpu.VMEM((LINE,) + block, dtype),
            pltpu.VMEM(((LINE,) if kind == "pair" else ()) + (rows, columns), dtype),
            pltpu.VMEM((LINE,) + block, dtype),
            pltpu.VMEM((LINE,) + block, dtype),
        ]
    small, parts = arrays[-2:]
    moved = sum(a.size * a.dtype.itemsize for a in arrays)
    return pl.pallas_call(
        functools.partial(final_sums_kernel, plan, count),
        name=f"final_sums_{collective_id}",
        out_shape=tuple(jax.ShapeDtypeStruct(a.shape, a.dtype) for a in arrays[:-1])
        + (jax.ShapeDtypeStruct(parts.shape[1:], parts.dtype),),
        in_specs=[pl.BlockSpec(memory_space=pl.ANY)] * count,
        out_specs=tuple(pl.BlockSpec(memory_space=pl.ANY) for _ in arrays),
        scratch_shapes=scratch + [
            pltpu.SemaphoreType.DMA((steps, 5)),
            pltpu.SemaphoreType.DMA((steps, 6, 4)),
            pltpu.SemaphoreType.DMA((steps, 4, 8)),
            pltpu.VMEM((2,) + small.shape, small.dtype),
            pltpu.SemaphoreType.DMA((2,)),
            pltpu.SemaphoreType.DMA((2,)),
        ] + narrow_sum_scratch(parts.shape[1:], parts.dtype),
        compiler_params=pltpu.CompilerParams(
            collective_id=collective_id, has_side_effects=True, vmem_limit_bytes=48 << 20),
        cost_estimate=pl.CostEstimate(flops=0, transcendentals=0, bytes_accessed=2 * moved),
    )(*arrays)


def own_exchange():
    return lax.axis_size("wide") == 8 and lax.axis_size("narrow") == 4


def gather_all(*arrays):
    if own_exchange():
        return gather_blocks(1, *arrays)
    return tuple(lax.all_gather(a, BOTH, axis=0) for a in arrays)


def scatter_all(*arrays):
    if own_exchange():
        return scatter_blocks(2, *arrays)
    return tuple(lax.psum_scatter(a, BOTH, scatter_dimension=0) for a in arrays)


FINAL_PLAN = (
    (4, 0, 72, "line", 0),
    (0, 0, 128, "pair", 0),
    (3, 0, 64, "line", 0),
    (0, 128, 128, "pair", 1),
    (1, 0, 128, "pair", 2),
    (1, 128, 128, "pair", 3),
    (2, 0, 128, "pair", 4),
    (2, 128, 128, "pair", 5),
)


def total_weights(weights, gains, everywhere, parts):
    if not own_exchange():
        totals = tuple(a.astype(jnp.float32) for a in lax.psum(tuple(a.astype(jnp.bfloat16) for a in weights), "wide"))
        own = lax.psum_scatter(parts, "narrow", scatter_dimension=0, tiled=True)
        return totals, lax.psum(gains, "wide"), lax.psum(everywhere, BOTH), own
    gain_rows = jnp.concatenate([a.reshape(-1, 128) for a in gains], axis=0)
    mine = lax.axis_index("narrow")
    gain_slots = lax.dynamic_update_slice_in_dim(jnp.zeros((4,) + gain_rows.shape, jnp.float32), gain_rows[None], mine, 0)
    pieces = [a.reshape(-1, 128) for a in everywhere] + [gain_slots.reshape(-1, 128)]
    small = jnp.concatenate(pieces, axis=0)
    arrays = [a.astype(jnp.bfloat16).reshape(LINE, 2, a.shape[0] // 8, a.shape[1]) for a in weights]
    results = final_sums(
        3, FINAL_PLAN, *arrays, small.reshape(LINE, 2, small.shape[0] // 8, 128), parts.reshape(4, -1, parts.shape[1])
    )
    totals = tuple(r.reshape(a.shape).astype(jnp.float32) for r, a in zip(results, weights))
    small_total = results[-2].reshape(small.shape)
    summed, begin = [], 0
    for array, piece in zip(everywhere, pieces):
        summed.append(small_total[begin:begin + piece.shape[0]].reshape(array.shape))
        begin += piece.shape[0]
    own_gains = lax.dynamic_slice_in_dim(small_total[begin:].reshape(gain_slots.shape), mine, 1, 0).reshape(len(gains), -1)
    return totals, tuple(own_gains[i].reshape(g.shape) for i, g in enumerate(gains)), tuple(summed), results[-1]


def narrow_sums(collective_id, values):
    if not own_exchange():
        return lax.psum(values, "narrow")
    total = narrow_total(collective_id, jnp.stack(values).reshape(-1, 128)).reshape(len(values), -1)
    return tuple(total[i] for i in range(len(values)))


def narrow_deal(collective_id, parts):
    if not own_exchange():
        return lax.psum_scatter(parts, "narrow", scatter_dimension=0, tiled=True)
    return narrow_sum(collective_id, parts.reshape(4, -1, parts.shape[1]))


def narrow_all(collective_id, block):
    if not own_exchange():
        return lax.all_gather(block, "narrow", axis=0, tiled=True)
    return narrow_gather(collective_id, block).reshape(-1, block.shape[1])


def experts_plain(rows_all, grads_all, places_here, probs_here, gate_weight, up_weight, down_weight, capacity):
    block_count, own_rows, model_width = rows_all.shape
    experts_here = gate_weight.shape[0]
    highest_precision = lax.Precision.HIGHEST
    pick = places_here[:, :, None, :] == jnp.arange(capacity, dtype=jnp.float32)[None, None, :, None]
    pick_low = pick.astype(jnp.bfloat16)
    slot_gate = jnp.sum(jnp.where(pick, probs_here[:, :, None, :], 0.0), axis=-1)
    slot_gate = slot_gate.transpose(1, 0, 2).reshape(experts_here, block_count * capacity, 1)

    def spread(rows):
        out = jnp.einsum("best,btd->ebsd", pick_low, rows, preferred_element_type=jnp.float32)
        return out.astype(jnp.bfloat16).reshape(experts_here, block_count * capacity, model_width)

    def collect(slots):
        out = jnp.einsum(
            "best,ebsd->btd",
            pick_low,
            slots.reshape(experts_here, block_count, capacity, model_width),
            preferred_element_type=jnp.float32,
        )
        return out.astype(jnp.bfloat16)

    slot_rows = spread(rows_all)
    slot_grads = spread(grads_all)
    gate_pre = jnp.einsum("erd,edf->erf", slot_rows, gate_weight, preferred_element_type=jnp.float32)
    up_pre = jnp.einsum("erd,edf->erf", slot_rows, up_weight, preferred_element_type=jnp.float32)
    activated, unit_back = jax.vjp(gated_unit, gate_pre, up_pre)
    gated_act = (activated * slot_gate).astype(jnp.bfloat16)
    raw_act_grad = jnp.einsum("erd,efd->erf", slot_grads, down_weight, preferred_element_type=jnp.float32)
    slot_gate_grads = jnp.sum(activated * raw_act_grad, axis=-1)
    gate_grad_full, up_grad_full = unit_back(raw_act_grad * slot_gate)
    gate_grad_low = gate_grad_full.astype(jnp.bfloat16)
    up_grad_low = up_grad_full.astype(jnp.bfloat16)
    gate_grad_parts = jnp.einsum(
        "best,ebs->bet",
        pick.astype(jnp.float32),
        slot_gate_grads.reshape(experts_here, block_count, capacity),
        precision=highest_precision,
    )
    back_slots = jnp.einsum(
        "erf,edf->erd", gate_grad_low, gate_weight, preferred_element_type=jnp.float32
    ) + jnp.einsum("erf,edf->erd", up_grad_low, up_weight, preferred_element_type=jnp.float32)
    out_slots = jnp.einsum("erf,efd->erd", gated_act, down_weight, preferred_element_type=jnp.float32)
    return (
        collect(out_slots.astype(jnp.bfloat16)),
        collect(back_slots.astype(jnp.bfloat16)),
        gate_grad_parts,
        jnp.einsum("erd,erf->edf", slot_rows, gate_grad_low, preferred_element_type=jnp.float32),
        jnp.einsum("erd,erf->edf", slot_rows, up_grad_low, preferred_element_type=jnp.float32),
        jnp.einsum("erf,erd->efd", gated_act, slot_grads, preferred_element_type=jnp.float32),
    )


STEP_BLOCKS = 4
COLUMNS = 512


def dot(left, right, left_dim=1, right_dim=0):
    return lax.dot_general(
        left, right, (((left_dim,), (right_dim,)), ((), ())), preferred_element_type=jnp.float32
    )


def experts_kernel(
    capacity, rows, grads, places, gates, gate_w, up_w, down_w,
    out, back, gate_grads, gate_dw, up_dw, down_dw, row_slots, grad_slots,
):
    experts, width = gate_w.shape[0], gate_w.shape[1]
    tokens = rows.shape[1]
    slot_ids = lax.broadcasted_iota(jnp.int32, (capacity, tokens), 0).astype(jnp.float32)

    @pl.when(pl.program_id(0) == 0)
    def _():
        for target in (gate_dw, up_dw, down_dw):
            @pl.loop(0, experts)
            def _(e):
                target[e] = jnp.zeros(target.shape[1:], jnp.float32)

    def chunks(body):
        @pl.loop(0, width // COLUMNS)
        def _(i):
            body(pl.ds(pl.multiple_of(i * COLUMNS, COLUMNS), COLUMNS))

    def pick_of(block, expert):
        return places[block, pl.ds(expert, 1), :] == slot_ids

    def picks(block):
        return jnp.concatenate(
            [pick_of(block, e).astype(jnp.float32) for e in range(experts)], axis=0
        ).astype(jnp.bfloat16)

    for block in range(STEP_BLOCKS):
        pick = picks(block)
        part = pl.ds(block * capacity, capacity)

        def spread(columns):
            for source, target in ((rows, row_slots), (grads, grad_slots)):
                slots = dot(pick, source[block, :, columns]).astype(jnp.bfloat16)
                for e in range(experts):
                    target[e, part, columns] = slots[e * capacity:(e + 1) * capacity]
        chunks(spread)

    @pl.loop(0, experts)
    def _(e):
        gate_pre, up_pre = dot(row_slots[e], gate_w[e]), dot(row_slots[e], up_w[e])
        raw = dot(grad_slots[e], down_w[e], 1, 1)
        slot_gate = jnp.concatenate([
            jnp.sum(jnp.where(pick_of(block, e), gates[block, pl.ds(e, 1), :], 0.0), axis=1, keepdims=True)
            for block in range(STEP_BLOCKS)
        ], axis=0)
        sigma = 1.0 / (1.0 + jnp.exp(-gate_pre))
        silu = gate_pre * sigma
        act = silu * up_pre
        slot_sum = jnp.sum(act * raw, axis=1, keepdims=True)
        for block in range(STEP_BLOCKS):
            gate_grads[block, pl.ds(e, 1), :] = jnp.sum(
                jnp.where(pick_of(block, e), slot_sum[block * capacity:(block + 1) * capacity], 0.0),
                axis=0, keepdims=True,
            )
        gated = (act * slot_gate).astype(jnp.bfloat16)
        act_grad = raw * slot_gate
        gate_low = (act_grad * up_pre * sigma * (1.0 + gate_pre * (1.0 - sigma))).astype(jnp.bfloat16)
        up_low = (act_grad * silu).astype(jnp.bfloat16)

        def columns_of(columns):
            down_dw[e, :, columns] += dot(gated, grad_slots[e, :, columns], 0, 0)
            grad_slots[e, :, columns] = dot(gated, down_w[e, :, columns]).astype(jnp.bfloat16)
            turned = row_slots[e, :, columns].T
            gate_dw[e, columns, :] += dot(turned, gate_low)
            up_dw[e, columns, :] += dot(turned, up_low)
            row_slots[e, :, columns] = (
                dot(gate_low, gate_w[e, columns, :], 1, 1) + dot(up_low, up_w[e, columns, :], 1, 1)
            ).astype(jnp.bfloat16)
        chunks(columns_of)

    for block in range(STEP_BLOCKS):
        pick = picks(block)
        part = pl.ds(block * capacity, capacity)

        def collect(columns):
            for source, target in ((row_slots, back), (grad_slots, out)):
                slots = jnp.concatenate([source[e, part, columns] for e in range(experts)], axis=0)
                target[block, :, columns] = dot(pick, slots, 0, 0).astype(jnp.bfloat16)
        chunks(collect)


def experts_fused(rows_all, grads_all, places_here, probs_here, gate_weight, up_weight, down_weight, capacity):
    block_count, own_rows, width = rows_all.shape
    experts, _, hidden = gate_weight.shape
    step_rows = STEP_BLOCKS * capacity

    def stepped(*shape):
        return pl.BlockSpec((STEP_BLOCKS,) + shape, lambda i: (i,) + (0,) * len(shape))

    def whole(array):
        return pl.BlockSpec(array.shape, lambda i: (0,) * array.ndim, pipeline_mode=pl.Buffered(1))
    weights = (gate_weight, up_weight, down_weight)
    flops = 2 * block_count * experts * (9 * capacity * width * hidden + 4 * capacity * own_rows * width)
    return pl.pallas_call(
        functools.partial(experts_kernel, capacity),
        name="experts",
        grid=(block_count // STEP_BLOCKS,),
        out_shape=(
            jax.ShapeDtypeStruct(rows_all.shape, jnp.bfloat16),
            jax.ShapeDtypeStruct(rows_all.shape, jnp.bfloat16),
            jax.ShapeDtypeStruct((block_count, experts, own_rows), jnp.float32),
        ) + tuple(jax.ShapeDtypeStruct(w.shape, jnp.float32) for w in weights),
        in_specs=[
            stepped(own_rows, width), stepped(own_rows, width), stepped(experts, own_rows), stepped(experts, own_rows),
        ] + [whole(w) for w in weights],
        out_specs=(stepped(own_rows, width), stepped(own_rows, width), stepped(experts, own_rows))
        + tuple(whole(w) for w in weights),
        scratch_shapes=[
            pltpu.VMEM((experts, step_rows, width), jnp.bfloat16),
            pltpu.VMEM((experts, step_rows, width), jnp.bfloat16),
        ],
        compiler_params=pltpu.CompilerParams(
            dimension_semantics=("arbitrary",), vmem_limit_bytes=67_000_000),
        cost_estimate=pl.CostEstimate(
            flops=flops, transcendentals=0,
            bytes_accessed=4 * 2 * rows_all.size + sum(6 * w.size for w in weights)),
    )(rows_all, grads_all, places_here, probs_here, *weights)


def local(
    block_input,
    attn_gain,
    query_weight,
    key_weight,
    value_weight,
    query_gain,
    key_gain,
    out_weight,
    moe_gain,
    router_weight,
    gate_weight,
    up_weight,
    down_weight,
    segment_ids,
    expert_ids,
    out_cotangent,
):
    group_rows, model_width = block_input.shape
    own_rows = out_cotangent.shape[0]
    local_width = query_weight.shape[1]
    head_size = HEAD_DIM
    local_heads = local_width // head_size
    wide_size = lax.axis_size("wide")
    experts_all = router_weight.shape[1]
    experts_here = gate_weight.shape[0]
    choose_count = expert_ids.shape[1]
    capacity = 3 * own_rows * choose_count // (2 * experts_all)
    row_begin = lax.axis_index("narrow") * own_rows
    blocks = group_rows // QBLK
    highest_precision = lax.Precision.HIGHEST
    block_count = wide_size * lax.axis_size("narrow")
    chosen = (expert_ids[:, :, None] == jnp.arange(experts_all)[None, None, :]).any(axis=1)
    token_order = jnp.arange(own_rows)
    earlier = jnp.dot(
        (token_order[:, None] > token_order[None, :]).astype(jnp.bfloat16),
        chosen.astype(jnp.bfloat16),
        preferred_element_type=jnp.float32,
    )
    grads_all = lax.all_gather(out_cotangent, BOTH, axis=0)
    inputs_all = block_input.astype(jnp.float32)
    normed_one = rms_scale(inputs_all, attn_gain.astype(jnp.float32)).astype(jnp.bfloat16)
    joined_weight = jnp.concatenate([query_weight, key_weight, value_weight], axis=1)
    projected = jnp.dot(normed_one, joined_weight, preferred_element_type=jnp.float32)
    query_proj = projected[:, :local_width]
    key_proj = projected[:, local_width : 2 * local_width]
    value_proj = projected[:, 2 * local_width :]
    rope_cos, rope_sin = rope_tables(group_rows, head_size)
    query_total, key_total = narrow_sums(
        4, (jnp.sum(query_proj * query_proj, axis=1), jnp.sum(key_proj * key_proj, axis=1))
    )
    query_inverse = lax.rsqrt(query_total / model_width + norm_epsilon)[:, None]
    key_inverse = lax.rsqrt(key_total / model_width + norm_epsilon)[:, None]
    query_scale = query_gain.astype(jnp.float32)
    key_scale = key_gain.astype(jnp.float32)
    query_normed = query_proj * query_inverse * query_scale
    key_normed = key_proj * key_inverse * key_scale

    def turn_both(query_in, key_in):
        return (
            rotate(query_in, rope_cos, rope_sin, head_size) * head_size ** (-0.5),
            rotate(key_in, rope_cos, rope_sin, head_size),
        )

    (turned_query, turned_key), turn_back = jax.vjp(turn_both, query_normed, key_normed)
    query_heads = turned_query.astype(jnp.bfloat16).reshape(group_rows, local_heads, head_size)
    key_heads = turned_key.astype(jnp.bfloat16).reshape(group_rows, local_heads, head_size)
    value_heads = value_proj.astype(jnp.bfloat16).reshape(group_rows, local_heads, head_size)
    positions = jnp.arange(group_rows)

    def block_scores(block_index):
        block_begin = block_index * QBLK
        query_block = lax.dynamic_slice_in_dim(query_heads, block_begin, QBLK, 0)
        query_segments = lax.dynamic_slice_in_dim(segment_ids, block_begin, QBLK, 0)
        query_places = block_begin + jnp.arange(QBLK)
        allowed = (query_segments[:, None] == segment_ids[None, :]) & (
            query_places[:, None] >= positions[None, :]
        )
        scores = jnp.einsum(
            "qhd,khd->hqk", query_block, key_heads, preferred_element_type=jnp.float32
        )
        return (query_block, jnp.where(allowed[None], scores, masked_score))

    def attend(block_index):
        query_block, scores = block_scores(block_index)
        highest = jnp.max(scores, axis=-1, keepdims=True)
        weights = jnp.exp(scores - highest)
        totals = jnp.sum(weights, axis=-1, keepdims=True)
        probs_low = (weights / totals).astype(jnp.bfloat16)
        mixed_rows = jnp.einsum(
            "hqk,khd->qhd", probs_low, value_heads, preferred_element_type=jnp.float32
        )
        return (mixed_rows, highest + jnp.log(totals))

    mixed_blocks, log_totals = lax.map(attend, jnp.arange(blocks))
    heads_out = mixed_blocks.reshape(group_rows, local_width).astype(jnp.bfloat16)
    attn_own = narrow_deal(
        6, jnp.dot(heads_out, out_weight, preferred_element_type=jnp.float32).astype(jnp.bfloat16)
    ).astype(jnp.float32)
    input_own = lax.dynamic_slice_in_dim(inputs_all, row_begin, own_rows, 0)
    hidden = input_own + attn_own
    normed_two_full, norm_two_back = jax.vjp(rms_scale, hidden, moe_gain.astype(jnp.float32))
    normed_two = normed_two_full.astype(jnp.bfloat16)
    logits = jnp.dot(normed_two, router_weight, preferred_element_type=jnp.float32)
    route_probs = jax.nn.softmax(logits, axis=-1)
    rows_all, routes_all = gather_all(
        normed_two, jnp.concatenate([route_probs.T, jnp.where(chosen, earlier, -1.0).T], axis=0)
    )
    expert_begin = lax.axis_index("wide") * experts_here
    probs_here = lax.dynamic_slice_in_dim(routes_all, expert_begin, experts_here, 1)
    places_here = lax.dynamic_slice_in_dim(routes_all, experts_all + expert_begin, experts_here, 1)
    experts = experts_fused if own_exchange() and capacity % 16 == 0 else experts_plain
    out_parts, back_parts, gate_grad_parts, gate_weight_grad, up_weight_grad, down_weight_grad = experts(
        rows_all, grads_all, places_here, probs_here, gate_weight, up_weight, down_weight, capacity
    )
    gate_grad_wide = lax.dynamic_update_slice_in_dim(
        jnp.zeros((block_count, experts_all, own_rows), jnp.float32), gate_grad_parts, expert_begin, 1
    )
    rows_back, prob_grads, moe_out = scatter_all(
        back_parts, gate_grad_wide, out_parts
    )
    rows_back, prob_grads, moe_out = rows_back.astype(jnp.float32), prob_grads.T, moe_out.astype(jnp.float32)
    block_output = (hidden + moe_out).astype(jnp.bfloat16)
    logit_grads = route_probs * (
        prob_grads - jnp.sum(route_probs * prob_grads, axis=-1, keepdims=True)
    )
    router_part = lax.dot_general(
        normed_two.astype(jnp.float32),
        logit_grads,
        (((0,), (0,)), ((), ())),
        precision=highest_precision,
    )
    router_back = lax.dot_general(
        logit_grads,
        router_weight.astype(jnp.float32),
        (((1,), (1,)), ((), ())),
        precision=highest_precision,
    )
    normed_two_grad = rows_back + router_back
    cotangent_full = out_cotangent.astype(jnp.float32)
    hidden_path, moe_gain_part = norm_two_back(normed_two_grad)
    hidden_grad = cotangent_full + hidden_path
    hidden_grad_low = hidden_grad.astype(jnp.bfloat16)
    gathered_piece = narrow_all(7, hidden_grad_low)
    heads_grad_acc = contract_last(gathered_piece, out_weight)
    out_weight_acc = contract_rows(heads_out, gathered_piece)
    heads_grad_low = heads_grad_acc.astype(jnp.bfloat16).reshape(group_rows, local_heads, head_size)

    def back_block(running, items):
        key_acc, value_acc = running
        block_index, log_total = items
        query_block, scores = block_scores(block_index)
        probs = jnp.exp(scores - log_total)
        probs_low = probs.astype(jnp.bfloat16)
        grad_block = lax.dynamic_slice_in_dim(heads_grad_low, block_index * QBLK, QBLK, 0)
        weight_grads = jnp.einsum(
            "qhd,khd->hqk", grad_block, value_heads, preferred_element_type=jnp.float32
        )
        row_dots = jnp.sum(probs * weight_grads, axis=-1, keepdims=True)
        score_grads = (probs * (weight_grads - row_dots)).astype(jnp.bfloat16)
        query_grad_block = jnp.einsum(
            "hqk,khd->qhd", score_grads, key_heads, preferred_element_type=jnp.float32
        )
        key_acc = key_acc + jnp.einsum(
            "hqk,qhd->khd", score_grads, query_block, preferred_element_type=jnp.float32
        )
        value_acc = value_acc + jnp.einsum(
            "hqk,qhd->khd", probs_low, grad_block, preferred_element_type=jnp.float32
        )
        return ((key_acc, value_acc), query_grad_block)

    zero_heads = jnp.zeros((group_rows, local_heads, head_size), jnp.float32)
    (key_grad, value_grad), query_grads = lax.scan(
        back_block, (zero_heads, zero_heads), (jnp.arange(blocks), log_totals)
    )
    query_normed_grad, key_normed_grad = turn_back(
        (query_grads.reshape(group_rows, local_width), key_grad.reshape(group_rows, local_width))
    )
    query_gain_part = jnp.sum(query_normed_grad * query_proj * query_inverse, axis=0)
    key_gain_part = jnp.sum(key_normed_grad * key_proj * key_inverse, axis=0)
    query_gained = query_normed_grad * query_scale
    key_gained = key_normed_grad * key_scale
    query_dot, key_dot = narrow_sums(
        5, (jnp.sum(query_proj * query_gained, axis=1), jnp.sum(key_proj * key_gained, axis=1))
    )
    query_proj_grad = (
        query_inverse * query_gained
        - query_proj * query_inverse**3 * (query_dot / model_width)[:, None]
    )
    key_proj_grad = (
        key_inverse * key_gained - key_proj * key_inverse**3 * (key_dot / model_width)[:, None]
    )
    proj_grad_low = jnp.concatenate(
        [query_proj_grad, key_proj_grad, value_grad.reshape(group_rows, local_width)], axis=1
    ).astype(jnp.bfloat16)
    weight_parts = tuple(
        contract_rows(normed_one, proj_grad_low[:, i * local_width : (i + 1) * local_width]) for i in range(3)
    ) + (out_weight_acc,)
    normed_one_part = contract_last(proj_grad_low, joined_weight)
    scaled_inputs = rms_scale(inputs_all, 1.0)
    attn_gain_part = jnp.sum(normed_one_part * scaled_inputs, axis=0)
    totals, gain_totals, summed, normed_one_own = total_weights(
        weight_parts,
        (query_gain_part, key_gain_part),
        (router_part, attn_gain_part, moe_gain_part),
        normed_one_part.astype(jnp.bfloat16),
    )
    query_weight_grad, key_weight_grad, value_weight_grad, out_weight_grad = totals
    query_gain_grad, key_gain_grad = gain_totals
    router_weight_grad, attn_gain_grad, moe_gain_grad = summed
    _, norm_one_back = jax.vjp(lambda v: rms_scale(v, attn_gain.astype(jnp.float32)), input_own)
    (input_path,) = norm_one_back(normed_one_own.astype(jnp.float32))
    input_grad = (hidden_grad + input_path).astype(jnp.bfloat16)
    return (
        block_output,
        input_grad,
        attn_gain_grad,
        query_weight_grad,
        key_weight_grad,
        value_weight_grad,
        query_gain_grad,
        key_gain_grad,
        out_weight_grad,
        moe_gain_grad,
        router_weight_grad,
        gate_weight_grad,
        up_weight_grad,
        down_weight_grad,
    )


def solution(mesh):
    in_specs = (
        P("wide", None),
        P(),
        P(None, "narrow"),
        P(None, "narrow"),
        P(None, "narrow"),
        P("narrow"),
        P("narrow"),
        P("narrow", None),
        P(),
        P(),
        P("wide", None, "narrow"),
        P("wide", None, "narrow"),
        P("wide", "narrow", None),
        P("wide"),
        P(("wide", "narrow"), None),
        P(("wide", "narrow"), None),
    )
    out_specs = (
        P(("wide", "narrow"), None),
        P(("wide", "narrow"), None),
        P(),
        P(None, "narrow"),
        P(None, "narrow"),
        P(None, "narrow"),
        P("narrow"),
        P("narrow"),
        P("narrow", None),
        P(),
        P(),
        P("wide", None, "narrow"),
        P("wide", None, "narrow"),
        P("wide", "narrow", None),
    )
    return jax.shard_map(local, mesh=mesh, in_specs=in_specs, out_specs=out_specs, check_vma=False)
```

```python
import functools

import jax
import jax.numpy as jnp
from jax import lax
from jax.experimental import pallas as pl
from jax.experimental.pallas import tpu as pltpu
from jax.sharding import PartitionSpec as P

HEAD_DIM = 128
QBLK = 512


norm_epsilon = 1e-05
rope_base = 10000.0
masked_score = -1e30


def rms_scale(values, gain):
    inverse = lax.rsqrt(jnp.mean(values * values, axis=-1, keepdims=True) + norm_epsilon)
    return values * inverse * gain


def rope_tables(length, head_size):
    half_size = head_size // 2
    exponent = jnp.arange(half_size, dtype=jnp.float32) * (2.0 / head_size)
    angle = jnp.arange(length, dtype=jnp.float32)[:, None] * (rope_base ** (-exponent))[None, :]
    return (jnp.cos(angle), jnp.sin(angle))


def rotate(normed, rope_cos, rope_sin, head_size):
    tokens_here = normed.shape[0]
    by_head = normed.reshape(tokens_here, -1, head_size)
    half_size = head_size // 2
    first_half = by_head[..., :half_size]
    second_half = by_head[..., half_size:]
    cos_rows = rope_cos[:, None, :]
    sin_rows = rope_sin[:, None, :]
    turned = jnp.concatenate(
        [
            first_half * cos_rows - second_half * sin_rows,
            second_half * cos_rows + first_half * sin_rows,
        ],
        axis=-1,
    )
    return turned.reshape(tokens_here, -1)


def gated_unit(gate_pre, up_pre):
    return jax.nn.silu(gate_pre) * up_pre


def contract_rows(left, right):
    return lax.dot_general(
        left, right, (((0,), (0,)), ((), ())), preferred_element_type=jnp.float32
    )


def contract_last(left, right):
    return lax.dot_general(
        left, right, (((1,), (1,)), ((), ())), preferred_element_type=jnp.float32
    )


BOTH = ("wide", "narrow")


MESH = pl.DeviceIdType.MESH
LINE = 4
ADD_ROWS = 16


def flip(bit, on):
    return bit + on * (1 - 2 * bit)


class Place:
    def __init__(self):
        wide, narrow = lax.axis_index("wide"), lax.axis_index("narrow")
        self.z, self.x = wide // 2, lax.rem(wide, 2)
        self.y, self.core = narrow // 2, lax.rem(narrow, 2)

    def device(self, z, first, second, other_core=0):
        core = flip(self.core, other_core)
        x = flip(self.x, first * (1 - core) + second * core)
        y = flip(self.y, first * core + second * (1 - core))
        return (z * 2 + x, y * 2 + core)

    def across(self, other_core=0):
        return (self.z * 2 + self.x, (1 - self.y) * 2 + flip(self.core, other_core))

    def block(self, z, first, second, other_core=0):
        wide, narrow = self.device(z, first, second, other_core)
        return wide * 4 + narrow


    def group(self, turn):
        return (flip(self.z // 2, turn // 4) * 4 + flip(lax.rem(self.z, 2), lax.rem(turn // 2, 2)) * 2
                + flip(self.x, lax.rem(turn, 2)))

    def stored(self, line, first, second, other_core=0):
        core = flip(self.core, other_core)
        turn = (flip(self.z // 2, line // 2) * 4 + flip(lax.rem(self.z, 2), line % 2) * 2
                + first * (1 - core) + second * core)
        return turn * 4 + self.device(line, first, second, other_core)[1]


def greet(devices_and_conditions):
    barrier = pltpu.get_barrier_semaphore()
    total = 0
    for device, condition in devices_and_conditions:
        if condition is None:
            pl.semaphore_signal(barrier, inc=1, device_id=device, device_id_type=MESH)
            total = total + 1
        else:
            @pl.when(condition)
            def _():
                pl.semaphore_signal(barrier, inc=1, device_id=device, device_id_type=MESH)
            total = total + condition.astype(jnp.int32)
    pl.semaphore_wait(barrier, total)


def add_into(target, *sources):
    rows = target.shape[0]
    step = ADD_ROWS if rows % ADD_ROWS == 0 else 8

    @pl.loop(0, rows // step)
    def _(i):
        part = pl.ds(pl.multiple_of(i * step, step), step)
        total = target[part].astype(jnp.float32)
        for source in sources:
            total = total + source[part].astype(jnp.float32)
        target[part] = total.astype(target.dtype)


def remote(source, target, send, recv, device):
    return pltpu.make_async_remote_copy(
        src_ref=source, dst_ref=target, send_sem=send, recv_sem=recv,
        device_id=device, device_id_type=MESH,
    )


PARTS = 2


def part_of(ref, part):
    rows = ref.shape[0] // PARTS
    return ref.at[pl.ds(part * rows, rows)]


class Gather:
    def __init__(self, at, ins, outs, held, send, recv, own_sem):
        self.at, self.ins, self.outs, self.held = at, ins, outs, held
        self.send, self.recv, self.own_sem = send, recv, own_sem
        self.count = len(ins)
        z = at.z
        up, down = at.device(z + 1, 0, 0), at.device(z - 1, 0, 0)
        one, two, twin = at.device(z, 1, 0), at.device(z, 0, 1), at.device(z, 0, 0, 1)
        self.routes = {"up": (0, up), "down": (1, down), "one": (2, one), "two": (3, two), "twin": (4, twin)}

    def greet(self):
        z = self.at.z
        conditions = {"up": z < LINE - 1, "down": z > 0}
        greet([(device, conditions.get(name)) for name, (_, device) in self.routes.items()])

    def copies(self, block, part, route, own=False):
        lane, device = self.routes[route]
        return [
            remote(part_of(self.ins[i] if own else self.outs[i].at[block], part), part_of(self.outs[i].at[block], part),
                   self.send.at[i, part, lane, block], self.recv.at[i, part, block], device)
            for i in range(self.count)
        ]

    def forward(self, block, part, *ways, own=False):
        for route in ways:
            for copy in self.copies(block, part, route, own):
                copy.start()

    def arrived(self, block, part):
        for copy in self.copies(block, part, "twin"):
            copy.wait_recv()

    def begin(self):
        z, mine = self.at.z, self.at.block(self.at.z, 0, 0)
        for part in range(PARTS):
            pl.when(z < LINE - 1)(functools.partial(self.forward, mine, part, "up", own=True))
            pl.when(z > 0)(functools.partial(self.forward, mine, part, "down", own=True))
            self.forward(mine, part, "one", "two", "twin", own=True)
        for way in (0, 1):
            moves = [
                pltpu.make_async_copy(self.ins[i], self.held[i], self.own_sem.at[i]) if way == 0
                else pltpu.make_async_copy(self.held[i], self.outs[i].at[mine], self.own_sem.at[i])
                for i in range(self.count)
            ]
            for move in moves:
                move.start()
            for move in moves:
                move.wait()

    def line(self, step):
        z = self.at.z
        for part in range(PARTS):
            @pl.when(z - step >= 0)
            def _():
                block = self.at.block(z - step, 0, 0)
                self.arrived(block, part)
                pl.when(z < LINE - 1)(functools.partial(self.forward, block, part, "up"))
                self.forward(block, part, "one", "two", "twin")

            @pl.when(z + step < LINE)
            def _():
                block = self.at.block(z + step, 0, 0)
                self.arrived(block, part)
                pl.when(z > 0)(functools.partial(self.forward, block, part, "down"))
                self.forward(block, part, "one", "two", "twin")

    def face(self, step, first, second):
        z = self.at.z
        ways = ("twin",) if second else ("two", "twin")
        for part in range(PARTS):
            def take(line):
                block = self.at.block(line, first, second)
                self.arrived(block, part)
                self.forward(block, part, *ways)
            if step == 0:
                take(z)
            else:
                pl.when(z - step >= 0)(functools.partial(take, z - step))
                pl.when(z + step < LINE)(functools.partial(take, z + step))

    def faces(self, step):
        self.face(step, 1, 0)
        self.face(step, 0, 1)

    def from_twin(self, group):
        for y in (0, 1):
            for part in range(PARTS):
                self.arrived(group * 4 + y * 2 + 1 - self.at.core, part)

    def end(self):
        z = self.at.z

        def sent(block, part, *ways):
            for route in ways:
                for copy in self.copies(block, part, route):
                    copy.wait_send()

        for line in range(LINE):
            for part in range(PARTS):
                block = self.at.block(line, 0, 0)
                pl.when((z >= line) & (z < LINE - 1))(functools.partial(sent, block, part, "up"))
                pl.when((z <= line) & (z > 0))(functools.partial(sent, block, part, "down"))
                sent(block, part, "one", "two", "twin")
                sent(self.at.block(line, 1, 0), part, "two", "twin")
                sent(self.at.block(line, 0, 1), part, "twin")
                sent(self.at.block(line, 1, 1), part, "twin")


PARTS = 2


def part_of(ref, part):
    rows = ref.shape[0] // PARTS
    return ref.at[pl.ds(part * rows, rows)]


ORDER = (3, 0, 2, 1)


def scatter_kernel(count, *refs):
    ins, outs = refs[:count], refs[count:2 * count]
    rest = [refs[2 * count + k * count:2 * count + (k + 1) * count] for k in range(6)]
    acc, from_twin, from_two, from_one, from_below, from_above = rest
    load_sem, store_sem, send, recv = refs[8 * count:]
    at = Place()
    z = at.z
    up, down = at.device(z + 1, 0, 0), at.device(z - 1, 0, 0)
    one, two, twin = at.device(z, 1, 0), at.device(z, 0, 1), at.device(z, 0, 0, 1)
    greet([(one, None), (two, None), (twin, None), (up, z < LINE - 1), (down, z > 0)])
    units = [(line, part) for line in ORDER for part in range(PARTS)]
    corners = [(1, 1), (1, 0), (0, 1), (0, 0)]

    def slot(line, second, first):
        return second * 8 + first * 4 + line

    def load(i, part, line, second, first):
        here = slot(line, second, first)
        return pltpu.make_async_copy(part_of(ins[i].at[at.stored(line, first, second)], part),
                                     part_of(acc[i].at[here], part), load_sem.at[i, part, here])

    def hop(i, part, source, target, lane, device):
        return remote(part_of(source, part), part_of(target, part), send.at[i, part, lane], recv.at[i, part, lane], device)

    def to_twin(i, part, line, second, first):
        here = slot(line, second, first)
        return hop(i, part, ins[i].at[at.stored(line, first, second, 1)], from_twin[i].at[here], here, twin)

    def to_two(i, part, line, first):
        return hop(i, part, acc[i].at[slot(line, 1, first)], from_two[i].at[first * 4 + line], 16 + first * 4 + line, two)

    def to_one(i, part, line):
        return hop(i, part, acc[i].at[slot(line, 0, 1)], from_one[i].at[line], 24 + line, one)

    def rise(i, part, line):
        return hop(i, part, acc[i].at[line], from_below[i].at[line], 28 + line, up)

    def fall(i, part, line):
        return hop(i, part, acc[i].at[line], from_above[i].at[line], 32 + line, down)

    def begin(line, part):
        for second, first in corners:
            for i in range(count):
                to_twin(i, part, line, second, first).start()
                load(i, part, line, second, first).start()

    def gathered(line, part, second, first):
        for i in range(count):
            load(i, part, line, second, first).wait()
            to_twin(i, part, line, second, first).wait_recv()
            sources = [from_twin[i].at[slot(line, second, first)]]
            if not second:
                to_two(i, part, line, first).wait_recv()
                sources.append(from_two[i].at[first * 4 + line])
                if not first:
                    to_one(i, part, line).wait_recv()
                    sources.append(from_one[i].at[line])
            add_into(part_of(acc[i].at[slot(line, second, first)], part), *[part_of(r, part) for r in sources])
            if second:
                to_two(i, part, line, first).start()
            elif first:
                to_one(i, part, line).start()

    def line_hop(line, part, hops):
        @pl.when(z == hops)
        def _():
            for i in range(count):
                if 0 < hops <= line:
                    rise(i, part, line).wait_recv()
                    add_into(part_of(acc[i].at[line], part), part_of(from_below[i].at[line], part))
                if hops < line:
                    rise(i, part, line).start()

        @pl.when(z == LINE - 1 - hops)
        def _():
            for i in range(count):
                if 0 < hops <= LINE - 1 - line:
                    fall(i, part, line).wait_recv()
                    add_into(part_of(acc[i].at[line], part), part_of(from_above[i].at[line], part))
                if hops < LINE - 1 - line:
                    fall(i, part, line).start()

    begin(*units[0])
    begin(*units[1])
    for step in range(len(units) + 2 + LINE):
        if step + 2 < len(units):
            begin(*units[step + 2])
        if step < len(units):
            gathered(*units[step], 1, 1)
            gathered(*units[step], 1, 0)
        if 0 <= step - 1 < len(units):
            gathered(*units[step - 1], 0, 1)
        if 0 <= step - 2 < len(units):
            gathered(*units[step - 2], 0, 0)
        for hops in range(LINE):
            if 0 <= step - 2 - hops < len(units):
                line_hop(*units[step - 2 - hops], hops)
    stores = [pltpu.make_async_copy(acc[i].at[z], outs[i], store_sem.at[i]) for i in range(count)]
    for store in stores:
        store.start()
    for line, part in units:
        for i in range(count):
            for second, first in corners:
                to_twin(i, part, line, second, first).wait_send()
            to_two(i, part, line, 0).wait_send()
            to_two(i, part, line, 1).wait_send()
            to_one(i, part, line).wait_send()
            if line > 0:
                pl.when(z < line)(rise(i, part, line).wait_send)
            if line < LINE - 1:
                pl.when(z > line)(fall(i, part, line).wait_send)
    for store in stores:
        store.wait()


def scatter_blocks(collective_id, *arrays):
    count = len(arrays)

    def slots(n):
        return [pltpu.VMEM((n,) + a.shape[1:], a.dtype) for a in arrays]
    return pl.pallas_call(
        functools.partial(scatter_kernel, count),
        name=f"scatter_blocks_{collective_id}",
        out_shape=tuple(jax.ShapeDtypeStruct(a.shape[1:], a.dtype) for a in arrays),
        in_specs=[pl.BlockSpec(memory_space=pl.ANY)] * count,
        out_specs=tuple(pl.BlockSpec(memory_space=pl.ANY) for _ in arrays),
        scratch_shapes=slots(16) + slots(16) + slots(8) + slots(4) + slots(4) + slots(4)
        + [
            pltpu.SemaphoreType.DMA((count, PARTS, 16)),
            pltpu.SemaphoreType.DMA((count,)),
            pltpu.SemaphoreType.DMA((count, PARTS, 36)),
            pltpu.SemaphoreType.DMA((count, PARTS, 36)),
        ],
        compiler_params=pltpu.CompilerParams(
            collective_id=collective_id, has_side_effects=True, vmem_limit_bytes=60 << 20),
        cost_estimate=pl.CostEstimate(
            flops=0, transcendentals=0, bytes_accessed=sum(a.size * a.dtype.itemsize for a in arrays)),
    )(*arrays)


def sum_task(at, kind, rows, source, result, held, from_pair, from_below, from_above, load_sem, send, recv, delay, prepare=None):
    z, x = at.z, at.x
    pair = ((z * 2 + 1 - x), at.y * 2 + at.core)
    up, down = ((z + 1) * 2 + x, at.y * 2 + at.core), ((z - 1) * 2 + x, at.y * 2 + at.core)
    pair_first = kind == "pair"
    for _ in range(delay):
        yield

    def part(ref, line, face):
        return ref.at[line, face, rows]

    if pair_first:
        def load(line):
            return pltpu.make_async_copy(part(source, line, x), held.at[line], load_sem.at[line])

        def give(line):
            return remote(part(source, line, 1 - x), from_pair.at[line], send.at[0, line], recv.at[0, line], pair)
        for line in ORDER:
            give(line).start()
            load(line).start()
        yield
        yield
        for line in ORDER:
            load(line).wait()
            give(line).wait_recv()
            add_into(held.at[line], from_pair.at[line])
    else:
        def load(line):
            return pltpu.make_async_copy(source.at[line, :, rows], held.at[line], load_sem.at[line])
        for line in ORDER:
            load(line).start()
        for line in ORDER:
            load(line).wait()
        if prepare is not None:
            yield from prepare(held)

    def add(target, extra):
        if pair_first:
            add_into(target, extra)
        else:
            for face in (0, 1):
                add_into(target.at[face], extra.at[face])

    def rise(line):
        return remote(held.at[line], from_below.at[line], send.at[1, line], recv.at[1, line], up)

    def fall(line):
        return remote(held.at[line], from_above.at[line], send.at[2, line], recv.at[2, line], down)

    for line in range(LINE - 1, 0, -1):
        other = LINE - 1 - line

        @pl.when(z < line)
        def _():
            @pl.when(z > 0)
            def _():
                rise(line).wait_recv()
                add(held.at[line], from_below.at[line])
            rise(line).start()

        @pl.when(z > other)
        def _():
            @pl.when(z < LINE - 1)
            def _():
                fall(other).wait_recv()
                add(held.at[other], from_above.at[other])
            fall(other).start()
        yield

    @pl.when(z > 0)
    def _():
        rise(z).wait_recv()
        add(held.at[z], from_below.at[z])

    @pl.when(z < LINE - 1)
    def _():
        fall(z).wait_recv()
        add(held.at[z], from_above.at[z])

    if pair_first:
        def over(line):
            return remote(part(result, line, x), part(result, line, x), send.at[3, line], recv.at[3, line * 2 + x], pair)

        def other_over(line):
            return remote(part(result, line, 1 - x), part(result, line, 1 - x), send.at[3, line],
                          recv.at[3, line * 2 + 1 - x], pair)

        def climb(line):
            return remote(part(result, line, x), part(result, line, x), send.at[4, line], recv.at[3, line * 2 + x], up)

        def sink(line):
            return remote(part(result, line, x), part(result, line, x), send.at[5, line], recv.at[3, line * 2 + x], down)
        own = pltpu.make_async_copy(held.at[z], part(result, z, x), load_sem.at[4])
    else:
        mine = held.at[z]
        swap = remote(mine.at[1 - x], from_pair, send.at[0, 0], recv.at[0, 0], pair)
        swap.start()
        yield
        swap.wait_recv()
        add_into(mine.at[x], from_pair)
        own = pltpu.make_async_copy(mine.at[x], part(result, z, x), load_sem.at[4])

        def over_block(face):
            return remote(part(result, z, face), part(result, z, face), send.at[3, 0], recv.at[3, face], pair)

        def climb(line):
            return remote(result.at[line, :, rows], result.at[line, :, rows], send.at[4, line], recv.at[3, 4 + line], up)

        def sink(line):
            return remote(result.at[line, :, rows], result.at[line, :, rows], send.at[5, line], recv.at[3, 4 + line], down)
    own.start()
    own.wait()
    if pair_first:
        over(z).start()
    else:
        over_block(x).start()
        yield
        over_block(1 - x).wait_recv()

    @pl.when(z < LINE - 1)
    def _():
        climb(z).start()

    @pl.when(z > 0)
    def _():
        sink(z).start()
    yield
    for step in range(1, LINE):
        @pl.when(z - step >= 0)
        def _():
            climb(z - step).wait_recv()

            @pl.when(z < LINE - 1)
            def _():
                climb(z - step).start()
            if pair_first:
                over(z - step).start()

        @pl.when(z + step < LINE)
        def _():
            sink(z + step).wait_recv()

            @pl.when(z > 0)
            def _():
                sink(z + step).start()
            if pair_first:
                over(z + step).start()
        yield
    if pair_first:
        for line in range(LINE):
            other_over(line).wait_recv()
    for line in range(LINE):
        if pair_first:
            give(line).wait_send()
            over(line).wait_send()
        if line > 0:
            pl.when(z < line)(rise(line).wait_send)
        if line < LINE - 1:
            pl.when(z > line)(fall(line).wait_send)
        pl.when((z >= line) & (z < LINE - 1))(climb(line).wait_send)
        pl.when((z <= line) & (z > 0))(sink(line).wait_send)
    if not pair_first:
        swap.wait_send()
        over_block(x).wait_send()


def narrow_sum_task(at, source, result, mine, from_twin, from_peer, load_sem, send, recv):
    twin, peer = at.device(at.z, 0, 0, 1), at.across()

    def give(y):
        return remote(source.at[y * 2 + 1 - at.core], from_twin.at[y], send.at[y], recv.at[y], twin)

    def load(y):
        return pltpu.make_async_copy(source.at[y * 2 + at.core], mine.at[y], load_sem.at[y])
    order = (1 - at.y, at.y)
    for y in order:
        give(y).start()
        load(y).start()
    other, own = order
    over = remote(mine.at[other], from_peer, send.at[2], recv.at[2], peer)
    for y in order:
        load(y).wait()
        give(y).wait_recv()
        add_into(mine.at[y], from_twin.at[y])
        if y is other:
            over.start()
    yield
    over.wait_recv()
    add_into(mine.at[own], from_peer)
    store = pltpu.make_async_copy(mine.at[own], result, load_sem.at[2])
    store.start()
    yield
    store.wait()
    over.wait_send()
    for y in order:
        give(y).wait_send()


def narrow_sum_scratch(block, dtype):
    return [
        pltpu.VMEM((2,) + block, dtype),
        pltpu.VMEM((2,) + block, dtype),
        pltpu.VMEM(block, dtype),
        pltpu.SemaphoreType.DMA((3,)),
        pltpu.SemaphoreType.DMA((3,)),
        pltpu.SemaphoreType.DMA((3,)),
    ]


def run_tasks(tasks):
    while tasks:
        tasks = [task for task in tasks if next(task, tasks) is not tasks]


def narrow_sum_kernel(source, result, *scratch):
    at = Place()
    greet([(at.device(at.z, 0, 0, 1), None), (at.across(), None)])
    run_tasks([narrow_sum_task(at, source, result, *scratch)])


def narrow_sum(collective_id, parts):
    block = parts.shape[1:]
    return pl.pallas_call(
        narrow_sum_kernel,
        name=f"narrow_sum_{collective_id}",
        out_shape=jax.ShapeDtypeStruct(block, parts.dtype),
        in_specs=[pl.BlockSpec(memory_space=pl.ANY)],
        out_specs=pl.BlockSpec(memory_space=pl.ANY),
        scratch_shapes=narrow_sum_scratch(block, parts.dtype),
        compiler_params=pltpu.CompilerParams(collective_id=collective_id, has_side_effects=True),
    )(parts)


def narrow_gather_kernel(block, result, held, load_sem, send, recv):
    at = Place()
    twin, peer = at.device(at.z, 0, 0, 1), at.across()
    greet([(twin, None), (peer, None)])
    here, there = at.y * 2 + at.core, (1 - at.y) * 2 + at.core
    load = pltpu.make_async_copy(block, held, load_sem.at[0])
    load.start()
    over = remote(block, result.at[here], send.at[0], recv.at[here], peer)
    beside = remote(block, result.at[here], send.at[1], recv.at[here], twin)
    over.start()
    beside.start()
    load.wait()
    store = pltpu.make_async_copy(held, result.at[here], load_sem.at[1])
    store.start()
    passed = remote(result.at[there], result.at[there], send.at[2], recv.at[there], twin)
    passed.wait_recv()
    passed.start()
    for y in (0, 1):
        remote(block, result.at[y * 2 + 1 - at.core], send.at[1], recv.at[y * 2 + 1 - at.core], twin).wait_recv()
    for copy in (over, beside, passed):
        copy.wait_send()
    store.wait()


def narrow_gather(collective_id, block):
    return pl.pallas_call(
        narrow_gather_kernel,
        name=f"narrow_gather_{collective_id}",
        out_shape=jax.ShapeDtypeStruct((4,) + block.shape, block.dtype),
        in_specs=[pl.BlockSpec(memory_space=pl.ANY)],
        out_specs=pl.BlockSpec(memory_space=pl.ANY),
        scratch_shapes=[
            pltpu.VMEM(block.shape, block.dtype),
            pltpu.SemaphoreType.DMA((2,)),
            pltpu.SemaphoreType.DMA((3,)),
            pltpu.SemaphoreType.DMA((4,)),
        ],
        compiler_params=pltpu.CompilerParams(collective_id=collective_id, has_side_effects=True),
    )(block)


def narrow_total_kernel(values, result, others, send, recv):
    at = Place()
    places = [at.device(at.z, 0, 0, 1), at.across(), at.across(1)]
    greet([(place, None) for place in places])
    copies = [remote(values, others.at[i], send.at[i], recv.at[i], place) for i, place in enumerate(places)]
    for copy in copies:
        copy.start()
    for copy in copies:
        copy.wait()
    result[...] = (values[...] + others[0]) + (others[1] + others[2])


def narrow_total(collective_id, values):
    return pl.pallas_call(
        narrow_total_kernel,
        name=f"narrow_total_{collective_id}",
        out_shape=jax.ShapeDtypeStruct(values.shape, values.dtype),
        in_specs=[pl.BlockSpec(memory_space=pltpu.VMEM)],
        out_specs=pl.BlockSpec(memory_space=pltpu.VMEM),
        scratch_shapes=[
            pltpu.VMEM((3,) + values.shape, values.dtype),
            pltpu.SemaphoreType.DMA((3,)),
            pltpu.SemaphoreType.DMA((3,)),
        ],
        compiler_params=pltpu.CompilerParams(collective_id=collective_id, has_side_effects=True),
    )(values)


def final_sums_kernel(plan, count, *refs):
    ins, outs, rest = refs[:count], refs[count:2 * count], list(refs[2 * count:])
    at = Place()
    pair = (at.z * 2 + 1 - at.x, at.y * 2 + at.core)
    up, down = ((at.z + 1) * 2 + at.x, at.y * 2 + at.core), ((at.z - 1) * 2 + at.x, at.y * 2 + at.core)
    twin, peer = at.device(at.z, 0, 0, 1), at.across()
    greet([(pair, None), (twin, None), (peer, None), (up, at.z < LINE - 1), (down, at.z > 0)])
    narrow_scratch, rest = rest[-6:], rest[:-6]
    load_sem, send, recv, others, other_send, other_recv = rest[-6:]

    def over_narrow(held):
        beside = remote(ins[count - 2], others.at[0], other_send.at[0], other_recv.at[0], twin)
        beside.start()
        yield
        beside.wait_recv()
        for line in range(LINE):
            for face in (0, 1):
                add_into(held.at[line, face], others.at[0, line, face])
        across = remote(held, others.at[1], other_send.at[1], other_recv.at[1], peer)
        across.start()
        yield
        across.wait()
        beside.wait_send()
        for line in range(LINE):
            for face in (0, 1):
                add_into(held.at[line, face], others.at[1, line, face])
    tasks = [narrow_sum_task(at, ins[-1], outs[-1], *narrow_scratch)]
    for number, (which, begin, rows, kind, delay) in enumerate(plan):
        held, from_pair, from_below, from_above = rest[4 * number:4 * number + 4]
        tasks.append(sum_task(at, kind, pl.ds(begin, rows), ins[which], outs[which], held, from_pair, from_below,
                              from_above, load_sem.at[number], send.at[number], recv.at[number], delay,
                              over_narrow if which == count - 2 else None))
    run_tasks(tasks)


def final_sums(collective_id, plan, *arrays):
    count, steps = len(arrays), len(plan)
    scratch = []
    for which, _, rows, kind, _ in plan:
        columns, dtype = arrays[which].shape[3], arrays[which].dtype
        block = (() if kind == "pair" else (2,)) + (rows, columns)
        scratch += [
            pltpu.VMEM((LINE,) + block, dtype),
            pltpu.VMEM(((LINE,) if kind == "pair" else ()) + (rows, columns), dtype),
            pltpu.VMEM((LINE,) + block, dtype),
            pltpu.VMEM((LINE,) + block, dtype),
        ]
    small, parts = arrays[-2:]
    moved = sum(a.size * a.dtype.itemsize for a in arrays)
    return pl.pallas_call(
        functools.partial(final_sums_kernel, plan, count),
        name=f"final_sums_{collective_id}",
        out_shape=tuple(jax.ShapeDtypeStruct(a.shape, a.dtype) for a in arrays[:-1])
        + (jax.ShapeDtypeStruct(parts.shape[1:], parts.dtype),),
        in_specs=[pl.BlockSpec(memory_space=pl.ANY)] * count,
        out_specs=tuple(pl.BlockSpec(memory_space=pl.ANY) for _ in arrays),
        scratch_shapes=scratch + [
            pltpu.SemaphoreType.DMA((steps, 5)),
            pltpu.SemaphoreType.DMA((steps, 6, 4)),
            pltpu.SemaphoreType.DMA((steps, 4, 8)),
            pltpu.VMEM((2,) + small.shape, small.dtype),
            pltpu.SemaphoreType.DMA((2,)),
            pltpu.SemaphoreType.DMA((2,)),
        ] + narrow_sum_scratch(parts.shape[1:], parts.dtype),
        compiler_params=pltpu.CompilerParams(
            collective_id=collective_id, has_side_effects=True, vmem_limit_bytes=48 << 20),
        cost_estimate=pl.CostEstimate(flops=0, transcendentals=0, bytes_accessed=2 * moved),
    )(*arrays)


def own_exchange():
    return lax.axis_size("wide") == 8 and lax.axis_size("narrow") == 4


def scatter_all(*arrays):
    if own_exchange():
        return scatter_blocks(2, *arrays)
    return tuple(lax.psum_scatter(a, BOTH, scatter_dimension=0) for a in arrays)


FINAL_PLAN = (
    (4, 0, 72, "line", 0),
    (0, 0, 128, "pair", 0),
    (3, 0, 64, "line", 0),
    (0, 128, 128, "pair", 1),
    (1, 0, 128, "pair", 2),
    (1, 128, 128, "pair", 3),
    (2, 0, 128, "pair", 4),
    (2, 128, 128, "pair", 5),
)


def total_weights(weights, gains, everywhere, parts):
    if not own_exchange():
        totals = tuple(a.astype(jnp.float32) for a in lax.psum(tuple(a.astype(jnp.bfloat16) for a in weights), "wide"))
        own = lax.psum_scatter(parts, "narrow", scatter_dimension=0, tiled=True)
        return totals, lax.psum(gains, "wide"), lax.psum(everywhere, BOTH), own
    gain_rows = jnp.concatenate([a.reshape(-1, 128) for a in gains], axis=0)
    mine = lax.axis_index("narrow")
    gain_slots = lax.dynamic_update_slice_in_dim(jnp.zeros((4,) + gain_rows.shape, jnp.float32), gain_rows[None], mine, 0)
    pieces = [a.reshape(-1, 128) for a in everywhere] + [gain_slots.reshape(-1, 128)]
    small = jnp.concatenate(pieces, axis=0)
    arrays = [a.astype(jnp.bfloat16).reshape(LINE, 2, a.shape[0] // 8, a.shape[1]) for a in weights]
    results = final_sums(
        3, FINAL_PLAN, *arrays, small.reshape(LINE, 2, small.shape[0] // 8, 128), parts.reshape(4, -1, parts.shape[1])
    )
    totals = tuple(r.reshape(a.shape).astype(jnp.float32) for r, a in zip(results, weights))
    small_total = results[-2].reshape(small.shape)
    summed, begin = [], 0
    for array, piece in zip(everywhere, pieces):
        summed.append(small_total[begin:begin + piece.shape[0]].reshape(array.shape))
        begin += piece.shape[0]
    own_gains = lax.dynamic_slice_in_dim(small_total[begin:].reshape(gain_slots.shape), mine, 1, 0).reshape(len(gains), -1)
    return totals, tuple(own_gains[i].reshape(g.shape) for i, g in enumerate(gains)), tuple(summed), results[-1]


def narrow_sums(collective_id, values):
    if not own_exchange():
        return lax.psum(values, "narrow")
    total = narrow_total(collective_id, jnp.stack(values).reshape(-1, 128)).reshape(len(values), -1)
    return tuple(total[i] for i in range(len(values)))


def narrow_deal(collective_id, parts):
    if not own_exchange():
        return lax.psum_scatter(parts, "narrow", scatter_dimension=0, tiled=True)
    return narrow_sum(collective_id, parts.reshape(4, -1, parts.shape[1]))


def narrow_all(collective_id, block):
    if not own_exchange():
        return lax.all_gather(block, "narrow", axis=0, tiled=True)
    return narrow_gather(collective_id, block).reshape(-1, block.shape[1])


def experts_plain(rows_all, grads_all, places_here, probs_here, gate_weight, up_weight, down_weight, capacity):
    block_count, own_rows, model_width = rows_all.shape
    experts_here = gate_weight.shape[0]
    highest_precision = lax.Precision.HIGHEST
    pick = places_here[:, :, None, :] == jnp.arange(capacity, dtype=jnp.float32)[None, None, :, None]
    pick_low = pick.astype(jnp.bfloat16)
    slot_gate = jnp.sum(jnp.where(pick, probs_here[:, :, None, :], 0.0), axis=-1)
    slot_gate = slot_gate.transpose(1, 0, 2).reshape(experts_here, block_count * capacity, 1)

    def spread(rows):
        out = jnp.einsum("best,btd->ebsd", pick_low, rows, preferred_element_type=jnp.float32)
        return out.astype(jnp.bfloat16).reshape(experts_here, block_count * capacity, model_width)

    def collect(slots):
        out = jnp.einsum(
            "best,ebsd->btd",
            pick_low,
            slots.reshape(experts_here, block_count, capacity, model_width),
            preferred_element_type=jnp.float32,
        )
        return out.astype(jnp.bfloat16)

    slot_rows = spread(rows_all)
    slot_grads = spread(grads_all)
    gate_pre = jnp.einsum("erd,edf->erf", slot_rows, gate_weight, preferred_element_type=jnp.float32)
    up_pre = jnp.einsum("erd,edf->erf", slot_rows, up_weight, preferred_element_type=jnp.float32)
    activated, unit_back = jax.vjp(gated_unit, gate_pre, up_pre)
    gated_act = (activated * slot_gate).astype(jnp.bfloat16)
    raw_act_grad = jnp.einsum("erd,efd->erf", slot_grads, down_weight, preferred_element_type=jnp.float32)
    slot_gate_grads = jnp.sum(activated * raw_act_grad, axis=-1)
    gate_grad_full, up_grad_full = unit_back(raw_act_grad * slot_gate)
    gate_grad_low = gate_grad_full.astype(jnp.bfloat16)
    up_grad_low = up_grad_full.astype(jnp.bfloat16)
    gate_grad_parts = jnp.einsum(
        "best,ebs->bet",
        pick.astype(jnp.float32),
        slot_gate_grads.reshape(experts_here, block_count, capacity),
        precision=highest_precision,
    )
    back_slots = jnp.einsum(
        "erf,edf->erd", gate_grad_low, gate_weight, preferred_element_type=jnp.float32
    ) + jnp.einsum("erf,edf->erd", up_grad_low, up_weight, preferred_element_type=jnp.float32)
    out_slots = jnp.einsum("erf,efd->erd", gated_act, down_weight, preferred_element_type=jnp.float32)
    return (
        collect(out_slots.astype(jnp.bfloat16)),
        collect(back_slots.astype(jnp.bfloat16)),
        gate_grad_parts,
        jnp.einsum("erd,erf->edf", slot_rows, gate_grad_low, preferred_element_type=jnp.float32),
        jnp.einsum("erd,erf->edf", slot_rows, up_grad_low, preferred_element_type=jnp.float32),
        jnp.einsum("erf,erd->efd", gated_act, slot_grads, preferred_element_type=jnp.float32),
    )


STEP_BLOCKS = 4


def dot(left, right, left_dim=1, right_dim=0):
    return lax.dot_general(
        left, right, (((left_dim,), (right_dim,)), ((), ())), preferred_element_type=jnp.float32
    )


def experts_kernel(
    capacity, rows_own, grads_own, routes_own, gate_w, up_w, down_w,
    rows_all, grads_all, routes_all, out, back, gate_grads, gate_dw, up_dw, down_dw,
    row_slots, grad_slots, rows_held, grads_held, routes_held, load_sem, send, recv, own_sem,
):
    experts = gate_w.shape[0]
    tokens = rows_own.shape[0]
    everywhere = routes_own.shape[0] // 2
    turn = pl.program_id(0)
    turns = LINE * 2
    at = Place()
    first_expert = lax.axis_index("wide") * experts
    gathered, held = (rows_all, grads_all, routes_all), (rows_held, grads_held, routes_held)
    gather = Gather(at, (rows_own, grads_own, routes_own), gathered, [h.at[1, 0] for h in held], send, recv, own_sem)
    slot_ids = lax.broadcasted_iota(jnp.int32, (capacity, tokens), 0).astype(jnp.float32)

    def loads(number):
        group = at.group(number)
        slot = lax.rem(number, 2)
        return [
            pltpu.make_async_copy(gathered[i].at[pl.ds(group * STEP_BLOCKS, STEP_BLOCKS)], held[i].at[slot],
                                  load_sem.at[i, slot])
            for i in range(3)
        ]

    def fetch(number):
        gather.from_twin(at.group(number))
        for load in loads(number):
            load.start()

    def on(number, *work):
        @pl.when(turn == number)
        def _():
            for piece, *arguments in work:
                piece(*arguments)

    @pl.when(turn == 0)
    def _():
        gather.greet()
        gather.begin()
        for target in (gate_dw, up_dw, down_dw):
            @pl.loop(0, experts)
            def _(e):
                target[e] = jnp.zeros(target.shape[1:], jnp.float32)
        gather.line(1)
        gather.faces(0)
        fetch(jnp.int32(0))

    for load in loads(turn):
        load.wait()
    slot = lax.rem(turn, 2)
    rows, grads, routes = rows_held.at[slot], grads_held.at[slot], routes_held.at[slot]

    def pick_of(block, expert):
        return routes[block, pl.ds(everywhere + first_expert + expert, 1), :] == slot_ids

    def picks(block):
        return jnp.concatenate(
            [pick_of(block, e).astype(jnp.float32) for e in range(experts)], axis=0
        ).astype(jnp.bfloat16)

    for block in range(STEP_BLOCKS):
        pick = picks(block)
        part = pl.ds(block * capacity, capacity)
        for source, target in ((rows, row_slots), (grads, grad_slots)):
            slots = dot(pick, source[block]).astype(jnp.bfloat16)
            for e in range(experts):
                target[e, part] = slots[e * capacity:(e + 1) * capacity]

    on(1, (gather.line, 2), (gather.faces, 1))
    on(2, (gather.line, 3), (gather.faces, 2))

    @pl.loop(0, experts)
    def _(e):
        gate_pre, up_pre = dot(row_slots[e], gate_w[e]), dot(row_slots[e], up_w[e])
        raw = dot(grad_slots[e], down_w[e], 1, 1)
        slot_gate = jnp.concatenate([
            jnp.sum(jnp.where(pick_of(block, e), routes[block, pl.ds(first_expert + e, 1), :], 0.0),
                    axis=1, keepdims=True)
            for block in range(STEP_BLOCKS)
        ], axis=0)
        sigma = 1.0 / (1.0 + jnp.exp(-gate_pre))
        silu = gate_pre * sigma
        act = silu * up_pre
        slot_sum = jnp.sum(act * raw, axis=1, keepdims=True)
        for block in range(STEP_BLOCKS):
            gate_grads[block, pl.ds(e, 1), :] = jnp.sum(
                jnp.where(pick_of(block, e), slot_sum[block * capacity:(block + 1) * capacity], 0.0),
                axis=0, keepdims=True,
            )
        gated = (act * slot_gate).astype(jnp.bfloat16)
        act_grad = raw * slot_gate
        gate_low = (act_grad * up_pre * sigma * (1.0 + gate_pre * (1.0 - sigma))).astype(jnp.bfloat16)
        up_low = (act_grad * silu).astype(jnp.bfloat16)
        down_dw[e] += dot(gated, grad_slots[e], 0, 0)
        grad_slots[e] = dot(gated, down_w[e]).astype(jnp.bfloat16)
        turned = row_slots[e].T
        gate_dw[e] += dot(turned, gate_low)
        up_dw[e] += dot(turned, up_low)
        row_slots[e] = (dot(gate_low, gate_w[e], 1, 1) + dot(up_low, up_w[e], 1, 1)).astype(jnp.bfloat16)

    on(0, (gather.face, 0, 1, 1))
    on(2, (gather.face, 1, 1, 1))
    on(3, (gather.faces, 3))
    on(4, (gather.face, 2, 1, 1))
    on(6, (gather.face, 3, 1, 1))

    @pl.when(turn < turns - 1)
    def _():
        fetch(turn + 1)

    for block in range(STEP_BLOCKS):
        pick = picks(block)
        part = pl.ds(block * capacity, capacity)
        for source, target in ((row_slots, back), (grad_slots, out)):
            slots = jnp.concatenate([source[e, part] for e in range(experts)], axis=0)
            target[block] = dot(pick, slots, 0, 0).astype(jnp.bfloat16)

    on(turns - 1, (gather.end,))


def gather_experts(collective_id, rows, grads, routes, gate_weight, up_weight, down_weight, capacity):
    own_rows, width = rows.shape
    experts, _, hidden = gate_weight.shape
    block_count = LINE * 2 * STEP_BLOCKS
    step_rows = STEP_BLOCKS * capacity

    def stepped(*shape):
        return pl.BlockSpec((STEP_BLOCKS,) + shape, lambda i: (i,) + (0,) * len(shape))

    def whole(array):
        return pl.BlockSpec(array.shape, lambda i: (0,) * array.ndim, pipeline_mode=pl.Buffered(1))
    weights, owns = (gate_weight, up_weight, down_weight), (rows, grads, routes)
    flops = 2 * block_count * experts * (9 * capacity * width * hidden + 4 * capacity * own_rows * width)
    shapes = jax.ShapeDtypeStruct
    results = pl.pallas_call(
        functools.partial(experts_kernel, capacity),
        name="gather_experts",
        grid=(block_count // STEP_BLOCKS,),
        out_shape=tuple(shapes((block_count,) + a.shape, a.dtype) for a in owns)
        + (
            shapes((block_count, own_rows, width), jnp.bfloat16),
            shapes((block_count, own_rows, width), jnp.bfloat16),
            shapes((block_count, experts, own_rows), jnp.float32),
        ) + tuple(shapes(w.shape, jnp.float32) for w in weights),
        in_specs=[pl.BlockSpec(memory_space=pl.ANY)] * 3 + [whole(w) for w in weights],
        out_specs=(pl.BlockSpec(memory_space=pl.ANY),) * 3
        + (stepped(own_rows, width), stepped(own_rows, width), stepped(experts, own_rows))
        + tuple(whole(w) for w in weights),
        scratch_shapes=[
            pltpu.VMEM((experts, step_rows, width), jnp.bfloat16),
            pltpu.VMEM((experts, step_rows, width), jnp.bfloat16),
        ] + [pltpu.VMEM((2, STEP_BLOCKS) + a.shape, a.dtype) for a in owns] + [
            pltpu.SemaphoreType.DMA((3, 2)),
            pltpu.SemaphoreType.DMA((3, PARTS, 5, block_count)),
            pltpu.SemaphoreType.DMA((3, PARTS, block_count)),
            pltpu.SemaphoreType.DMA((3,)),
        ],
        compiler_params=pltpu.CompilerParams(
            collective_id=collective_id, has_side_effects=True,
            dimension_semantics=("arbitrary",), vmem_limit_bytes=67_000_000),
        cost_estimate=pl.CostEstimate(
            flops=flops, transcendentals=0,
            bytes_accessed=8 * block_count * rows.size + sum(6 * w.size for w in weights)),
    )(*owns, *weights)
    return results[3:]


def local(
    block_input,
    attn_gain,
    query_weight,
    key_weight,
    value_weight,
    query_gain,
    key_gain,
    out_weight,
    moe_gain,
    router_weight,
    gate_weight,
    up_weight,
    down_weight,
    segment_ids,
    expert_ids,
    out_cotangent,
):
    group_rows, model_width = block_input.shape
    own_rows = out_cotangent.shape[0]
    local_width = query_weight.shape[1]
    head_size = HEAD_DIM
    local_heads = local_width // head_size
    wide_size = lax.axis_size("wide")
    experts_all = router_weight.shape[1]
    experts_here = gate_weight.shape[0]
    choose_count = expert_ids.shape[1]
    capacity = 3 * own_rows * choose_count // (2 * experts_all)
    row_begin = lax.axis_index("narrow") * own_rows
    blocks = group_rows // QBLK
    highest_precision = lax.Precision.HIGHEST
    block_count = wide_size * lax.axis_size("narrow")
    chosen = (expert_ids[:, :, None] == jnp.arange(experts_all)[None, None, :]).any(axis=1)
    token_order = jnp.arange(own_rows)
    earlier = jnp.dot(
        (token_order[:, None] > token_order[None, :]).astype(jnp.bfloat16),
        chosen.astype(jnp.bfloat16),
        preferred_element_type=jnp.float32,
    )
    inputs_all = block_input.astype(jnp.float32)
    normed_one = rms_scale(inputs_all, attn_gain.astype(jnp.float32)).astype(jnp.bfloat16)
    joined_weight = jnp.concatenate([query_weight, key_weight, value_weight], axis=1)
    projected = jnp.dot(normed_one, joined_weight, preferred_element_type=jnp.float32)
    query_proj = projected[:, :local_width]
    key_proj = projected[:, local_width : 2 * local_width]
    value_proj = projected[:, 2 * local_width :]
    rope_cos, rope_sin = rope_tables(group_rows, head_size)
    query_total, key_total = narrow_sums(
        4, (jnp.sum(query_proj * query_proj, axis=1), jnp.sum(key_proj * key_proj, axis=1))
    )
    query_inverse = lax.rsqrt(query_total / model_width + norm_epsilon)[:, None]
    key_inverse = lax.rsqrt(key_total / model_width + norm_epsilon)[:, None]
    query_scale = query_gain.astype(jnp.float32)
    key_scale = key_gain.astype(jnp.float32)
    query_normed = query_proj * query_inverse * query_scale
    key_normed = key_proj * key_inverse * key_scale

    def turn_both(query_in, key_in):
        return (
            rotate(query_in, rope_cos, rope_sin, head_size) * head_size ** (-0.5),
            rotate(key_in, rope_cos, rope_sin, head_size),
        )

    (turned_query, turned_key), turn_back = jax.vjp(turn_both, query_normed, key_normed)
    query_heads = turned_query.astype(jnp.bfloat16).reshape(group_rows, local_heads, head_size)
    key_heads = turned_key.astype(jnp.bfloat16).reshape(group_rows, local_heads, head_size)
    value_heads = value_proj.astype(jnp.bfloat16).reshape(group_rows, local_heads, head_size)
    positions = jnp.arange(group_rows)

    def block_scores(block_index):
        block_begin = block_index * QBLK
        query_block = lax.dynamic_slice_in_dim(query_heads, block_begin, QBLK, 0)
        query_segments = lax.dynamic_slice_in_dim(segment_ids, block_begin, QBLK, 0)
        query_places = block_begin + jnp.arange(QBLK)
        allowed = (query_segments[:, None] == segment_ids[None, :]) & (
            query_places[:, None] >= positions[None, :]
        )
        scores = jnp.einsum(
            "qhd,khd->hqk", query_block, key_heads, preferred_element_type=jnp.float32
        )
        return (query_block, jnp.where(allowed[None], scores, masked_score))

    def attend(block_index):
        query_block, scores = block_scores(block_index)
        highest = jnp.max(scores, axis=-1, keepdims=True)
        weights = jnp.exp(scores - highest)
        totals = jnp.sum(weights, axis=-1, keepdims=True)
        probs_low = (weights / totals).astype(jnp.bfloat16)
        mixed_rows = jnp.einsum(
            "hqk,khd->qhd", probs_low, value_heads, preferred_element_type=jnp.float32
        )
        return (mixed_rows, highest + jnp.log(totals))

    mixed_blocks, log_totals = lax.map(attend, jnp.arange(blocks))
    heads_out = mixed_blocks.reshape(group_rows, local_width).astype(jnp.bfloat16)
    attn_own = narrow_deal(
        6, jnp.dot(heads_out, out_weight, preferred_element_type=jnp.float32).astype(jnp.bfloat16)
    ).astype(jnp.float32)
    input_own = lax.dynamic_slice_in_dim(inputs_all, row_begin, own_rows, 0)
    hidden = input_own + attn_own
    normed_two_full, norm_two_back = jax.vjp(rms_scale, hidden, moe_gain.astype(jnp.float32))
    normed_two = normed_two_full.astype(jnp.bfloat16)
    logits = jnp.dot(normed_two, router_weight, preferred_element_type=jnp.float32)
    route_probs = jax.nn.softmax(logits, axis=-1)
    routes = jnp.concatenate([route_probs.T, jnp.where(chosen, earlier, -1.0).T], axis=0)
    expert_begin = lax.axis_index("wide") * experts_here
    expert_weights = (gate_weight, up_weight, down_weight)
    if own_exchange():
        results = gather_experts(1, normed_two, out_cotangent, routes, *expert_weights, capacity)
    else:
        rows_all, grads_all, routes_all = (lax.all_gather(a, BOTH, axis=0) for a in (normed_two, out_cotangent, routes))
        probs_here = lax.dynamic_slice_in_dim(routes_all, expert_begin, experts_here, 1)
        places_here = lax.dynamic_slice_in_dim(routes_all, experts_all + expert_begin, experts_here, 1)
        results = experts_plain(rows_all, grads_all, places_here, probs_here, *expert_weights, capacity)
    out_parts, back_parts, gate_grad_parts, gate_weight_grad, up_weight_grad, down_weight_grad = results
    gate_grad_wide = lax.dynamic_update_slice_in_dim(
        jnp.zeros((block_count, experts_all, own_rows), jnp.float32), gate_grad_parts, expert_begin, 1
    )
    rows_back, prob_grads, moe_out = scatter_all(
        back_parts, gate_grad_wide, out_parts
    )
    rows_back, prob_grads, moe_out = rows_back.astype(jnp.float32), prob_grads.T, moe_out.astype(jnp.float32)
    block_output = (hidden + moe_out).astype(jnp.bfloat16)
    logit_grads = route_probs * (
        prob_grads - jnp.sum(route_probs * prob_grads, axis=-1, keepdims=True)
    )
    router_part = lax.dot_general(
        normed_two.astype(jnp.float32),
        logit_grads,
        (((0,), (0,)), ((), ())),
        precision=highest_precision,
    )
    router_back = lax.dot_general(
        logit_grads,
        router_weight.astype(jnp.float32),
        (((1,), (1,)), ((), ())),
        precision=highest_precision,
    )
    normed_two_grad = rows_back + router_back
    cotangent_full = out_cotangent.astype(jnp.float32)
    hidden_path, moe_gain_part = norm_two_back(normed_two_grad)
    hidden_grad = cotangent_full + hidden_path
    hidden_grad_low = hidden_grad.astype(jnp.bfloat16)
    gathered_piece = narrow_all(7, hidden_grad_low)
    heads_grad_acc = contract_last(gathered_piece, out_weight)
    out_weight_acc = contract_rows(heads_out, gathered_piece)
    heads_grad_low = heads_grad_acc.astype(jnp.bfloat16).reshape(group_rows, local_heads, head_size)

    def back_block(running, items):
        key_acc, value_acc = running
        block_index, log_total = items
        query_block, scores = block_scores(block_index)
        probs = jnp.exp(scores - log_total)
        probs_low = probs.astype(jnp.bfloat16)
        grad_block = lax.dynamic_slice_in_dim(heads_grad_low, block_index * QBLK, QBLK, 0)
        weight_grads = jnp.einsum(
            "qhd,khd->hqk", grad_block, value_heads, preferred_element_type=jnp.float32
        )
        row_dots = jnp.sum(probs * weight_grads, axis=-1, keepdims=True)
        score_grads = (probs * (weight_grads - row_dots)).astype(jnp.bfloat16)
        query_grad_block = jnp.einsum(
            "hqk,khd->qhd", score_grads, key_heads, preferred_element_type=jnp.float32
        )
        key_acc = key_acc + jnp.einsum(
            "hqk,qhd->khd", score_grads, query_block, preferred_element_type=jnp.float32
        )
        value_acc = value_acc + jnp.einsum(
            "hqk,qhd->khd", probs_low, grad_block, preferred_element_type=jnp.float32
        )
        return ((key_acc, value_acc), query_grad_block)

    zero_heads = jnp.zeros((group_rows, local_heads, head_size), jnp.float32)
    (key_grad, value_grad), query_grads = lax.scan(
        back_block, (zero_heads, zero_heads), (jnp.arange(blocks), log_totals)
    )
    query_normed_grad, key_normed_grad = turn_back(
        (query_grads.reshape(group_rows, local_width), key_grad.reshape(group_rows, local_width))
    )
    query_gain_part = jnp.sum(query_normed_grad * query_proj * query_inverse, axis=0)
    key_gain_part = jnp.sum(key_normed_grad * key_proj * key_inverse, axis=0)
    query_gained = query_normed_grad * query_scale
    key_gained = key_normed_grad * key_scale
    query_dot, key_dot = narrow_sums(
        5, (jnp.sum(query_proj * query_gained, axis=1), jnp.sum(key_proj * key_gained, axis=1))
    )
    query_proj_grad = (
        query_inverse * query_gained
        - query_proj * query_inverse**3 * (query_dot / model_width)[:, None]
    )
    key_proj_grad = (
        key_inverse * key_gained - key_proj * key_inverse**3 * (key_dot / model_width)[:, None]
    )
    proj_grad_low = jnp.concatenate(
        [query_proj_grad, key_proj_grad, value_grad.reshape(group_rows, local_width)], axis=1
    ).astype(jnp.bfloat16)
    weight_parts = tuple(
        contract_rows(normed_one, proj_grad_low[:, i * local_width : (i + 1) * local_width]) for i in range(3)
    ) + (out_weight_acc,)
    normed_one_part = contract_last(proj_grad_low, joined_weight)
    scaled_inputs = rms_scale(inputs_all, 1.0)
    attn_gain_part = jnp.sum(normed_one_part * scaled_inputs, axis=0)
    totals, gain_totals, summed, normed_one_own = total_weights(
        weight_parts,
        (query_gain_part, key_gain_part),
        (router_part, attn_gain_part, moe_gain_part),
        normed_one_part.astype(jnp.bfloat16),
    )
    query_weight_grad, key_weight_grad, value_weight_grad, out_weight_grad = totals
    query_gain_grad, key_gain_grad = gain_totals
    router_weight_grad, attn_gain_grad, moe_gain_grad = summed
    _, norm_one_back = jax.vjp(lambda v: rms_scale(v, attn_gain.astype(jnp.float32)), input_own)
    (input_path,) = norm_one_back(normed_one_own.astype(jnp.float32))
    input_grad = (hidden_grad + input_path).astype(jnp.bfloat16)
    return (
        block_output,
        input_grad,
        attn_gain_grad,
        query_weight_grad,
        key_weight_grad,
        value_weight_grad,
        query_gain_grad,
        key_gain_grad,
        out_weight_grad,
        moe_gain_grad,
        router_weight_grad,
        gate_weight_grad,
        up_weight_grad,
        down_weight_grad,
    )


def solution(mesh):
    in_specs = (
        P("wide", None),
        P(),
        P(None, "narrow"),
        P(None, "narrow"),
        P(None, "narrow"),
        P("narrow"),
        P("narrow"),
        P("narrow", None),
        P(),
        P(),
        P("wide", None, "narrow"),
        P("wide", None, "narrow"),
        P("wide", "narrow", None),
        P("wide"),
        P(("wide", "narrow"), None),
        P(("wide", "narrow"), None),
    )
    out_specs = (
        P(("wide", "narrow"), None),
        P(("wide", "narrow"), None),
        P(),
        P(None, "narrow"),
        P(None, "narrow"),
        P(None, "narrow"),
        P("narrow"),
        P("narrow"),
        P("narrow", None),
        P(),
        P(),
        P("wide", None, "narrow"),
        P("wide", None, "narrow"),
        P("wide", "narrow", None),
    )
    return jax.shard_map(local, mesh=mesh, in_specs=in_specs, out_specs=out_specs, check_vma=False)
```

```python
import functools

import jax
import jax.numpy as jnp
from jax import lax
from jax.experimental import pallas as pl
from jax.experimental.pallas import tpu as pltpu
from jax.sharding import PartitionSpec as P

HEAD_DIM = 128
QBLK = 512


norm_epsilon = 1e-05
rope_base = 10000.0
masked_score = -1e30


def rms_scale(values, gain):
    inverse = lax.rsqrt(jnp.mean(values * values, axis=-1, keepdims=True) + norm_epsilon)
    return values * inverse * gain


def rope_tables(length, head_size):
    half_size = head_size // 2
    exponent = jnp.arange(half_size, dtype=jnp.float32) * (2.0 / head_size)
    angle = jnp.arange(length, dtype=jnp.float32)[:, None] * (rope_base ** (-exponent))[None, :]
    return (jnp.cos(angle), jnp.sin(angle))


def rotate(normed, rope_cos, rope_sin, head_size):
    tokens_here = normed.shape[0]
    by_head = normed.reshape(tokens_here, -1, head_size)
    half_size = head_size // 2
    first_half = by_head[..., :half_size]
    second_half = by_head[..., half_size:]
    cos_rows = rope_cos[:, None, :]
    sin_rows = rope_sin[:, None, :]
    turned = jnp.concatenate(
        [
            first_half * cos_rows - second_half * sin_rows,
            second_half * cos_rows + first_half * sin_rows,
        ],
        axis=-1,
    )
    return turned.reshape(tokens_here, -1)


def gated_unit(gate_pre, up_pre):
    return jax.nn.silu(gate_pre) * up_pre


def contract_rows(left, right):
    return lax.dot_general(
        left, right, (((0,), (0,)), ((), ())), preferred_element_type=jnp.float32
    )


def contract_last(left, right):
    return lax.dot_general(
        left, right, (((1,), (1,)), ((), ())), preferred_element_type=jnp.float32
    )


BOTH = ("wide", "narrow")


MESH = pl.DeviceIdType.MESH
LINE = 4
ADD_ROWS = 16


def flip(bit, on):
    return bit + on * (1 - 2 * bit)


class Place:
    def __init__(self):
        wide, narrow = lax.axis_index("wide"), lax.axis_index("narrow")
        self.z, self.x = wide // 2, lax.rem(wide, 2)
        self.y, self.core = narrow // 2, lax.rem(narrow, 2)

    def device(self, z, first, second, other_core=0):
        core = flip(self.core, other_core)
        x = flip(self.x, first * (1 - core) + second * core)
        y = flip(self.y, first * core + second * (1 - core))
        return (z * 2 + x, y * 2 + core)

    def across(self, other_core=0):
        return (self.z * 2 + self.x, (1 - self.y) * 2 + flip(self.core, other_core))

    def block(self, z, first, second, other_core=0):
        wide, narrow = self.device(z, first, second, other_core)
        return wide * 4 + narrow


    def group(self, turn):
        return (flip(self.z // 2, turn // 4) * 4 + flip(lax.rem(self.z, 2), lax.rem(turn // 2, 2)) * 2
                + flip(self.x, lax.rem(turn, 2)))

    def stored(self, line, first, second, other_core=0):
        core = flip(self.core, other_core)
        turn = (flip(self.z // 2, line // 2) * 4 + flip(lax.rem(self.z, 2), line % 2) * 2
                + first * (1 - core) + second * core)
        return turn * 4 + self.device(line, first, second, other_core)[1]


def greet(devices_and_conditions):
    barrier = pltpu.get_barrier_semaphore()
    total = 0
    for device, condition in devices_and_conditions:
        if condition is None:
            pl.semaphore_signal(barrier, inc=1, device_id=device, device_id_type=MESH)
            total = total + 1
        else:
            @pl.when(condition)
            def _():
                pl.semaphore_signal(barrier, inc=1, device_id=device, device_id_type=MESH)
            total = total + condition.astype(jnp.int32)
    pl.semaphore_wait(barrier, total)


def add_into(target, *sources):
    rows = target.shape[0]
    step = ADD_ROWS if rows % ADD_ROWS == 0 else 8

    @pl.loop(0, rows // step)
    def _(i):
        part = pl.ds(pl.multiple_of(i * step, step), step)
        total = target[part].astype(jnp.float32)
        for source in sources:
            total = total + source[part].astype(jnp.float32)
        target[part] = total.astype(target.dtype)


def remote(source, target, send, recv, device):
    return pltpu.make_async_remote_copy(
        src_ref=source, dst_ref=target, send_sem=send, recv_sem=recv,
        device_id=device, device_id_type=MESH,
    )


PARTS = 2


def part_of(ref, part):
    rows = ref.shape[0] // PARTS
    return ref.at[pl.ds(part * rows, rows)]


class Gather:
    def __init__(self, at, ins, outs, held, send, recv, own_sem):
        self.at, self.ins, self.outs, self.held = at, ins, outs, held
        self.send, self.recv, self.own_sem = send, recv, own_sem
        self.count = len(ins)
        z = at.z
        up, down = at.device(z + 1, 0, 0), at.device(z - 1, 0, 0)
        one, two, twin = at.device(z, 1, 0), at.device(z, 0, 1), at.device(z, 0, 0, 1)
        self.routes = {"up": (0, up), "down": (1, down), "one": (2, one), "two": (3, two), "twin": (4, twin)}

    def greet(self):
        z = self.at.z
        conditions = {"up": z < LINE - 1, "down": z > 0}
        greet([(device, conditions.get(name)) for name, (_, device) in self.routes.items()])

    def copies(self, block, part, route, own=False):
        lane, device = self.routes[route]
        return [
            remote(part_of(self.ins[i] if own else self.outs[i].at[block], part), part_of(self.outs[i].at[block], part),
                   self.send.at[i, part, lane, block], self.recv.at[i, part, block], device)
            for i in range(self.count)
        ]

    def forward(self, block, part, *ways, own=False):
        for route in ways:
            for copy in self.copies(block, part, route, own):
                copy.start()

    def arrived(self, block, part):
        for copy in self.copies(block, part, "twin"):
            copy.wait_recv()

    def begin(self):
        z, mine = self.at.z, self.at.block(self.at.z, 0, 0)
        for part in range(PARTS):
            pl.when(z < LINE - 1)(functools.partial(self.forward, mine, part, "up", own=True))
            pl.when(z > 0)(functools.partial(self.forward, mine, part, "down", own=True))
            self.forward(mine, part, "one", "two", "twin", own=True)
        for way in (0, 1):
            moves = [
                pltpu.make_async_copy(self.ins[i], self.held[i], self.own_sem.at[i]) if way == 0
                else pltpu.make_async_copy(self.held[i], self.outs[i].at[mine], self.own_sem.at[i])
                for i in range(self.count)
            ]
            for move in moves:
                move.start()
            for move in moves:
                move.wait()

    def line(self, step, part):
        z = self.at.z

        @pl.when(z - step >= 0)
        def _():
            block = self.at.block(z - step, 0, 0)
            self.arrived(block, part)
            pl.when(z < LINE - 1)(functools.partial(self.forward, block, part, "up"))
            self.forward(block, part, "one", "two", "twin")

        @pl.when(z + step < LINE)
        def _():
            block = self.at.block(z + step, 0, 0)
            self.arrived(block, part)
            pl.when(z > 0)(functools.partial(self.forward, block, part, "down"))
            self.forward(block, part, "one", "two", "twin")

    def face(self, step, part, first, second):
        z = self.at.z
        ways = ("twin",) if second else ("two", "twin")

        def take(line):
            block = self.at.block(line, first, second)
            self.arrived(block, part)
            self.forward(block, part, *ways)
        if step == 0:
            take(z)
        else:
            pl.when(z - step >= 0)(functools.partial(take, z - step))
            pl.when(z + step < LINE)(functools.partial(take, z + step))

    def piece(self, kind, step, part):
        if kind == "line":
            self.line(step, part)
        elif kind == "faces":
            self.face(step, part, 1, 0)
            self.face(step, part, 0, 1)
        else:
            self.face(step, part, 1, 1)

    def from_twin(self, group):
        for y in (0, 1):
            for part in range(PARTS):
                self.arrived(group * 4 + y * 2 + 1 - self.at.core, part)

    def end(self):
        z = self.at.z

        def sent(block, part, *ways):
            for route in ways:
                for copy in self.copies(block, part, route):
                    copy.wait_send()

        for line in range(LINE):
            for part in range(PARTS):
                block = self.at.block(line, 0, 0)
                pl.when((z >= line) & (z < LINE - 1))(functools.partial(sent, block, part, "up"))
                pl.when((z <= line) & (z > 0))(functools.partial(sent, block, part, "down"))
                sent(block, part, "one", "two", "twin")
                sent(self.at.block(line, 1, 0), part, "two", "twin")
                sent(self.at.block(line, 0, 1), part, "twin")
                sent(self.at.block(line, 1, 1), part, "twin")


PARTS = 2


def part_of(ref, part):
    rows = ref.shape[0] // PARTS
    return ref.at[pl.ds(part * rows, rows)]


ORDER = (3, 0, 2, 1)


def scatter_kernel(count, *refs):
    ins, outs = refs[:count], refs[count:2 * count]
    rest = [refs[2 * count + k * count:2 * count + (k + 1) * count] for k in range(6)]
    acc, from_twin, from_two, from_one, from_below, from_above = rest
    load_sem, store_sem, send, recv = refs[8 * count:]
    at = Place()
    z = at.z
    up, down = at.device(z + 1, 0, 0), at.device(z - 1, 0, 0)
    one, two, twin = at.device(z, 1, 0), at.device(z, 0, 1), at.device(z, 0, 0, 1)
    greet([(one, None), (two, None), (twin, None), (up, z < LINE - 1), (down, z > 0)])
    units = [(line, part) for line in ORDER for part in range(PARTS)]
    corners = [(1, 1), (1, 0), (0, 1), (0, 0)]

    def slot(line, second, first):
        return second * 8 + first * 4 + line

    def load(i, part, line, second, first):
        here = slot(line, second, first)
        return pltpu.make_async_copy(part_of(ins[i].at[at.stored(line, first, second)], part),
                                     part_of(acc[i].at[here], part), load_sem.at[i, part, here])

    def hop(i, part, source, target, lane, device):
        return remote(part_of(source, part), part_of(target, part), send.at[i, part, lane], recv.at[i, part, lane], device)

    def to_twin(i, part, line, second, first):
        here = slot(line, second, first)
        return hop(i, part, ins[i].at[at.stored(line, first, second, 1)], from_twin[i].at[here], here, twin)

    def to_two(i, part, line, first):
        return hop(i, part, acc[i].at[slot(line, 1, first)], from_two[i].at[first * 4 + line], 16 + first * 4 + line, two)

    def to_one(i, part, line):
        return hop(i, part, acc[i].at[slot(line, 0, 1)], from_one[i].at[line], 24 + line, one)

    def rise(i, part, line):
        return hop(i, part, acc[i].at[line], from_below[i].at[line], 28 + line, up)

    def fall(i, part, line):
        return hop(i, part, acc[i].at[line], from_above[i].at[line], 32 + line, down)

    def begin(line, part):
        for second, first in corners:
            for i in range(count):
                to_twin(i, part, line, second, first).start()
                load(i, part, line, second, first).start()

    def gathered(line, part, second, first):
        for i in range(count):
            load(i, part, line, second, first).wait()
            to_twin(i, part, line, second, first).wait_recv()
            sources = [from_twin[i].at[slot(line, second, first)]]
            if not second:
                to_two(i, part, line, first).wait_recv()
                sources.append(from_two[i].at[first * 4 + line])
                if not first:
                    to_one(i, part, line).wait_recv()
                    sources.append(from_one[i].at[line])
            add_into(part_of(acc[i].at[slot(line, second, first)], part), *[part_of(r, part) for r in sources])
            if second:
                to_two(i, part, line, first).start()
            elif first:
                to_one(i, part, line).start()

    def line_hop(line, part, hops):
        @pl.when(z == hops)
        def _():
            for i in range(count):
                if 0 < hops <= line:
                    rise(i, part, line).wait_recv()
                    add_into(part_of(acc[i].at[line], part), part_of(from_below[i].at[line], part))
                if hops < line:
                    rise(i, part, line).start()

        @pl.when(z == LINE - 1 - hops)
        def _():
            for i in range(count):
                if 0 < hops <= LINE - 1 - line:
                    fall(i, part, line).wait_recv()
                    add_into(part_of(acc[i].at[line], part), part_of(from_above[i].at[line], part))
                if hops < LINE - 1 - line:
                    fall(i, part, line).start()

    begin(*units[0])
    begin(*units[1])
    for step in range(len(units) + 2 + LINE):
        if step + 2 < len(units):
            begin(*units[step + 2])
        if step < len(units):
            gathered(*units[step], 1, 1)
            gathered(*units[step], 1, 0)
        if 0 <= step - 1 < len(units):
            gathered(*units[step - 1], 0, 1)
        if 0 <= step - 2 < len(units):
            gathered(*units[step - 2], 0, 0)
        for hops in range(LINE):
            if 0 <= step - 2 - hops < len(units):
                line_hop(*units[step - 2 - hops], hops)
    stores = [pltpu.make_async_copy(acc[i].at[z], outs[i], store_sem.at[i]) for i in range(count)]
    for store in stores:
        store.start()
    for line, part in units:
        for i in range(count):
            for second, first in corners:
                to_twin(i, part, line, second, first).wait_send()
            to_two(i, part, line, 0).wait_send()
            to_two(i, part, line, 1).wait_send()
            to_one(i, part, line).wait_send()
            if line > 0:
                pl.when(z < line)(rise(i, part, line).wait_send)
            if line < LINE - 1:
                pl.when(z > line)(fall(i, part, line).wait_send)
    for store in stores:
        store.wait()


def scatter_blocks(collective_id, *arrays):
    count = len(arrays)

    def slots(n):
        return [pltpu.VMEM((n,) + a.shape[1:], a.dtype) for a in arrays]
    return pl.pallas_call(
        functools.partial(scatter_kernel, count),
        name=f"scatter_blocks_{collective_id}",
        out_shape=tuple(jax.ShapeDtypeStruct(a.shape[1:], a.dtype) for a in arrays),
        in_specs=[pl.BlockSpec(memory_space=pl.ANY)] * count,
        out_specs=tuple(pl.BlockSpec(memory_space=pl.ANY) for _ in arrays),
        scratch_shapes=slots(16) + slots(16) + slots(8) + slots(4) + slots(4) + slots(4)
        + [
            pltpu.SemaphoreType.DMA((count, PARTS, 16)),
            pltpu.SemaphoreType.DMA((count,)),
            pltpu.SemaphoreType.DMA((count, PARTS, 36)),
            pltpu.SemaphoreType.DMA((count, PARTS, 36)),
        ],
        compiler_params=pltpu.CompilerParams(
            collective_id=collective_id, has_side_effects=True, vmem_limit_bytes=60 << 20),
        cost_estimate=pl.CostEstimate(
            flops=0, transcendentals=0, bytes_accessed=sum(a.size * a.dtype.itemsize for a in arrays)),
    )(*arrays)


def sum_task(at, kind, rows, source, result, held, from_pair, from_below, from_above, load_sem, send, recv, delay, prepare=None):
    z, x = at.z, at.x
    pair = ((z * 2 + 1 - x), at.y * 2 + at.core)
    up, down = ((z + 1) * 2 + x, at.y * 2 + at.core), ((z - 1) * 2 + x, at.y * 2 + at.core)
    pair_first = kind == "pair"
    for _ in range(delay):
        yield

    def part(ref, line, face):
        return ref.at[line, face, rows]

    if pair_first:
        def load(line):
            return pltpu.make_async_copy(part(source, line, x), held.at[line], load_sem.at[line])

        def give(line):
            return remote(part(source, line, 1 - x), from_pair.at[line], send.at[0, line], recv.at[0, line], pair)
        for line in ORDER:
            give(line).start()
            load(line).start()
        yield
        yield
        for line in ORDER:
            load(line).wait()
            give(line).wait_recv()
            add_into(held.at[line], from_pair.at[line])
    else:
        def load(line):
            return pltpu.make_async_copy(source.at[line, :, rows], held.at[line], load_sem.at[line])
        for line in ORDER:
            load(line).start()
        for line in ORDER:
            load(line).wait()
        if prepare is not None:
            yield from prepare(held)

    def add(target, extra):
        if pair_first:
            add_into(target, extra)
        else:
            for face in (0, 1):
                add_into(target.at[face], extra.at[face])

    def rise(line):
        return remote(held.at[line], from_below.at[line], send.at[1, line], recv.at[1, line], up)

    def fall(line):
        return remote(held.at[line], from_above.at[line], send.at[2, line], recv.at[2, line], down)

    for line in range(LINE - 1, 0, -1):
        other = LINE - 1 - line

        @pl.when(z < line)
        def _():
            @pl.when(z > 0)
            def _():
                rise(line).wait_recv()
                add(held.at[line], from_below.at[line])
            rise(line).start()

        @pl.when(z > other)
        def _():
            @pl.when(z < LINE - 1)
            def _():
                fall(other).wait_recv()
                add(held.at[other], from_above.at[other])
            fall(other).start()
        yield

    @pl.when(z > 0)
    def _():
        rise(z).wait_recv()
        add(held.at[z], from_below.at[z])

    @pl.when(z < LINE - 1)
    def _():
        fall(z).wait_recv()
        add(held.at[z], from_above.at[z])

    if pair_first:
        def over(line):
            return remote(part(result, line, x), part(result, line, x), send.at[3, line], recv.at[3, line * 2 + x], pair)

        def other_over(line):
            return remote(part(result, line, 1 - x), part(result, line, 1 - x), send.at[3, line],
                          recv.at[3, line * 2 + 1 - x], pair)

        def climb(line):
            return remote(part(result, line, x), part(result, line, x), send.at[4, line], recv.at[3, line * 2 + x], up)

        def sink(line):
            return remote(part(result, line, x), part(result, line, x), send.at[5, line], recv.at[3, line * 2 + x], down)
        own = pltpu.make_async_copy(held.at[z], part(result, z, x), load_sem.at[4])
    else:
        mine = held.at[z]
        swap = remote(mine.at[1 - x], from_pair, send.at[0, 0], recv.at[0, 0], pair)
        swap.start()
        yield
        swap.wait_recv()
        add_into(mine.at[x], from_pair)
        own = pltpu.make_async_copy(mine.at[x], part(result, z, x), load_sem.at[4])

        def over_block(face):
            return remote(part(result, z, face), part(result, z, face), send.at[3, 0], recv.at[3, face], pair)

        def climb(line):
            return remote(result.at[line, :, rows], result.at[line, :, rows], send.at[4, line], recv.at[3, 4 + line], up)

        def sink(line):
            return remote(result.at[line, :, rows], result.at[line, :, rows], send.at[5, line], recv.at[3, 4 + line], down)
    own.start()
    own.wait()
    if pair_first:
        over(z).start()
    else:
        over_block(x).start()
        yield
        over_block(1 - x).wait_recv()

    @pl.when(z < LINE - 1)
    def _():
        climb(z).start()

    @pl.when(z > 0)
    def _():
        sink(z).start()
    yield
    for step in range(1, LINE):
        @pl.when(z - step >= 0)
        def _():
            climb(z - step).wait_recv()

            @pl.when(z < LINE - 1)
            def _():
                climb(z - step).start()
            if pair_first:
                over(z - step).start()

        @pl.when(z + step < LINE)
        def _():
            sink(z + step).wait_recv()

            @pl.when(z > 0)
            def _():
                sink(z + step).start()
            if pair_first:
                over(z + step).start()
        yield
    if pair_first:
        for line in range(LINE):
            other_over(line).wait_recv()
    for line in range(LINE):
        if pair_first:
            give(line).wait_send()
            over(line).wait_send()
        if line > 0:
            pl.when(z < line)(rise(line).wait_send)
        if line < LINE - 1:
            pl.when(z > line)(fall(line).wait_send)
        pl.when((z >= line) & (z < LINE - 1))(climb(line).wait_send)
        pl.when((z <= line) & (z > 0))(sink(line).wait_send)
    if not pair_first:
        swap.wait_send()
        over_block(x).wait_send()


def narrow_sum_task(at, source, result, mine, from_twin, from_peer, load_sem, send, recv):
    twin, peer = at.device(at.z, 0, 0, 1), at.across()

    def give(y):
        return remote(source.at[y * 2 + 1 - at.core], from_twin.at[y], send.at[y], recv.at[y], twin)

    def load(y):
        return pltpu.make_async_copy(source.at[y * 2 + at.core], mine.at[y], load_sem.at[y])
    order = (1 - at.y, at.y)
    for y in order:
        give(y).start()
        load(y).start()
    other, own = order
    over = remote(mine.at[other], from_peer, send.at[2], recv.at[2], peer)
    for y in order:
        load(y).wait()
        give(y).wait_recv()
        add_into(mine.at[y], from_twin.at[y])
        if y is other:
            over.start()
    yield
    over.wait_recv()
    add_into(mine.at[own], from_peer)
    store = pltpu.make_async_copy(mine.at[own], result, load_sem.at[2])
    store.start()
    yield
    store.wait()
    over.wait_send()
    for y in order:
        give(y).wait_send()


def narrow_sum_scratch(block, dtype):
    return [
        pltpu.VMEM((2,) + block, dtype),
        pltpu.VMEM((2,) + block, dtype),
        pltpu.VMEM(block, dtype),
        pltpu.SemaphoreType.DMA((3,)),
        pltpu.SemaphoreType.DMA((3,)),
        pltpu.SemaphoreType.DMA((3,)),
    ]


def run_tasks(tasks):
    while tasks:
        tasks = [task for task in tasks if next(task, tasks) is not tasks]


def narrow_sum_kernel(source, result, *scratch):
    at = Place()
    greet([(at.device(at.z, 0, 0, 1), None), (at.across(), None)])
    run_tasks([narrow_sum_task(at, source, result, *scratch)])


def narrow_sum(collective_id, parts):
    block = parts.shape[1:]
    return pl.pallas_call(
        narrow_sum_kernel,
        name=f"narrow_sum_{collective_id}",
        out_shape=jax.ShapeDtypeStruct(block, parts.dtype),
        in_specs=[pl.BlockSpec(memory_space=pl.ANY)],
        out_specs=pl.BlockSpec(memory_space=pl.ANY),
        scratch_shapes=narrow_sum_scratch(block, parts.dtype),
        compiler_params=pltpu.CompilerParams(collective_id=collective_id, has_side_effects=True),
    )(parts)


def narrow_gather_kernel(block, result, held, load_sem, send, recv):
    at = Place()
    twin, peer = at.device(at.z, 0, 0, 1), at.across()
    greet([(twin, None), (peer, None)])
    here, there = at.y * 2 + at.core, (1 - at.y) * 2 + at.core
    load = pltpu.make_async_copy(block, held, load_sem.at[0])
    load.start()
    over = remote(block, result.at[here], send.at[0], recv.at[here], peer)
    beside = remote(block, result.at[here], send.at[1], recv.at[here], twin)
    over.start()
    beside.start()
    load.wait()
    store = pltpu.make_async_copy(held, result.at[here], load_sem.at[1])
    store.start()
    passed = remote(result.at[there], result.at[there], send.at[2], recv.at[there], twin)
    passed.wait_recv()
    passed.start()
    for y in (0, 1):
        remote(block, result.at[y * 2 + 1 - at.core], send.at[1], recv.at[y * 2 + 1 - at.core], twin).wait_recv()
    for copy in (over, beside, passed):
        copy.wait_send()
    store.wait()


def narrow_gather(collective_id, block):
    return pl.pallas_call(
        narrow_gather_kernel,
        name=f"narrow_gather_{collective_id}",
        out_shape=jax.ShapeDtypeStruct((4,) + block.shape, block.dtype),
        in_specs=[pl.BlockSpec(memory_space=pl.ANY)],
        out_specs=pl.BlockSpec(memory_space=pl.ANY),
        scratch_shapes=[
            pltpu.VMEM(block.shape, block.dtype),
            pltpu.SemaphoreType.DMA((2,)),
            pltpu.SemaphoreType.DMA((3,)),
            pltpu.SemaphoreType.DMA((4,)),
        ],
        compiler_params=pltpu.CompilerParams(collective_id=collective_id, has_side_effects=True),
    )(block)


def narrow_total_kernel(values, result, others, send, recv):
    at = Place()
    places = [at.device(at.z, 0, 0, 1), at.across(), at.across(1)]
    greet([(place, None) for place in places])
    copies = [remote(values, others.at[i], send.at[i], recv.at[i], place) for i, place in enumerate(places)]
    for copy in copies:
        copy.start()
    for copy in copies:
        copy.wait()
    result[...] = (values[...] + others[0]) + (others[1] + others[2])


def narrow_total(collective_id, values):
    return pl.pallas_call(
        narrow_total_kernel,
        name=f"narrow_total_{collective_id}",
        out_shape=jax.ShapeDtypeStruct(values.shape, values.dtype),
        in_specs=[pl.BlockSpec(memory_space=pltpu.VMEM)],
        out_specs=pl.BlockSpec(memory_space=pltpu.VMEM),
        scratch_shapes=[
            pltpu.VMEM((3,) + values.shape, values.dtype),
            pltpu.SemaphoreType.DMA((3,)),
            pltpu.SemaphoreType.DMA((3,)),
        ],
        compiler_params=pltpu.CompilerParams(collective_id=collective_id, has_side_effects=True),
    )(values)


def final_sums_kernel(plan, count, *refs):
    ins, outs, rest = refs[:count], refs[count:2 * count], list(refs[2 * count:])
    at = Place()
    pair = (at.z * 2 + 1 - at.x, at.y * 2 + at.core)
    up, down = ((at.z + 1) * 2 + at.x, at.y * 2 + at.core), ((at.z - 1) * 2 + at.x, at.y * 2 + at.core)
    twin, peer = at.device(at.z, 0, 0, 1), at.across()
    greet([(pair, None), (twin, None), (peer, None), (up, at.z < LINE - 1), (down, at.z > 0)])
    narrow_scratch, rest = rest[-6:], rest[:-6]
    load_sem, send, recv, others, other_send, other_recv = rest[-6:]

    def over_narrow(held):
        beside = remote(ins[count - 2], others.at[0], other_send.at[0], other_recv.at[0], twin)
        beside.start()
        yield
        beside.wait_recv()
        for line in range(LINE):
            for face in (0, 1):
                add_into(held.at[line, face], others.at[0, line, face])
        across = remote(held, others.at[1], other_send.at[1], other_recv.at[1], peer)
        across.start()
        yield
        across.wait()
        beside.wait_send()
        for line in range(LINE):
            for face in (0, 1):
                add_into(held.at[line, face], others.at[1, line, face])
    tasks = [narrow_sum_task(at, ins[-1], outs[-1], *narrow_scratch)]
    for number, (which, begin, rows, kind, delay) in enumerate(plan):
        held, from_pair, from_below, from_above = rest[4 * number:4 * number + 4]
        tasks.append(sum_task(at, kind, pl.ds(begin, rows), ins[which], outs[which], held, from_pair, from_below,
                              from_above, load_sem.at[number], send.at[number], recv.at[number], delay,
                              over_narrow if which == count - 2 else None))
    run_tasks(tasks)


def final_sums(collective_id, plan, *arrays):
    count, steps = len(arrays), len(plan)
    scratch = []
    for which, _, rows, kind, _ in plan:
        columns, dtype = arrays[which].shape[3], arrays[which].dtype
        block = (() if kind == "pair" else (2,)) + (rows, columns)
        scratch += [
            pltpu.VMEM((LINE,) + block, dtype),
            pltpu.VMEM(((LINE,) if kind == "pair" else ()) + (rows, columns), dtype),
            pltpu.VMEM((LINE,) + block, dtype),
            pltpu.VMEM((LINE,) + block, dtype),
        ]
    small, parts = arrays[-2:]
    moved = sum(a.size * a.dtype.itemsize for a in arrays)
    return pl.pallas_call(
        functools.partial(final_sums_kernel, plan, count),
        name=f"final_sums_{collective_id}",
        out_shape=tuple(jax.ShapeDtypeStruct(a.shape, a.dtype) for a in arrays[:-1])
        + (jax.ShapeDtypeStruct(parts.shape[1:], parts.dtype),),
        in_specs=[pl.BlockSpec(memory_space=pl.ANY)] * count,
        out_specs=tuple(pl.BlockSpec(memory_space=pl.ANY) for _ in arrays),
        scratch_shapes=scratch + [
            pltpu.SemaphoreType.DMA((steps, 5)),
            pltpu.SemaphoreType.DMA((steps, 6, 4)),
            pltpu.SemaphoreType.DMA((steps, 4, 8)),
            pltpu.VMEM((2,) + small.shape, small.dtype),
            pltpu.SemaphoreType.DMA((2,)),
            pltpu.SemaphoreType.DMA((2,)),
        ] + narrow_sum_scratch(parts.shape[1:], parts.dtype),
        compiler_params=pltpu.CompilerParams(
            collective_id=collective_id, has_side_effects=True, vmem_limit_bytes=48 << 20),
        cost_estimate=pl.CostEstimate(flops=0, transcendentals=0, bytes_accessed=2 * moved),
    )(*arrays)


def own_exchange():
    return lax.axis_size("wide") == 8 and lax.axis_size("narrow") == 4


def scatter_all(*arrays):
    if own_exchange():
        return scatter_blocks(2, *arrays)
    return tuple(lax.psum_scatter(a, BOTH, scatter_dimension=0) for a in arrays)


FINAL_PLAN = (
    (4, 0, 72, "line", 0),
    (0, 0, 128, "pair", 0),
    (3, 0, 64, "line", 0),
    (0, 128, 128, "pair", 1),
    (1, 0, 128, "pair", 2),
    (1, 128, 128, "pair", 3),
    (2, 0, 128, "pair", 4),
    (2, 128, 128, "pair", 5),
)


def total_weights(weights, gains, everywhere, parts):
    if not own_exchange():
        totals = tuple(a.astype(jnp.float32) for a in lax.psum(tuple(a.astype(jnp.bfloat16) for a in weights), "wide"))
        own = lax.psum_scatter(parts, "narrow", scatter_dimension=0, tiled=True)
        return totals, lax.psum(gains, "wide"), lax.psum(everywhere, BOTH), own
    gain_rows = jnp.concatenate([a.reshape(-1, 128) for a in gains], axis=0)
    mine = lax.axis_index("narrow")
    gain_slots = lax.dynamic_update_slice_in_dim(jnp.zeros((4,) + gain_rows.shape, jnp.float32), gain_rows[None], mine, 0)
    pieces = [a.reshape(-1, 128) for a in everywhere] + [gain_slots.reshape(-1, 128)]
    small = jnp.concatenate(pieces, axis=0)
    arrays = [a.astype(jnp.bfloat16).reshape(LINE, 2, a.shape[0] // 8, a.shape[1]) for a in weights]
    results = final_sums(
        3, FINAL_PLAN, *arrays, small.reshape(LINE, 2, small.shape[0] // 8, 128), parts.reshape(4, -1, parts.shape[1])
    )
    totals = tuple(r.reshape(a.shape).astype(jnp.float32) for r, a in zip(results, weights))
    small_total = results[-2].reshape(small.shape)
    summed, begin = [], 0
    for array, piece in zip(everywhere, pieces):
        summed.append(small_total[begin:begin + piece.shape[0]].reshape(array.shape))
        begin += piece.shape[0]
    own_gains = lax.dynamic_slice_in_dim(small_total[begin:].reshape(gain_slots.shape), mine, 1, 0).reshape(len(gains), -1)
    return totals, tuple(own_gains[i].reshape(g.shape) for i, g in enumerate(gains)), tuple(summed), results[-1]


def narrow_sums(collective_id, values):
    if not own_exchange():
        return lax.psum(values, "narrow")
    total = narrow_total(collective_id, jnp.stack(values).reshape(-1, 128)).reshape(len(values), -1)
    return tuple(total[i] for i in range(len(values)))


def narrow_deal(collective_id, parts):
    if not own_exchange():
        return lax.psum_scatter(parts, "narrow", scatter_dimension=0, tiled=True)
    return narrow_sum(collective_id, parts.reshape(4, -1, parts.shape[1]))


def narrow_all(collective_id, block):
    if not own_exchange():
        return lax.all_gather(block, "narrow", axis=0, tiled=True)
    return narrow_gather(collective_id, block).reshape(-1, block.shape[1])


def experts_plain(rows_all, grads_all, places_here, probs_here, gate_weight, up_weight, down_weight, capacity):
    block_count, own_rows, model_width = rows_all.shape
    experts_here = gate_weight.shape[0]
    highest_precision = lax.Precision.HIGHEST
    pick = places_here[:, :, None, :] == jnp.arange(capacity, dtype=jnp.float32)[None, None, :, None]
    pick_low = pick.astype(jnp.bfloat16)
    slot_gate = jnp.sum(jnp.where(pick, probs_here[:, :, None, :], 0.0), axis=-1)
    slot_gate = slot_gate.transpose(1, 0, 2).reshape(experts_here, block_count * capacity, 1)

    def spread(rows):
        out = jnp.einsum("best,btd->ebsd", pick_low, rows, preferred_element_type=jnp.float32)
        return out.astype(jnp.bfloat16).reshape(experts_here, block_count * capacity, model_width)

    def collect(slots):
        out = jnp.einsum(
            "best,ebsd->btd",
            pick_low,
            slots.reshape(experts_here, block_count, capacity, model_width),
            preferred_element_type=jnp.float32,
        )
        return out.astype(jnp.bfloat16)

    slot_rows = spread(rows_all)
    slot_grads = spread(grads_all)
    gate_pre = jnp.einsum("erd,edf->erf", slot_rows, gate_weight, preferred_element_type=jnp.float32)
    up_pre = jnp.einsum("erd,edf->erf", slot_rows, up_weight, preferred_element_type=jnp.float32)
    activated, unit_back = jax.vjp(gated_unit, gate_pre, up_pre)
    gated_act = (activated * slot_gate).astype(jnp.bfloat16)
    raw_act_grad = jnp.einsum("erd,efd->erf", slot_grads, down_weight, preferred_element_type=jnp.float32)
    slot_gate_grads = jnp.sum(activated * raw_act_grad, axis=-1)
    gate_grad_full, up_grad_full = unit_back(raw_act_grad * slot_gate)
    gate_grad_low = gate_grad_full.astype(jnp.bfloat16)
    up_grad_low = up_grad_full.astype(jnp.bfloat16)
    gate_grad_parts = jnp.einsum(
        "best,ebs->bet",
        pick.astype(jnp.float32),
        slot_gate_grads.reshape(experts_here, block_count, capacity),
        precision=highest_precision,
    )
    back_slots = jnp.einsum(
        "erf,edf->erd", gate_grad_low, gate_weight, preferred_element_type=jnp.float32
    ) + jnp.einsum("erf,edf->erd", up_grad_low, up_weight, preferred_element_type=jnp.float32)
    out_slots = jnp.einsum("erf,efd->erd", gated_act, down_weight, preferred_element_type=jnp.float32)
    return (
        collect(out_slots.astype(jnp.bfloat16)),
        collect(back_slots.astype(jnp.bfloat16)),
        gate_grad_parts,
        jnp.einsum("erd,erf->edf", slot_rows, gate_grad_low, preferred_element_type=jnp.float32),
        jnp.einsum("erd,erf->edf", slot_rows, up_grad_low, preferred_element_type=jnp.float32),
        jnp.einsum("erf,erd->efd", gated_act, slot_grads, preferred_element_type=jnp.float32),
    )


STEP_BLOCKS = 4
GATHER_PLAN = (
    (-1, 1, "faces", 0, 0),
    (-1, 1, "faces", 0, 1),
    (-1, 1, "line", 1, 1),
    (-1, 1, "line", 1, 0),
    (0, 0, "corner", 0, 0),
    (0, 0, "corner", 0, 1),
    (1, 1, "faces", 1, 0),
    (1, 1, "faces", 1, 1),
    (2, 1, "corner", 1, 0),
    (2, 3, "line", 2, 0),
    (2, 3, "line", 2, 1),
    (2, 3, "corner", 1, 1),
    (3, 4, "faces", 2, 0),
    (3, 4, "faces", 2, 1),
    (4, 0, "corner", 2, 0),
    (4, 2, "corner", 2, 1),
    (4, 3, "line", 3, 0),
    (4, 4, "line", 3, 1),
    (5, 0, "faces", 3, 0),
    (5, 0, "faces", 3, 1),
    (6, 1, "corner", 3, 0),
    (6, 1, "corner", 3, 1),
)


def dot(left, right, left_dim=1, right_dim=0):
    return lax.dot_general(
        left, right, (((left_dim,), (right_dim,)), ((), ())), preferred_element_type=jnp.float32
    )


def experts_kernel(
    capacity, rows_own, grads_own, routes_own, gate_w, up_w, down_w,
    rows_all, grads_all, routes_all, out, back, gate_grads, gate_dw, up_dw, down_dw,
    row_slots, grad_slots, rows_held, grads_held, routes_held, load_sem, send, recv, own_sem,
):
    experts = gate_w.shape[0]
    tokens = rows_own.shape[0]
    everywhere = routes_own.shape[0] // 2
    turn = pl.program_id(0)
    turns = LINE * 2
    at = Place()
    first_expert = lax.axis_index("wide") * experts
    gathered, held = (rows_all, grads_all, routes_all), (rows_held, grads_held, routes_held)
    gather = Gather(at, (rows_own, grads_own, routes_own), gathered, [h.at[1, 0] for h in held], send, recv, own_sem)
    slot_ids = lax.broadcasted_iota(jnp.int32, (capacity, tokens), 0).astype(jnp.float32)

    def loads(number):
        group = at.group(number)
        slot = lax.rem(number, 2)
        return [
            pltpu.make_async_copy(gathered[i].at[pl.ds(group * STEP_BLOCKS, STEP_BLOCKS)], held[i].at[slot],
                                  load_sem.at[i, slot])
            for i in range(3)
        ]

    def fetch(number):
        gather.from_twin(at.group(number))
        for load in loads(number):
            load.start()

    def issue(place, expert=None):
        for number in sorted({entry[0] for entry in GATHER_PLAN}):
            work = [entry[2:] for entry in GATHER_PLAN if entry[:2] == (number, place)]
            if work:
                @pl.when(turn == number if expert is None else (turn == number) & (expert == place - 1))
                def _():
                    for piece in work:
                        gather.piece(*piece)

    @pl.when(turn == 0)
    def _():
        gather.greet()
        gather.begin()
        for target in (gate_dw, up_dw, down_dw):
            @pl.loop(0, experts)
            def _(e):
                target[e] = jnp.zeros(target.shape[1:], jnp.float32)
        for entry in GATHER_PLAN:
            if entry[0] < 0:
                gather.piece(*entry[2:])
        fetch(jnp.int32(0))

    for load in loads(turn):
        load.wait()
    slot = lax.rem(turn, 2)
    rows, grads, routes = rows_held.at[slot], grads_held.at[slot], routes_held.at[slot]

    def pick_of(block, expert):
        return routes[block, pl.ds(everywhere + first_expert + expert, 1), :] == slot_ids

    def picks(block):
        return jnp.concatenate(
            [pick_of(block, e).astype(jnp.float32) for e in range(experts)], axis=0
        ).astype(jnp.bfloat16)

    for block in range(STEP_BLOCKS):
        pick = picks(block)
        part = pl.ds(block * capacity, capacity)
        for source, target in ((rows, row_slots), (grads, grad_slots)):
            slots = dot(pick, source[block]).astype(jnp.bfloat16)
            for e in range(experts):
                target[e, part] = slots[e * capacity:(e + 1) * capacity]

    issue(0)

    @pl.loop(0, experts)
    def _(e):
        gate_pre, up_pre = dot(row_slots[e], gate_w[e]), dot(row_slots[e], up_w[e])
        raw = dot(grad_slots[e], down_w[e], 1, 1)
        slot_gate = jnp.concatenate([
            jnp.sum(jnp.where(pick_of(block, e), routes[block, pl.ds(first_expert + e, 1), :], 0.0),
                    axis=1, keepdims=True)
            for block in range(STEP_BLOCKS)
        ], axis=0)
        sigma = 1.0 / (1.0 + jnp.exp(-gate_pre))
        silu = gate_pre * sigma
        act = silu * up_pre
        slot_sum = jnp.sum(act * raw, axis=1, keepdims=True)
        for block in range(STEP_BLOCKS):
            gate_grads[block, pl.ds(e, 1), :] = jnp.sum(
                jnp.where(pick_of(block, e), slot_sum[block * capacity:(block + 1) * capacity], 0.0),
                axis=0, keepdims=True,
            )
        gated = (act * slot_gate).astype(jnp.bfloat16)
        act_grad = raw * slot_gate
        gate_low = (act_grad * up_pre * sigma * (1.0 + gate_pre * (1.0 - sigma))).astype(jnp.bfloat16)
        up_low = (act_grad * silu).astype(jnp.bfloat16)
        down_dw[e] += dot(gated, grad_slots[e], 0, 0)
        grad_slots[e] = dot(gated, down_w[e]).astype(jnp.bfloat16)
        turned = row_slots[e].T
        gate_dw[e] += dot(turned, gate_low)
        up_dw[e] += dot(turned, up_low)
        row_slots[e] = (dot(gate_low, gate_w[e], 1, 1) + dot(up_low, up_w[e], 1, 1)).astype(jnp.bfloat16)
        for place in range(1, 5):
            issue(place, e)

    @pl.when(turn < turns - 1)
    def _():
        fetch(turn + 1)

    for block in range(STEP_BLOCKS):
        pick = picks(block)
        part = pl.ds(block * capacity, capacity)
        for source, target in ((row_slots, back), (grad_slots, out)):
            slots = jnp.concatenate([source[e, part] for e in range(experts)], axis=0)
            target[block] = dot(pick, slots, 0, 0).astype(jnp.bfloat16)

    issue(5)
    pl.when(turn == turns - 1)(gather.end)


def gather_experts(collective_id, rows, grads, routes, gate_weight, up_weight, down_weight, capacity):
    own_rows, width = rows.shape
    experts, _, hidden = gate_weight.shape
    block_count = LINE * 2 * STEP_BLOCKS
    step_rows = STEP_BLOCKS * capacity

    def stepped(*shape):
        return pl.BlockSpec((STEP_BLOCKS,) + shape, lambda i: (i,) + (0,) * len(shape))

    def whole(array):
        return pl.BlockSpec(array.shape, lambda i: (0,) * array.ndim, pipeline_mode=pl.Buffered(1))
    weights, owns = (gate_weight, up_weight, down_weight), (rows, grads, routes)
    flops = 2 * block_count * experts * (9 * capacity * width * hidden + 4 * capacity * own_rows * width)
    shapes = jax.ShapeDtypeStruct
    results = pl.pallas_call(
        functools.partial(experts_kernel, capacity),
        name="gather_experts",
        grid=(block_count // STEP_BLOCKS,),
        out_shape=tuple(shapes((block_count,) + a.shape, a.dtype) for a in owns)
        + (
            shapes((block_count, own_rows, width), jnp.bfloat16),
            shapes((block_count, own_rows, width), jnp.bfloat16),
            shapes((block_count, experts, own_rows), jnp.float32),
        ) + tuple(shapes(w.shape, jnp.float32) for w in weights),
        in_specs=[pl.BlockSpec(memory_space=pl.ANY)] * 3 + [whole(w) for w in weights],
        out_specs=(pl.BlockSpec(memory_space=pl.ANY),) * 3
        + (stepped(own_rows, width), stepped(own_rows, width), stepped(experts, own_rows))
        + tuple(whole(w) for w in weights),
        scratch_shapes=[
            pltpu.VMEM((experts, step_rows, width), jnp.bfloat16),
            pltpu.VMEM((experts, step_rows, width), jnp.bfloat16),
        ] + [pltpu.VMEM((2, STEP_BLOCKS) + a.shape, a.dtype) for a in owns] + [
            pltpu.SemaphoreType.DMA((3, 2)),
            pltpu.SemaphoreType.DMA((3, PARTS, 5, block_count)),
            pltpu.SemaphoreType.DMA((3, PARTS, block_count)),
            pltpu.SemaphoreType.DMA((3,)),
        ],
        compiler_params=pltpu.CompilerParams(
            collective_id=collective_id, has_side_effects=True,
            dimension_semantics=("arbitrary",), vmem_limit_bytes=67_000_000),
        cost_estimate=pl.CostEstimate(
            flops=flops, transcendentals=0,
            bytes_accessed=8 * block_count * rows.size + sum(6 * w.size for w in weights)),
    )(*owns, *weights)
    return results[3:]


def local(
    block_input,
    attn_gain,
    query_weight,
    key_weight,
    value_weight,
    query_gain,
    key_gain,
    out_weight,
    moe_gain,
    router_weight,
    gate_weight,
    up_weight,
    down_weight,
    segment_ids,
    expert_ids,
    out_cotangent,
):
    group_rows, model_width = block_input.shape
    own_rows = out_cotangent.shape[0]
    local_width = query_weight.shape[1]
    head_size = HEAD_DIM
    local_heads = local_width // head_size
    wide_size = lax.axis_size("wide")
    experts_all = router_weight.shape[1]
    experts_here = gate_weight.shape[0]
    choose_count = expert_ids.shape[1]
    capacity = 3 * own_rows * choose_count // (2 * experts_all)
    row_begin = lax.axis_index("narrow") * own_rows
    blocks = group_rows // QBLK
    highest_precision = lax.Precision.HIGHEST
    block_count = wide_size * lax.axis_size("narrow")
    chosen = (expert_ids[:, :, None] == jnp.arange(experts_all)[None, None, :]).any(axis=1)
    token_order = jnp.arange(own_rows)
    earlier = jnp.dot(
        (token_order[:, None] > token_order[None, :]).astype(jnp.bfloat16),
        chosen.astype(jnp.bfloat16),
        preferred_element_type=jnp.float32,
    )
    inputs_all = block_input.astype(jnp.float32)
    normed_one = rms_scale(inputs_all, attn_gain.astype(jnp.float32)).astype(jnp.bfloat16)
    joined_weight = jnp.concatenate([query_weight, key_weight, value_weight], axis=1)
    projected = jnp.dot(normed_one, joined_weight, preferred_element_type=jnp.float32)
    query_proj = projected[:, :local_width]
    key_proj = projected[:, local_width : 2 * local_width]
    value_proj = projected[:, 2 * local_width :]
    rope_cos, rope_sin = rope_tables(group_rows, head_size)
    query_total, key_total = narrow_sums(
        4, (jnp.sum(query_proj * query_proj, axis=1), jnp.sum(key_proj * key_proj, axis=1))
    )
    query_inverse = lax.rsqrt(query_total / model_width + norm_epsilon)[:, None]
    key_inverse = lax.rsqrt(key_total / model_width + norm_epsilon)[:, None]
    query_scale = query_gain.astype(jnp.float32)
    key_scale = key_gain.astype(jnp.float32)
    query_normed = query_proj * query_inverse * query_scale
    key_normed = key_proj * key_inverse * key_scale

    def turn_both(query_in, key_in):
        return (
            rotate(query_in, rope_cos, rope_sin, head_size) * head_size ** (-0.5),
            rotate(key_in, rope_cos, rope_sin, head_size),
        )

    (turned_query, turned_key), turn_back = jax.vjp(turn_both, query_normed, key_normed)
    query_heads = turned_query.astype(jnp.bfloat16).reshape(group_rows, local_heads, head_size)
    key_heads = turned_key.astype(jnp.bfloat16).reshape(group_rows, local_heads, head_size)
    value_heads = value_proj.astype(jnp.bfloat16).reshape(group_rows, local_heads, head_size)
    positions = jnp.arange(group_rows)

    def block_scores(block_index):
        block_begin = block_index * QBLK
        query_block = lax.dynamic_slice_in_dim(query_heads, block_begin, QBLK, 0)
        query_segments = lax.dynamic_slice_in_dim(segment_ids, block_begin, QBLK, 0)
        query_places = block_begin + jnp.arange(QBLK)
        allowed = (query_segments[:, None] == segment_ids[None, :]) & (
            query_places[:, None] >= positions[None, :]
        )
        scores = jnp.einsum(
            "qhd,khd->hqk", query_block, key_heads, preferred_element_type=jnp.float32
        )
        return (query_block, jnp.where(allowed[None], scores, masked_score))

    def attend(block_index):
        query_block, scores = block_scores(block_index)
        highest = jnp.max(scores, axis=-1, keepdims=True)
        weights = jnp.exp(scores - highest)
        totals = jnp.sum(weights, axis=-1, keepdims=True)
        probs_low = (weights / totals).astype(jnp.bfloat16)
        mixed_rows = jnp.einsum(
            "hqk,khd->qhd", probs_low, value_heads, preferred_element_type=jnp.float32
        )
        return (mixed_rows, highest + jnp.log(totals))

    mixed_blocks, log_totals = lax.map(attend, jnp.arange(blocks))
    heads_out = mixed_blocks.reshape(group_rows, local_width).astype(jnp.bfloat16)
    attn_own = narrow_deal(
        6, jnp.dot(heads_out, out_weight, preferred_element_type=jnp.float32).astype(jnp.bfloat16)
    ).astype(jnp.float32)
    input_own = lax.dynamic_slice_in_dim(inputs_all, row_begin, own_rows, 0)
    hidden = input_own + attn_own
    normed_two_full, norm_two_back = jax.vjp(rms_scale, hidden, moe_gain.astype(jnp.float32))
    normed_two = normed_two_full.astype(jnp.bfloat16)
    logits = jnp.dot(normed_two, router_weight, preferred_element_type=jnp.float32)
    route_probs = jax.nn.softmax(logits, axis=-1)
    routes = jnp.concatenate([route_probs.T, jnp.where(chosen, earlier, -1.0).T], axis=0)
    expert_begin = lax.axis_index("wide") * experts_here
    expert_weights = (gate_weight, up_weight, down_weight)
    if own_exchange():
        results = gather_experts(1, normed_two, out_cotangent, routes, *expert_weights, capacity)
    else:
        rows_all, grads_all, routes_all = (lax.all_gather(a, BOTH, axis=0) for a in (normed_two, out_cotangent, routes))
        probs_here = lax.dynamic_slice_in_dim(routes_all, expert_begin, experts_here, 1)
        places_here = lax.dynamic_slice_in_dim(routes_all, experts_all + expert_begin, experts_here, 1)
        results = experts_plain(rows_all, grads_all, places_here, probs_here, *expert_weights, capacity)
    out_parts, back_parts, gate_grad_parts, gate_weight_grad, up_weight_grad, down_weight_grad = results
    gate_grad_wide = lax.dynamic_update_slice_in_dim(
        jnp.zeros((block_count, experts_all, own_rows), jnp.float32), gate_grad_parts, expert_begin, 1
    )
    rows_back, prob_grads, moe_out = scatter_all(
        back_parts, gate_grad_wide, out_parts
    )
    rows_back, prob_grads, moe_out = rows_back.astype(jnp.float32), prob_grads.T, moe_out.astype(jnp.float32)
    block_output = (hidden + moe_out).astype(jnp.bfloat16)
    logit_grads = route_probs * (
        prob_grads - jnp.sum(route_probs * prob_grads, axis=-1, keepdims=True)
    )
    router_part = lax.dot_general(
        normed_two.astype(jnp.float32),
        logit_grads,
        (((0,), (0,)), ((), ())),
        precision=highest_precision,
    )
    router_back = lax.dot_general(
        logit_grads,
        router_weight.astype(jnp.float32),
        (((1,), (1,)), ((), ())),
        precision=highest_precision,
    )
    normed_two_grad = rows_back + router_back
    cotangent_full = out_cotangent.astype(jnp.float32)
    hidden_path, moe_gain_part = norm_two_back(normed_two_grad)
    hidden_grad = cotangent_full + hidden_path
    hidden_grad_low = hidden_grad.astype(jnp.bfloat16)
    gathered_piece = narrow_all(7, hidden_grad_low)
    heads_grad_acc = contract_last(gathered_piece, out_weight)
    out_weight_acc = contract_rows(heads_out, gathered_piece)
    heads_grad_low = heads_grad_acc.astype(jnp.bfloat16).reshape(group_rows, local_heads, head_size)

    def back_block(running, items):
        key_acc, value_acc = running
        block_index, log_total = items
        query_block, scores = block_scores(block_index)
        probs = jnp.exp(scores - log_total)
        probs_low = probs.astype(jnp.bfloat16)
        grad_block = lax.dynamic_slice_in_dim(heads_grad_low, block_index * QBLK, QBLK, 0)
        weight_grads = jnp.einsum(
            "qhd,khd->hqk", grad_block, value_heads, preferred_element_type=jnp.float32
        )
        row_dots = jnp.sum(probs * weight_grads, axis=-1, keepdims=True)
        score_grads = (probs * (weight_grads - row_dots)).astype(jnp.bfloat16)
        query_grad_block = jnp.einsum(
            "hqk,khd->qhd", score_grads, key_heads, preferred_element_type=jnp.float32
        )
        key_acc = key_acc + jnp.einsum(
            "hqk,qhd->khd", score_grads, query_block, preferred_element_type=jnp.float32
        )
        value_acc = value_acc + jnp.einsum(
            "hqk,qhd->khd", probs_low, grad_block, preferred_element_type=jnp.float32
        )
        return ((key_acc, value_acc), query_grad_block)

    zero_heads = jnp.zeros((group_rows, local_heads, head_size), jnp.float32)
    (key_grad, value_grad), query_grads = lax.scan(
        back_block, (zero_heads, zero_heads), (jnp.arange(blocks), log_totals)
    )
    query_normed_grad, key_normed_grad = turn_back(
        (query_grads.reshape(group_rows, local_width), key_grad.reshape(group_rows, local_width))
    )
    query_gain_part = jnp.sum(query_normed_grad * query_proj * query_inverse, axis=0)
    key_gain_part = jnp.sum(key_normed_grad * key_proj * key_inverse, axis=0)
    query_gained = query_normed_grad * query_scale
    key_gained = key_normed_grad * key_scale
    query_dot, key_dot = narrow_sums(
        5, (jnp.sum(query_proj * query_gained, axis=1), jnp.sum(key_proj * key_gained, axis=1))
    )
    query_proj_grad = (
        query_inverse * query_gained
        - query_proj * query_inverse**3 * (query_dot / model_width)[:, None]
    )
    key_proj_grad = (
        key_inverse * key_gained - key_proj * key_inverse**3 * (key_dot / model_width)[:, None]
    )
    proj_grad_low = jnp.concatenate(
        [query_proj_grad, key_proj_grad, value_grad.reshape(group_rows, local_width)], axis=1
    ).astype(jnp.bfloat16)
    weight_parts = tuple(
        contract_rows(normed_one, proj_grad_low[:, i * local_width : (i + 1) * local_width]) for i in range(3)
    ) + (out_weight_acc,)
    normed_one_part = contract_last(proj_grad_low, joined_weight)
    scaled_inputs = rms_scale(inputs_all, 1.0)
    attn_gain_part = jnp.sum(normed_one_part * scaled_inputs, axis=0)
    totals, gain_totals, summed, normed_one_own = total_weights(
        weight_parts,
        (query_gain_part, key_gain_part),
        (router_part, attn_gain_part, moe_gain_part),
        normed_one_part.astype(jnp.bfloat16),
    )
    query_weight_grad, key_weight_grad, value_weight_grad, out_weight_grad = totals
    query_gain_grad, key_gain_grad = gain_totals
    router_weight_grad, attn_gain_grad, moe_gain_grad = summed
    _, norm_one_back = jax.vjp(lambda v: rms_scale(v, attn_gain.astype(jnp.float32)), input_own)
    (input_path,) = norm_one_back(normed_one_own.astype(jnp.float32))
    input_grad = (hidden_grad + input_path).astype(jnp.bfloat16)
    return (
        block_output,
        input_grad,
        attn_gain_grad,
        query_weight_grad,
        key_weight_grad,
        value_weight_grad,
        query_gain_grad,
        key_gain_grad,
        out_weight_grad,
        moe_gain_grad,
        router_weight_grad,
        gate_weight_grad,
        up_weight_grad,
        down_weight_grad,
    )


def solution(mesh):
    in_specs = (
        P("wide", None),
        P(),
        P(None, "narrow"),
        P(None, "narrow"),
        P(None, "narrow"),
        P("narrow"),
        P("narrow"),
        P("narrow", None),
        P(),
        P(),
        P("wide", None, "narrow"),
        P("wide", None, "narrow"),
        P("wide", "narrow", None),
        P("wide"),
        P(("wide", "narrow"), None),
        P(("wide", "narrow"), None),
    )
    out_specs = (
        P(("wide", "narrow"), None),
        P(("wide", "narrow"), None),
        P(),
        P(None, "narrow"),
        P(None, "narrow"),
        P(None, "narrow"),
        P("narrow"),
        P("narrow"),
        P("narrow", None),
        P(),
        P(),
        P("wide", None, "narrow"),
        P("wide", None, "narrow"),
        P("wide", "narrow", None),
    )
    return jax.shard_map(local, mesh=mesh, in_specs=in_specs, out_specs=out_specs, check_vma=False)
```
